32 devices in a mesh: dp: 8 (over y, x, core), expert: 4 (over z).
Axes of the slice: x: 2, y: 2, z: 4, core: 2. Of those that a mesh axis runs over, the one named last changes fastest.
Arguments:
- tokens: bfloat16 [8192, 2048], P(('dp', 'expert')), may hold values from -6 to 6
- cotangent: bfloat16 [8192, 2048], P(('dp', 'expert')), may hold values from -6 to 6
- gain_one: bfloat16 [2048], P(('dp', 'expert')), may hold values from 0.5 to 1.5
- gain_two: bfloat16 [2048], P(('dp', 'expert')), may hold values from 0.5 to 1.5
- kv_weight: bfloat16 [2048, 4096], P(('dp', 'expert')), may hold values from -0.125 to 0.125
- att_router: bfloat16 [2048, 4], P(('dp', 'expert')), may hold values from -0.09375 to 0.09375
- ffn_router: bfloat16 [2048, 4], P(('dp', 'expert')), may hold values from -0.09375 to 0.09375
- query_weight: bfloat16 [4, 2048, 2048], P('expert', 'dp'), may hold values from -0.125 to 0.125
- output_weight: bfloat16 [4, 2048, 2048], P('expert', 'dp'), may hold values from -1 to 1
- gate_weight: bfloat16 [4, 2048, 5632], P('expert', 'dp'), may hold values from -0.125 to 0.125
- up_weight: bfloat16 [4, 2048, 5632], P('expert', 'dp'), may hold values from -0.125 to 0.125
- down_weight: bfloat16 [4, 5632, 2048], P('expert', 'dp'), may hold values from -0.078125 to 0.078125
- leaf_parent: int32 [8, 8], P('dp'), may hold values from 1 to 4, as said below
- att_route: int32 [8192, 2], P(('dp', 'expert')), may hold values from 0 to 3, all different within a row; in each aligned block of 256 rows (0 to 255, 256 to 511, ...) at most 160 rows name the same one
- ffn_route: int32 [8192, 2], P(('dp', 'expert')), may hold values from 0 to 3, all different within a row; in each aligned block of 256 rows (0 to 255, 256 to 511, ...) at most 160 rows name the same one
Outputs:
- layer_out: bfloat16 [8192, 2048], P(('dp', 'expert'))
- input_grad: float32 [8192, 2048], P(('dp', 'expert'))
- gain_one_grad: float32 [2048], P(('dp', 'expert'))
- gain_two_grad: float32 [2048], P(('dp', 'expert'))
- kv_grad: float32 [2048, 4096], P(('dp', 'expert'))
- att_router_grad: float32 [2048, 4], P(('dp', 'expert'))
- ffn_router_grad: float32 [2048, 4], P(('dp', 'expert'))
- query_grad: float32 [4, 2048, 2048], P('expert', 'dp')
- output_grad: float32 [4, 2048, 2048], P('expert', 'dp')
- gate_grad: float32 [4, 2048, 5632], P('expert', 'dp')
- up_grad: float32 [4, 2048, 5632], P('expert', 'dp')
- down_grad: float32 [4, 5632, 2048], P('expert', 'dp')
The draws below stay inside these ranges and needn't reach their ends.
Inputs may be any that keep to these rules, and one draw needn't show every extreme that they name: leaf_parent[t, l] is the branch segment that leaf l of tree t continues; each branch has exactly two leaves. `att_route`: each row names two different experts; among the 256 rows of one device no expert is named by more than 160 rows, a bound that some block reaches. `ffn_route`: each row names two different experts; among the 256 rows of one device no expert is named by more than 160 rows, a bound that some block reaches.
All inputs are finite; a program needn't handle non-finite values.
Results may differ from the reference program's by a relative error of at most 0.019.
Values may be sent and summed in bfloat16 or wider, within the bound.
No kernel may reach another device: no remote copies, remote signals or barrier semaphores. Data moves between devices by JAX's collectives and lax.ppermute only.
A program may use at most 448 MiB of HBM per device.

```python
import math
import jax
import jax.numpy as jnp
import numpy as np
from jax import lax

D = 2048
HEADS = 16
HEAD = 128
FF = 5632
TRUNK = 512
BRANCH = 64
LEAF = 32
EXPERTS = 4
HD = 2048
TREE = 1024
TREES = 8
TOK_DEV = 256
TOKENS = 8192
CAP = 160


def draw_leaf_parent(key, part):
    branch_ids = jnp.arange(8, dtype=jnp.int32) // 2 + 1
    tree_keys = jax.random.split(key, TREES)
    return jax.vmap(lambda tree_key: jax.random.permutation(tree_key, branch_ids))(tree_keys).astype(jnp.int32)


def levels(stream_key, shape, cuts, smallest, top_value):
    loudness = 1.0
    for dim, parts in cuts:
        heights = jax.random.uniform(jax.random.fold_in(jax.random.fold_in(stream_key, 6), dim), (parts,), jnp.float32, smallest / len(cuts), top_value / len(cuts))
        loudness = loudness * jnp.repeat(jnp.exp(heights), shape[dim] // parts).reshape((-1,) + (1,) * (len(shape) - 1 - dim))
    return loudness


def deal_out(stream_key, own, number, rows, number_of, top, bound, lean):
    ranking = jax.random.permutation(stream_key, number_of)
    packed, common = portions_of(number_of, rows * top, bound, lean, True), portions_of(number_of, rows * top, bound, lean, False)
    places = jnp.arange(number_of)

    def named(sizes, offset_by):
        used = int((sizes > 0).sum())
        fixed = max(1, used // 4)
        moved = fixed + (places - fixed + offset_by * (used - fixed)) % max(1, number_of - fixed)
        return jnp.zeros((number_of,), jnp.int32).at[ranking[jnp.where(places < fixed, places, moved)]].set(jnp.asarray(sizes, jnp.int32))

    sizes = jnp.where(number % 4 == 0, named(packed, number // 4), named(common, number - number // 4 - 1))
    mixed = jax.random.permutation(jax.random.fold_in(own, 3), number_of)
    giver, taker = mixed[0:number_of // 2 * 2:2], mixed[1:number_of // 2 * 2:2]
    room = jnp.minimum(sizes[giver] - 1, bound - sizes[taker]) // 2
    room = jnp.where((giver == ranking[0]) | (taker == ranking[0]) | (sizes[taker] == 0), 0, jnp.maximum(room, 0))
    moved = jax.random.randint(jax.random.fold_in(own, 4), (number_of // 2,), 0, 1 << 20) % (room + 1)
    sizes = sizes.at[giver].add(-moved).at[taker].add(moved)
    members = jnp.searchsorted(jnp.cumsum(sizes), jnp.arange(rows * top), side="right").astype(jnp.int32)
    table = members.reshape(top, rows).T
    table = table[jax.random.permutation(jax.random.fold_in(own, 1), rows)]
    offset_by = jax.random.randint(jax.random.fold_in(own, 2), (rows, 1), 0, top)
    return jnp.take_along_axis(table, (jnp.arange(top)[None, :] + offset_by) % top, axis=1)


def portions_of(amount, total, limit, skew, full):
    weights = [(1 << 20) // math.isqrt(rank ** skew) + 1 for rank in range(1, amount + 1)]
    largest = limit if full else min(limit, max(-(-total // amount), total * weights[0] // sum(weights)))
    least = 1 if total - largest >= amount - 1 else 0
    counts, rest = [largest] + [least] * (amount - 1), total - largest - least * (amount - 1)
    while rest > 0:
        free = [i for i in range(1, amount) if counts[i] < largest] or [i for i in range(1, amount) if counts[i] < limit]
        mass, remaining = sum([weights[i] for i in free]), rest
        for i in free:
            addition = min(limit - counts[i], max(1, remaining * weights[i] // mass), rest)
            counts[i] = counts[i] + addition
            rest = rest - addition
    return np.array(counts)


def scatter_about(stream_key, dims, spread, most, cuts=(), kind=jnp.bfloat16):
    loudness = levels(stream_key, dims, cuts, -0.22, 0.18) if cuts else 1.0
    values = jax.random.normal(stream_key, dims, jnp.float32) * spread * loudness
    return jnp.minimum(jnp.maximum(values, -most), most).astype(kind)


def setup_inputs(seed: int = 0) -> dict:
    key_of = jax.random.split(jax.random.key(seed), 16)
    tokens = scatter_about(key_of[0], (TOKENS, D), 1.0, 6.0, ((0, 32),))
    cotangent = scatter_about(key_of[1], (TOKENS, D), 1.0, 6.0, ((0, 32),))
    gain_one = jnp.clip(1.0 + 0.1 * jax.random.normal(key_of[2], (D,), jnp.float32), 0.5, 1.5).astype(jnp.bfloat16)
    gain_two = jnp.clip(1.0 + 0.1 * jax.random.normal(key_of[3], (D,), jnp.float32), 0.5, 1.5).astype(jnp.bfloat16)
    kv_weight = scatter_about(key_of[4], (D, 2 * HD), D ** -0.5, 0.125, ((0, 32),))
    att_router = scatter_about(key_of[5], (D, EXPERTS), (2 * D) ** -0.5, 0.09375, ((0, 32),))
    ffn_router = scatter_about(key_of[6], (D, EXPERTS), (2 * D) ** -0.5, 0.09375, ((0, 32),))
    query_weight = scatter_about(key_of[7], (EXPERTS, D, HD), D ** -0.5, 0.125, ((0, 4), (1, 8)))
    output_weight = scatter_about(key_of[8], (EXPERTS, HD, D), (HD // 64) ** -0.5, 1.0, ((0, 4), (1, 8)))
    gate_weight = scatter_about(key_of[9], (EXPERTS, D, FF), D ** -0.5, 0.125, ((0, 4), (1, 8)))
    up_weight = scatter_about(key_of[10], (EXPERTS, D, FF), D ** -0.5, 0.125, ((0, 4), (1, 8)))
    down_weight = scatter_about(key_of[11], (EXPERTS, FF, D), FF ** -0.5, 0.078125, ((0, 4), (1, 8)))
    leaf_parent = draw_leaf_parent(jax.random.fold_in(key_of[15], 71), 0)
    att_route_keys = jax.random.split(jax.random.fold_in(key_of[13], 1), TOKENS // TOK_DEV)
    att_route_turns = jax.random.permutation(jax.random.fold_in(key_of[13], 3), TOKENS // TOK_DEV)
    att_route = jax.vmap(lambda own, number: deal_out(jax.random.fold_in(key_of[13], 2), own, number, TOK_DEV, EXPERTS, 2, CAP, 1))(att_route_keys, att_route_turns).reshape((TOKENS, 2))
    ffn_route_keys = jax.random.split(jax.random.fold_in(key_of[14], 1), TOKENS // TOK_DEV)
    ffn_route_turns = jax.random.permutation(jax.random.fold_in(key_of[14], 3), TOKENS // TOK_DEV)
    ffn_route = jax.vmap(lambda own, number: deal_out(jax.random.fold_in(key_of[14], 2), own, number, TOK_DEV, EXPERTS, 2, CAP, 1))(ffn_route_keys, ffn_route_turns).reshape((TOKENS, 2))
    return dict(tokens=tokens, cotangent=cotangent, gain_one=gain_one, gain_two=gain_two, kv_weight=kv_weight, att_router=att_router, ffn_router=ffn_router, query_weight=query_weight, output_weight=output_weight, gate_weight=gate_weight, up_weight=up_weight, down_weight=down_weight, leaf_parent=leaf_parent, att_route=att_route, ffn_route=ffn_route)


@jax.custom_vjp
def low(v):
    return lax.optimization_barrier(v.astype(jnp.bfloat16)).astype(jnp.float32)

@jax.custom_vjp
def low_back(v):
    return v

def low_keep(v):
    return (low(v), None)

def low_pass(kept, grad):
    return (grad,)

def back_keep(v):
    return (v, None)

def back_low(kept, grad):
    return (low(grad),)
low.defvjp(low_keep, low_pass)
low_back.defvjp(back_keep, back_low)
norm_eps = 1e-05
highest = lax.Precision.HIGHEST
masked_score = -1e+30

def matmul(left, right):
    return jnp.dot(left, right, precision=highest, preferred_element_type=jnp.float32)

def layout(row_index):
    past_trunk = row_index - TRUNK
    in_branch = (row_index >= TRUNK) & (past_trunk < 4 * BRANCH)
    leaf_offset = past_trunk - 4 * BRANCH
    segment = jnp.where(row_index < TRUNK, 0, jnp.where(in_branch, 1 + past_trunk // BRANCH, 5 + leaf_offset // LEAF))
    position = jnp.where(row_index < TRUNK, row_index, jnp.where(in_branch, TRUNK + past_trunk % BRANCH, TRUNK + BRANCH + leaf_offset % LEAF))
    return (segment.astype(jnp.int32), position.astype(jnp.int32))

def visible(query_index, query_segment, key_index, key_segment, parents):
    leaf_slot = query_segment - 5
    branch_of = lax.optimization_barrier(jnp.sum(jnp.where(leaf_slot[:, None] == jnp.arange(8, dtype=jnp.int32)[None, :], parents[None, :], 0), 1))
    ancestor = jnp.where(query_segment >= 5, branch_of, -1)
    same_segment = (key_segment[None, :] == query_segment[:, None]) & (key_index[None, :] <= query_index[:, None])
    from_trunk = (key_segment[None, :] == 0) & (query_segment[:, None] > 0)
    from_branch = key_segment[None, :] == ancestor[:, None]
    return same_segment | from_trunk | from_branch

def rotary_tables(position):
    half_width = HEAD // 2
    frequency = 10000.0 ** (-2.0 * jnp.arange(half_width, dtype=jnp.float32) / HEAD)
    angle = position.astype(jnp.float32)[:, None] * frequency[None, :]
    return (jnp.cos(angle), jnp.sin(angle))

def rotate(vector, cosine, sine_table):
    length = vector.shape[0]
    heads_view = vector.reshape(length, HEADS, HEAD)
    lead_half = heads_view[..., :HEAD // 2]
    tail_half = heads_view[..., HEAD // 2:]
    cos_part = cosine[:, None, :]
    sin_part = sine_table[:, None, :]
    turned = jnp.concatenate([lead_half * cos_part - tail_half * sin_part, tail_half * cos_part + lead_half * sin_part], -1)
    return turned.reshape(length, HEADS * HEAD)

def route_gates(logits, route):
    picks = (route[:, :, None] == jnp.arange(EXPERTS, dtype=jnp.int32)[None, None, :]).astype(jnp.float32)
    chosen = lax.optimization_barrier(jnp.sum(picks * logits[:, None, :], -1))
    weights = jax.nn.softmax(chosen, -1)
    return lax.optimization_barrier(jnp.sum(weights[:, :, None] * picks, 1))

def attend(queries, key_block, value_block, key_mask):
    length = queries.shape[0]
    query_heads = queries.reshape(length, HEADS, HEAD)
    key_heads = key_block.reshape(key_block.shape[0], HEADS, HEAD)
    value_heads = value_block.reshape(value_block.shape[0], HEADS, HEAD)
    scores = low_back(jnp.einsum('qhd,khd->hqk', query_heads, key_heads, precision=highest) * HEAD ** (-0.5))
    scores = jnp.where(key_mask[None], scores, masked_score)
    weights = low(jax.nn.softmax(scores, -1))
    return jnp.einsum('hqk,khd->qhd', weights, value_heads, precision=highest).reshape(length, HEADS * HEAD)

def attention_expert(rows_in, query_map, output_map, key_block, value_block, key_mask, cosine, sine_table):
    routed = low_back(rows_in)
    query_raw = low_back(matmul(routed, query_map))
    queries = low(rotate(query_raw, cosine, sine_table))
    attended = low(low_back(attend(queries, key_block, value_block, key_mask)))
    return low(low_back(matmul(attended, output_map)))

def ffn_expert(rows_in, gate_map, up_map, down_map):
    routed = low_back(rows_in)
    gate_value = low_back(matmul(routed, gate_map))
    up_value = low_back(matmul(routed, up_map))
    hidden = low(jax.nn.silu(gate_value) * up_value)
    return low(low_back(matmul(hidden, down_map)))

def tree_forward(params, tree_tokens, parents, att_route, ffn_route):
    gain_one, gain_two, kv_weight, att_router, ffn_router, query_weight, output_weight, gate_weight, up_weight, down_weight = params
    row_index = jnp.arange(TREE, dtype=jnp.int32)
    segment, position = layout(row_index)
    cosine, sine_table = rotary_tables(position)
    key_mask = visible(row_index, segment, row_index, segment, parents)
    inverse_one = lax.rsqrt(lax.optimization_barrier(jnp.mean(tree_tokens * tree_tokens, -1, keepdims=True)) + norm_eps)
    normed_one = low(tree_tokens * inverse_one * gain_one)
    kv_raw = low_back(matmul(normed_one, kv_weight))
    key_block = low(rotate(kv_raw[:, :HEADS * HEAD], cosine, sine_table))
    value_block = low(kv_raw[:, HEADS * HEAD:])
    att_gates = route_gates(matmul(normed_one, att_router), att_route)
    mixed_stream = tree_tokens
    for expert in range(EXPERTS):
        branch_out = jax.checkpoint(attention_expert)(normed_one, query_weight[expert], output_weight[expert], key_block, value_block, key_mask, cosine, sine_table)
        mixed_stream = mixed_stream + att_gates[:, expert:expert + 1] * branch_out
    inverse_two = lax.rsqrt(lax.optimization_barrier(jnp.mean(mixed_stream * mixed_stream, -1, keepdims=True)) + norm_eps)
    normed_two = low(mixed_stream * inverse_two * gain_two)
    ffn_gates = route_gates(matmul(normed_two, ffn_router), ffn_route)
    result = mixed_stream
    for expert in range(EXPERTS):
        branch_out = jax.checkpoint(ffn_expert)(normed_two, gate_weight[expert], up_weight[expert], down_weight[expert])
        result = result + ffn_gates[:, expert:expert + 1] * branch_out
    return result

def reference(tokens, cotangent, gain_one, gain_two, kv_weight, att_router, ffn_router, query_weight, output_weight, gate_weight, up_weight, down_weight, leaf_parent, att_route, ffn_route):
    params = tuple((array.astype(jnp.float32) for array in (gain_one, gain_two, kv_weight, att_router, ffn_router, query_weight, output_weight, gate_weight, up_weight, down_weight)))
    scanned = (leaf_parent.astype(jnp.int32), att_route.reshape(TREES, TREE, 2).astype(jnp.int32), ffn_route.reshape(TREES, TREE, 2).astype(jnp.int32))

    def forward(params_in, tokens_in):

        def tree_step(carried, slices):
            tree_tokens, parents, att_slice, ffn_slice = slices
            return (carried, jax.checkpoint(tree_forward)(params_in, tree_tokens, parents, att_slice, ffn_slice))
        _, outputs = lax.scan(tree_step, 0, (tokens_in.reshape(TREES, TREE, D), scanned[0], scanned[1], scanned[2]))
        return outputs.reshape(TOKENS, D)
    layer_value, pullback = jax.vjp(forward, params, tokens.astype(jnp.float32))
    grads, token_grad = pullback(cotangent.astype(jnp.float32))
    return (layer_value.astype(jnp.bfloat16), token_grad, grads[0], grads[1], grads[2], grads[3], grads[4], grads[5], grads[6], grads[7], grads[8], grads[9])
```

```python
import jax
import jax.numpy as jnp
from jax import lax
from jax.sharding import PartitionSpec as P

HEADS = 16
HEAD = 128
TRUNK = 512
BRANCH = 64
LEAF = 32
PAD = 128


norm_eps = 1e-05
highest = lax.Precision.HIGHEST
masked_score = -1e30
score_scale = HEAD ** (-0.5)
bf16 = jnp.bfloat16
f32 = jnp.float32


def layout(row_index):
    past_trunk = row_index - TRUNK
    in_branch = (row_index >= TRUNK) & (past_trunk < 4 * BRANCH)
    leaf_offset = past_trunk - 4 * BRANCH
    segment = jnp.where(
        row_index < TRUNK,
        0,
        jnp.where(in_branch, 1 + past_trunk // BRANCH, 5 + leaf_offset // LEAF),
    )
    position = jnp.where(
        row_index < TRUNK,
        row_index,
        jnp.where(in_branch, TRUNK + past_trunk % BRANCH, TRUNK + BRANCH + leaf_offset % LEAF),
    )
    return (segment, position)


def visible(query_index, query_segment, key_index, key_segment, parents):
    leaf_slot = query_segment - 5
    branch_of = jnp.sum(
        jnp.where(
            leaf_slot[:, None] == jnp.arange(8, dtype=jnp.int32)[None, :], parents[None, :], 0
        ),
        1,
    )
    ancestor = jnp.where(query_segment >= 5, branch_of, -1)
    same_segment = (key_segment[None, :] == query_segment[:, None]) & (
        key_index[None, :] <= query_index[:, None]
    )
    from_trunk = (key_segment[None, :] == 0) & (query_segment[:, None] > 0)
    from_branch = key_segment[None, :] == ancestor[:, None]
    return same_segment | from_trunk | from_branch


def rotary_tables(position):
    half_width = HEAD // 2
    frequency = 10000.0 ** (-2.0 * jnp.arange(half_width, dtype=f32) / HEAD)
    angle = position.astype(f32)[:, None] * frequency[None, :]
    return (jnp.cos(angle), jnp.sin(angle))


def rotate(vector, cosine, sine_table):
    length, width = vector.shape
    heads_view = vector.reshape(length, width // HEAD, HEAD)
    lead_half = heads_view[..., : HEAD // 2]
    tail_half = heads_view[..., HEAD // 2 :]
    cos_part = cosine[:, None, :]
    sin_part = sine_table[:, None, :]
    turned = jnp.concatenate(
        [lead_half * cos_part - tail_half * sin_part, tail_half * cos_part + lead_half * sin_part],
        -1,
    )
    return turned.reshape(length, width)


def rotate_back(grad_in, cosine, sine_table):
    return rotate(grad_in, cosine, -sine_table)


def mm(left, right):
    return jnp.dot(left, right, preferred_element_type=f32)


def mm_tn(left, right):
    return lax.dot_general(left, right, (((0,), (0,)), ((), ())), preferred_element_type=f32)


def mm_nt(left, right):
    return lax.dot_general(left, right, (((1,), (1,)), ((), ())), preferred_element_type=f32)


def earlier_count(named):
    rows = named.shape[0]
    before = jnp.tril(jnp.ones((rows, rows), bf16), -1)
    return mm(before, named.astype(bf16)).astype(jnp.int32)


def placement_of(routes, capacity, experts):
    picks = (routes[:, :, None] == jnp.arange(experts, dtype=jnp.int32)[None, None, :]).astype(
        jnp.int32
    )
    rank = earlier_count(jnp.sum(picks, 1))
    target = routes * capacity + jnp.sum(picks * rank[:, None, :], 2)
    slots_all = jnp.arange(experts * capacity, dtype=jnp.int32)
    return (target.T[:, :, None] == slots_all[None, None, :]).astype(bf16)


def gate_weights(logits, routes, experts):
    picks = (routes[:, :, None] == jnp.arange(experts, dtype=jnp.int32)[None, None, :]).astype(f32)
    chosen = jnp.sum(picks * logits[:, None, :], -1)
    return (jax.nn.softmax(chosen, -1), picks)


def router_back(gates, picks, picked, stream_grad):
    gate_grad = jnp.sum(picked * stream_grad[None], 2).T
    chosen_grad = gates * (gate_grad - jnp.sum(gates * gate_grad, 1, keepdims=True))
    return jnp.sum(picks * chosen_grad[:, :, None], 1)


def send_rows(place, values, experts):
    packed = mm_tn(place[0] + place[1], values).astype(bf16)
    return packed.reshape(experts, -1, values.shape[1])


def send_grads(place, gates, grad_in, experts):
    scaled = (gates.T[:, :, None] * grad_in[None]).astype(bf16)
    packed = (mm_tn(place[0], scaled[0]) + mm_tn(place[1], scaled[1])).astype(bf16)
    return packed.reshape(experts, -1, grad_in.shape[1])


def take_back(place, returned):
    flat_back = returned.reshape(place.shape[2], -1)
    return jnp.stack([mm(place[0], flat_back), mm(place[1], flat_back)])


def exchange(packed):
    return lax.all_to_all(packed, "expert", split_axis=0, concat_axis=0, tiled=True)


def ring_step(block, experts):
    return lax.ppermute(block, "expert", [(i, (i + 1) % experts) for i in range(experts)])


def ring_gather(block, experts):
    blocks = [block]
    for _ in range(experts - 1):
        blocks.append(ring_step(blocks[-1], experts))
    return blocks


def norm_back(stream, inverse, gain, grad_in):
    scaled = grad_in * gain
    return inverse * scaled - stream * inverse**3 * jnp.mean(scaled * stream, -1, keepdims=True)


def group_scores(queries, keys):
    heads = queries.shape[1] // HEAD
    return (
        jnp.einsum(
            "qhd,khd->hqk",
            queries.reshape(-1, heads, HEAD),
            keys.reshape(-1, heads, HEAD),
            preferred_element_type=f32,
        )
        * score_scale
    )


def attend(queries, keys, values, key_mask):
    heads = queries.shape[1] // HEAD
    scores = jnp.where(key_mask[None], group_scores(queries, keys), masked_score)
    row_peak = jnp.max(scores, -1, keepdims=True)
    exponent = jnp.exp(scores - row_peak)
    row_total = jnp.sum(exponent, -1, keepdims=True)
    attended = jnp.einsum(
        "hqk,khd->qhd",
        (exponent / row_total).astype(bf16),
        values.reshape(-1, heads, HEAD),
        preferred_element_type=f32,
    ).reshape(queries.shape)
    return (attended.astype(bf16), row_peak + jnp.log(row_total))


def attend_back(queries, keys, values, key_mask, log_total, attended, attended_grad):
    heads = queries.shape[1] // HEAD
    scores = jnp.where(key_mask[None], group_scores(queries, keys), masked_score)
    probs = jnp.exp(scores - log_total)
    grad_heads = attended_grad.reshape(-1, heads, HEAD)
    value_heads = values.reshape(-1, heads, HEAD)
    prob_grad = jnp.einsum("qhd,khd->hqk", grad_heads, value_heads, preferred_element_type=f32)
    row_delta = jnp.sum(
        grad_heads.astype(f32) * attended.reshape(-1, heads, HEAD).astype(f32), -1
    ).T[:, :, None]
    score_grad = (probs * (prob_grad - row_delta)).astype(bf16)
    query_grad = jnp.einsum(
        "hqk,khd->qhd", score_grad, keys.reshape(-1, heads, HEAD), preferred_element_type=f32
    ).reshape(queries.shape)
    key_grad = jnp.einsum(
        "hqk,qhd->khd", score_grad, queries.reshape(-1, heads, HEAD), preferred_element_type=f32
    ).reshape(keys.shape)
    value_grad = jnp.einsum(
        "hqk,qhd->khd", probs.astype(bf16), grad_heads, preferred_element_type=f32
    ).reshape(values.shape)
    return (query_grad * score_scale, key_grad * score_scale, value_grad)


def gather_dp(weight):
    return lax.all_gather(weight[0], "dp", axis=0, tiled=True)


def reduce_dp(part):
    return lax.psum_scatter(part, "dp", scatter_dimension=0, tiled=True)


def body(
    tokens,
    cotangent,
    gain_one,
    gain_two,
    kv_weight,
    att_router,
    ffn_router,
    query_weight,
    output_weight,
    gate_weight,
    up_weight,
    down_weight,
    leaf_parent,
    att_route,
    ffn_route,
):
    row_count, model_width = tokens.shape
    experts = att_router.shape[1]
    capacity = row_count * 5 // (2 * experts)
    head_width = HEADS * HEAD
    width = head_width // experts
    shard_rows = kv_weight.shape[0]
    parents = leaf_parent[0]
    own = lax.axis_index("expert")
    backs = [(own - k) % experts for k in range(experts)]

    small = jnp.concatenate(
        [
            att_router,
            ffn_router,
            gain_one[:, None],
            gain_two[:, None],
            jnp.zeros((shard_rows, PAD - 2 * experts - 2), bf16),
        ],
        1,
    )
    bundle = jnp.concatenate(
        [
            kv_weight.reshape(shard_rows, 2, experts, width)
            .transpose(2, 0, 1, 3)
            .reshape(experts, shard_rows, 2 * width),
            jnp.broadcast_to(small[None], (experts, shard_rows, PAD)),
        ],
        2,
    )
    bundle = exchange(bundle).reshape(experts * shard_rows, 2 * width + PAD)
    bundle = lax.all_gather(bundle, "dp", axis=0, tiled=True)
    kv_all = bundle[:, : 2 * width]
    att_all = bundle[:, 2 * width : 2 * width + experts]
    ffn_all = bundle[:, 2 * width + experts : 2 * width + 2 * experts]
    gain_first = bundle[:, 2 * width + 2 * experts].astype(f32)
    gain_second = bundle[:, 2 * width + 2 * experts + 1].astype(f32)

    query_all = gather_dp(query_weight)
    output_all = gather_dp(output_weight)
    gate_all = gather_dp(gate_weight)
    up_all = gather_dp(up_weight)
    down_all = gather_dp(down_weight)

    tagged = jnp.concatenate(
        [tokens, att_route.astype(bf16), jnp.zeros((row_count, PAD - 2), bf16)], 1
    )
    tree = jnp.zeros((experts * row_count, model_width + PAD), bf16)
    for k, block in enumerate(ring_gather(tagged, experts)):
        tree = lax.dynamic_update_slice_in_dim(tree, block, backs[k] * row_count, 0)
    tree_tokens = tree[:, :model_width].astype(f32)
    tree_routes = tree[:, model_width : model_width + 2].astype(jnp.int32)
    tree_index = jnp.arange(experts * row_count, dtype=jnp.int32)
    tree_segment, tree_position = layout(tree_index)
    tree_cos, tree_sin = rotary_tables(tree_position)
    tree_inverse = lax.rsqrt(jnp.mean(tree_tokens * tree_tokens, -1, keepdims=True) + norm_eps)
    normed_tree = (tree_tokens * tree_inverse * gain_first).astype(bf16)
    inputs = tokens.astype(f32)
    own_start = own * row_count
    inverse_one = lax.dynamic_slice_in_dim(tree_inverse, own_start, row_count, 0)
    normed_one = lax.dynamic_slice_in_dim(normed_tree, own_start, row_count, 0)

    kv_raw = mm(normed_tree, kv_all)
    kv_own = jnp.concatenate(
        [rotate(kv_raw[:, :width], tree_cos, tree_sin), kv_raw[:, width:]], 1
    ).astype(bf16)
    kv_blocks = ring_gather(kv_own, experts)

    named = jnp.any(tree_routes == own, 1).reshape(experts, row_count)
    rank = earlier_count(named.T).T
    slots = jnp.arange(capacity, dtype=jnp.int32)
    chosen = named[:, None, :] & (rank[:, None, :] == slots[None, :, None])
    chosen_index = tree_index.reshape(experts, 1, row_count)
    query_index = jnp.sum(jnp.where(chosen, chosen_index, 0), 2).reshape(-1)
    chosen = chosen.astype(bf16)
    query_rows = (
        jnp.einsum(
            "ksr,krd->ksd",
            chosen,
            normed_tree.reshape(experts, row_count, model_width),
            preferred_element_type=f32,
        )
        .astype(bf16)
        .reshape(-1, model_width)
    )
    query_segment, query_position = layout(query_index)
    query_cos, query_sin = rotary_tables(query_position)
    key_mask = visible(query_index, query_segment, tree_index, tree_segment, parents)
    queries = rotate(mm(query_rows, query_all), query_cos, query_sin).astype(bf16)

    attended = jnp.zeros(queries.shape, bf16)
    saved = []
    for k in range(experts):
        start = backs[k] * width
        group_queries = lax.dynamic_slice_in_dim(queries, start, width, 1)
        keys, values = kv_blocks[k][:, :width], kv_blocks[k][:, width:]
        group_attended, log_total = attend(group_queries, keys, values, key_mask)
        attended = lax.dynamic_update_slice_in_dim(attended, group_attended, start, 1)
        saved.append((group_queries, keys, values, key_mask, log_total, group_attended))
    att_branch = mm(attended, output_all).astype(bf16)
    att_back = exchange(att_branch.reshape(experts, capacity, -1))

    att_logits = mm(normed_one, att_all)
    att_gate, att_picks = gate_weights(att_logits, att_route, experts)
    att_place = placement_of(att_route, capacity, experts)
    att_picked = take_back(att_place, att_back)
    mixed_stream = inputs + jnp.sum(att_gate.T[:, :, None] * att_picked, 0)
    inverse_two = lax.rsqrt(jnp.mean(mixed_stream * mixed_stream, -1, keepdims=True) + norm_eps)
    normed_two = (mixed_stream * inverse_two * gain_second).astype(bf16)
    ffn_logits = mm(normed_two, ffn_all)
    ffn_gate, ffn_picks = gate_weights(ffn_logits, ffn_route, experts)
    ffn_place = placement_of(ffn_route, capacity, experts)
    ffn_rows = exchange(send_rows(ffn_place, normed_two, experts)).reshape(-1, model_width)
    grad_out = cotangent.astype(f32)
    ffn_grad_rows = exchange(send_grads(ffn_place, ffn_gate, grad_out, experts)).reshape(
        -1, model_width
    )
    gate_value = mm(ffn_rows, gate_all)
    up_value = mm(ffn_rows, up_all)
    sigmoid_gate = jax.nn.sigmoid(gate_value)
    hidden = (gate_value * sigmoid_gate * up_value).astype(bf16)
    down_part = mm_tn(hidden, ffn_grad_rows).astype(bf16)
    down_sum = reduce_dp(down_part)
    ffn_branch = mm(hidden, down_all).astype(bf16)
    ffn_picked = take_back(ffn_place, exchange(ffn_branch.reshape(experts, capacity, -1)))
    result = mixed_stream + jnp.sum(ffn_gate.T[:, :, None] * ffn_picked, 0)
    ffn_logit_grad = router_back(ffn_gate, ffn_picks, ffn_picked, grad_out)
    hidden_grad = mm_nt(ffn_grad_rows, down_all)
    gate_grad = (
        hidden_grad * up_value * sigmoid_gate * (1.0 + gate_value * (1.0 - sigmoid_gate))
    ).astype(bf16)
    up_grad = (hidden_grad * gate_value * sigmoid_gate).astype(bf16)
    ffn_rows_grad = (mm_nt(gate_grad, gate_all) + mm_nt(up_grad, up_all)).astype(bf16)
    ffn_rows_back = exchange(ffn_rows_grad.reshape(experts, capacity, -1)).reshape(
        experts * capacity, -1
    )
    gate_sum = reduce_dp(mm_tn(ffn_rows, gate_grad).astype(bf16))
    up_sum = reduce_dp(mm_tn(ffn_rows, up_grad).astype(bf16))
    normed_two_grad = mm(ffn_place[0] + ffn_place[1], ffn_rows_back) + jnp.dot(
        ffn_logit_grad, ffn_all.astype(f32).T, precision=highest
    )
    gain_two_part = jnp.sum(normed_two_grad * mixed_stream * inverse_two, 0)
    mixed_grad = grad_out + norm_back(mixed_stream, inverse_two, gain_second, normed_two_grad)

    att_logit_grad = router_back(att_gate, att_picks, att_picked, mixed_grad)
    att_grad_rows = exchange(send_grads(att_place, att_gate, mixed_grad, experts)).reshape(
        -1, model_width
    )
    attended_grad = mm_nt(att_grad_rows, output_all).astype(bf16)
    output_sum = reduce_dp(mm_tn(attended, att_grad_rows).astype(bf16))
    query_grad = jnp.zeros(queries.shape, f32)
    kv_grad = None
    for step in range(1, experts + 1):
        k = step % experts
        start = backs[k] * width
        group_grad = lax.dynamic_slice_in_dim(attended_grad, start, width, 1)
        group_query_grad, key_grad, value_grad = attend_back(*saved[k], group_grad)
        query_grad = lax.dynamic_update_slice_in_dim(query_grad, group_query_grad, start, 1)
        part = jnp.concatenate([key_grad, value_grad], 1)
        if kv_grad is not None:
            part = part + kv_grad.astype(f32)
        kv_grad = part if k == 0 else ring_step(part.astype(bf16), experts)
    query_raw_grad = rotate_back(query_grad, query_cos, query_sin).astype(bf16)
    query_sum = reduce_dp(mm_tn(query_rows, query_raw_grad).astype(bf16))
    att_rows_grad = mm_nt(query_raw_grad, query_all).astype(bf16)
    kv_raw_grad = jnp.concatenate(
        [rotate_back(kv_grad[:, :width], tree_cos, tree_sin), kv_grad[:, width:]], 1
    ).astype(bf16)
    tree_grad = mm_nt(kv_raw_grad, kv_all).reshape(experts, row_count, -1) + jnp.einsum(
        "ksr,ksd->krd",
        chosen,
        att_rows_grad.reshape(experts, capacity, -1),
        preferred_element_type=f32,
    )
    normed_one_grad = None
    for step in range(1, experts + 1):
        k = step % experts
        part = lax.dynamic_index_in_dim(tree_grad, backs[k], 0, keepdims=False)
        if normed_one_grad is not None:
            part = part + normed_one_grad.astype(f32)
        normed_one_grad = part if k == 0 else ring_step(part.astype(bf16), experts)
    normed_one_grad = normed_one_grad + jnp.dot(
        att_logit_grad, att_all.astype(f32).T, precision=highest
    )
    gain_one_part = jnp.sum(normed_one_grad * inputs * inverse_one, 0)
    input_grad = mixed_grad + norm_back(inputs, inverse_one, gain_first, normed_one_grad)
    att_router_part = lax.dot_general(
        normed_one.astype(f32), att_logit_grad, (((0,), (0,)), ((), ())), precision=highest
    )
    ffn_router_part = lax.dot_general(
        normed_two.astype(f32), ffn_logit_grad, (((0,), (0,)), ((), ())), precision=highest
    )
    shared_part = jnp.concatenate(
        [
            mm_tn(normed_tree, kv_raw_grad).astype(bf16),
            att_router_part.astype(bf16),
            ffn_router_part.astype(bf16),
            gain_one_part[:, None].astype(bf16),
            gain_two_part[:, None].astype(bf16),
            jnp.zeros((model_width, PAD - 2 * experts - 2), bf16),
        ],
        1,
    )
    shared_sum = exchange(reduce_dp(shared_part).reshape(experts, shard_rows, -1)).astype(f32)
    kv_sum = (
        shared_sum[:, :, : 2 * width]
        .reshape(experts, shard_rows, 2, width)
        .transpose(1, 2, 0, 3)
        .reshape(shard_rows, 2 * head_width)
    )
    small_sum = jnp.sum(shared_sum[:, :, 2 * width :], 0)
    return (
        result.astype(bf16),
        input_grad,
        small_sum[:, 2 * experts],
        small_sum[:, 2 * experts + 1],
        kv_sum,
        small_sum[:, :experts],
        small_sum[:, experts : 2 * experts],
        query_sum.astype(f32)[None],
        output_sum.astype(f32)[None],
        gate_sum.astype(f32)[None],
        up_sum.astype(f32)[None],
        down_sum.astype(f32)[None],
    )

def solution(mesh):
    in_specs = (
        P(("dp", "expert"), None),
        P(("dp", "expert"), None),
        P(("dp", "expert")),
        P(("dp", "expert")),
        P(("dp", "expert"), None),
        P(("dp", "expert"), None),
        P(("dp", "expert"), None),
        P("expert", "dp", None),
        P("expert", "dp", None),
        P("expert", "dp", None),
        P("expert", "dp", None),
        P("expert", "dp", None),
        P("dp", None),
        P(("dp", "expert"), None),
        P(("dp", "expert"), None),
    )
    out_specs = (
        P(("dp", "expert"), None),
        P(("dp", "expert"), None),
        P(("dp", "expert")),
        P(("dp", "expert")),
        P(("dp", "expert"), None),
        P(("dp", "expert"), None),
        P(("dp", "expert"), None),
        P("expert", "dp", None),
        P("expert", "dp", None),
        P("expert", "dp", None),
        P("expert", "dp", None),
        P("expert", "dp", None),
    )
    return jax.shard_map(body, mesh=mesh, in_specs=in_specs, out_specs=out_specs, check_vma=False)
```

```python
import jax
import jax.numpy as jnp
from jax import lax
from jax.sharding import PartitionSpec as P

HEADS = 16
HEAD = 128
TRUNK = 512
BRANCH = 64
LEAF = 32
PAD = 128


norm_eps = 1e-05
highest = lax.Precision.HIGHEST
masked_score = -1e30
score_scale = HEAD ** (-0.5)
bf16 = jnp.bfloat16
f32 = jnp.float32


def layout(row_index):
    past_trunk = row_index - TRUNK
    in_branch = (row_index >= TRUNK) & (past_trunk < 4 * BRANCH)
    leaf_offset = past_trunk - 4 * BRANCH
    segment = jnp.where(
        row_index < TRUNK,
        0,
        jnp.where(in_branch, 1 + past_trunk // BRANCH, 5 + leaf_offset // LEAF),
    )
    position = jnp.where(
        row_index < TRUNK,
        row_index,
        jnp.where(in_branch, TRUNK + past_trunk % BRANCH, TRUNK + BRANCH + leaf_offset % LEAF),
    )
    return (segment, position)


def visible(query_index, query_segment, key_index, key_segment, parents):
    leaf_slot = query_segment - 5
    branch_of = jnp.sum(
        jnp.where(
            leaf_slot[:, None] == jnp.arange(8, dtype=jnp.int32)[None, :], parents[None, :], 0
        ),
        1,
    )
    ancestor = jnp.where(query_segment >= 5, branch_of, -1)
    same_segment = (key_segment[None, :] == query_segment[:, None]) & (
        key_index[None, :] <= query_index[:, None]
    )
    from_trunk = (key_segment[None, :] == 0) & (query_segment[:, None] > 0)
    from_branch = key_segment[None, :] == ancestor[:, None]
    return same_segment | from_trunk | from_branch


def rotary_tables(position):
    half_width = HEAD // 2
    frequency = 10000.0 ** (-2.0 * jnp.arange(half_width, dtype=f32) / HEAD)
    angle = position.astype(f32)[:, None] * frequency[None, :]
    return (jnp.cos(angle), jnp.sin(angle))


def rotate(vector, cosine, sine_table):
    length, width = vector.shape
    heads_view = vector.reshape(length, width // HEAD, HEAD)
    lead_half = heads_view[..., : HEAD // 2]
    tail_half = heads_view[..., HEAD // 2 :]
    cos_part = cosine[:, None, :]
    sin_part = sine_table[:, None, :]
    turned = jnp.concatenate(
        [lead_half * cos_part - tail_half * sin_part, tail_half * cos_part + lead_half * sin_part],
        -1,
    )
    return turned.reshape(length, width)


def rotate_back(grad_in, cosine, sine_table):
    return rotate(grad_in, cosine, -sine_table)


def mm(left, right):
    return jnp.dot(left, right, preferred_element_type=f32)


def mm_tn(left, right):
    return lax.dot_general(left, right, (((0,), (0,)), ((), ())), preferred_element_type=f32)


def mm_nt(left, right):
    return lax.dot_general(left, right, (((1,), (1,)), ((), ())), preferred_element_type=f32)


def earlier_count(named):
    rows = named.shape[0]
    before = jnp.tril(jnp.ones((rows, rows), bf16), -1)
    return mm(before, named.astype(bf16)).astype(jnp.int32)


def placement_of(routes, capacity, experts):
    picks = (routes[:, :, None] == jnp.arange(experts, dtype=jnp.int32)[None, None, :]).astype(
        jnp.int32
    )
    rank = earlier_count(jnp.sum(picks, 1))
    target = routes * capacity + jnp.sum(picks * rank[:, None, :], 2)
    slots_all = jnp.arange(experts * capacity, dtype=jnp.int32)
    return (target.T[:, :, None] == slots_all[None, None, :]).astype(bf16)


def gate_weights(logits, routes, experts):
    picks = (routes[:, :, None] == jnp.arange(experts, dtype=jnp.int32)[None, None, :]).astype(f32)
    chosen = jnp.sum(picks * logits[:, None, :], -1)
    return (jax.nn.softmax(chosen, -1), picks)


def router_back(gates, picks, picked, stream_grad):
    gate_grad = jnp.sum(picked * stream_grad[None], 2).T
    chosen_grad = gates * (gate_grad - jnp.sum(gates * gate_grad, 1, keepdims=True))
    return jnp.sum(picks * chosen_grad[:, :, None], 1)


def send_rows(place, values, experts):
    packed = mm_tn(place[0] + place[1], values).astype(bf16)
    return packed.reshape(experts, -1, values.shape[1])


def send_grads(place, gates, grad_in, experts):
    scaled = (gates.T[:, :, None] * grad_in[None]).astype(bf16)
    packed = (mm_tn(place[0], scaled[0]) + mm_tn(place[1], scaled[1])).astype(bf16)
    return packed.reshape(experts, -1, grad_in.shape[1])


def take_back(place, returned):
    flat_back = returned.reshape(place.shape[2], -1)
    return jnp.stack([mm(place[0], flat_back), mm(place[1], flat_back)])


def exchange(packed):
    return lax.all_to_all(packed, "expert", split_axis=0, concat_axis=0, tiled=True)


def exchange_direct(packed, experts, own):
    received = jnp.zeros(packed.shape, packed.dtype)
    for k in range(experts):
        block = lax.dynamic_index_in_dim(packed, (own + k) % experts, 0)
        if k:
            block = lax.ppermute(block, "expert", [(i, (i + k) % experts) for i in range(experts)])
        received = lax.dynamic_update_slice_in_dim(received, block, (own - k) % experts, 0)
    return received


def ring_step(block, experts):
    return lax.ppermute(block, "expert", [(i, (i + 1) % experts) for i in range(experts)])


def ring_gather(block, experts):
    blocks = [block]
    for _ in range(experts - 1):
        blocks.append(ring_step(blocks[-1], experts))
    return blocks


def norm_back(stream, inverse, gain, grad_in):
    scaled = grad_in * gain
    return inverse * scaled - stream * inverse**3 * jnp.mean(scaled * stream, -1, keepdims=True)


def group_scores(queries, keys):
    heads = queries.shape[1] // HEAD
    return (
        jnp.einsum(
            "qhd,khd->hqk",
            queries.reshape(-1, heads, HEAD),
            keys.reshape(-1, heads, HEAD),
            preferred_element_type=f32,
        )
        * score_scale
    )


def attend(queries, keys, values, key_mask):
    heads = queries.shape[1] // HEAD
    scores = jnp.where(key_mask[None], group_scores(queries, keys), masked_score)
    row_peak = jnp.max(scores, -1, keepdims=True)
    exponent = jnp.exp(scores - row_peak)
    row_total = jnp.sum(exponent, -1, keepdims=True)
    attended = jnp.einsum(
        "hqk,khd->qhd",
        (exponent / row_total).astype(bf16),
        values.reshape(-1, heads, HEAD),
        preferred_element_type=f32,
    ).reshape(queries.shape)
    return (attended.astype(bf16), row_peak + jnp.log(row_total))


def attend_back(queries, keys, values, key_mask, log_total, attended, attended_grad):
    heads = queries.shape[1] // HEAD
    scores = jnp.where(key_mask[None], group_scores(queries, keys), masked_score)
    probs = jnp.exp(scores - log_total)
    grad_heads = attended_grad.reshape(-1, heads, HEAD)
    value_heads = values.reshape(-1, heads, HEAD)
    prob_grad = jnp.einsum("qhd,khd->hqk", grad_heads, value_heads, preferred_element_type=f32)
    row_delta = jnp.sum(
        grad_heads.astype(f32) * attended.reshape(-1, heads, HEAD).astype(f32), -1
    ).T[:, :, None]
    score_grad = (probs * (prob_grad - row_delta)).astype(bf16)
    query_grad = jnp.einsum(
        "hqk,khd->qhd", score_grad, keys.reshape(-1, heads, HEAD), preferred_element_type=f32
    ).reshape(queries.shape)
    key_grad = jnp.einsum(
        "hqk,qhd->khd", score_grad, queries.reshape(-1, heads, HEAD), preferred_element_type=f32
    ).reshape(keys.shape)
    value_grad = jnp.einsum(
        "hqk,qhd->khd", probs.astype(bf16), grad_heads, preferred_element_type=f32
    ).reshape(values.shape)
    return (query_grad * score_scale, key_grad * score_scale, value_grad)


def gather_dp(weight):
    return lax.all_gather(weight[0], "dp", axis=0, tiled=True)


def reduce_dp(part):
    return lax.psum_scatter(part, "dp", scatter_dimension=0, tiled=True)


def body(
    tokens,
    cotangent,
    gain_one,
    gain_two,
    kv_weight,
    att_router,
    ffn_router,
    query_weight,
    output_weight,
    gate_weight,
    up_weight,
    down_weight,
    leaf_parent,
    att_route,
    ffn_route,
):
    row_count, model_width = tokens.shape
    experts = att_router.shape[1]
    capacity = row_count * 5 // (2 * experts)
    head_width = HEADS * HEAD
    width = head_width // experts
    shard_rows = kv_weight.shape[0]
    parents = leaf_parent[0]
    own = lax.axis_index("expert")
    backs = [(own - k) % experts for k in range(experts)]

    small = jnp.concatenate(
        [
            att_router,
            ffn_router,
            gain_one[:, None],
            gain_two[:, None],
            jnp.zeros((shard_rows, PAD - 2 * experts - 2), bf16),
        ],
        1,
    )
    bundle = jnp.concatenate(
        [
            kv_weight.reshape(shard_rows, 2, experts, width)
            .transpose(2, 0, 1, 3)
            .reshape(experts, shard_rows, 2 * width),
            jnp.broadcast_to(small[None], (experts, shard_rows, PAD)),
        ],
        2,
    )
    bundle = exchange_direct(bundle, experts, own).reshape(experts * shard_rows, 2 * width + PAD)
    bundle = lax.all_gather(bundle, "dp", axis=0, tiled=True)
    kv_all = bundle[:, : 2 * width]
    att_all = bundle[:, 2 * width : 2 * width + experts]
    ffn_all = bundle[:, 2 * width + experts : 2 * width + 2 * experts]
    gain_first = bundle[:, 2 * width + 2 * experts].astype(f32)
    gain_second = bundle[:, 2 * width + 2 * experts + 1].astype(f32)

    query_all = gather_dp(query_weight)
    output_all = gather_dp(output_weight)
    gate_all = gather_dp(gate_weight)
    up_all = gather_dp(up_weight)
    down_all = gather_dp(down_weight)

    tagged = jnp.concatenate(
        [tokens, att_route.astype(bf16), jnp.zeros((row_count, PAD - 2), bf16)], 1
    )
    tree = jnp.zeros((experts * row_count, model_width + PAD), bf16)
    for k, block in enumerate(ring_gather(tagged, experts)):
        tree = lax.dynamic_update_slice_in_dim(tree, block, backs[k] * row_count, 0)
    tree_tokens = tree[:, :model_width].astype(f32)
    tree_routes = tree[:, model_width : model_width + 2].astype(jnp.int32)
    tree_index = jnp.arange(experts * row_count, dtype=jnp.int32)
    tree_segment, tree_position = layout(tree_index)
    tree_cos, tree_sin = rotary_tables(tree_position)
    tree_inverse = lax.rsqrt(jnp.mean(tree_tokens * tree_tokens, -1, keepdims=True) + norm_eps)
    normed_tree = (tree_tokens * tree_inverse * gain_first).astype(bf16)
    inputs = tokens.astype(f32)
    own_start = own * row_count
    inverse_one = lax.dynamic_slice_in_dim(tree_inverse, own_start, row_count, 0)
    normed_one = lax.dynamic_slice_in_dim(normed_tree, own_start, row_count, 0)

    kv_raw = mm(normed_tree, kv_all)
    kv_own = jnp.concatenate(
        [rotate(kv_raw[:, :width], tree_cos, tree_sin), kv_raw[:, width:]], 1
    ).astype(bf16)
    kv_blocks = ring_gather(kv_own, experts)

    named = jnp.any(tree_routes == own, 1).reshape(experts, row_count)
    rank = earlier_count(named.T).T
    slots = jnp.arange(capacity, dtype=jnp.int32)
    chosen = named[:, None, :] & (rank[:, None, :] == slots[None, :, None])
    chosen_index = tree_index.reshape(experts, 1, row_count)
    query_index = jnp.sum(jnp.where(chosen, chosen_index, 0), 2).reshape(-1)
    chosen = chosen.astype(bf16)
    query_rows = (
        jnp.einsum(
            "ksr,krd->ksd",
            chosen,
            normed_tree.reshape(experts, row_count, model_width),
            preferred_element_type=f32,
        )
        .astype(bf16)
        .reshape(-1, model_width)
    )
    query_segment, query_position = layout(query_index)
    query_cos, query_sin = rotary_tables(query_position)
    key_mask = visible(query_index, query_segment, tree_index, tree_segment, parents)
    queries = rotate(mm(query_rows, query_all), query_cos, query_sin).astype(bf16)

    attended = jnp.zeros(queries.shape, bf16)
    saved = []
    for k in range(experts):
        start = backs[k] * width
        group_queries = lax.dynamic_slice_in_dim(queries, start, width, 1)
        kv_block = kv_blocks[k]
        if k:
            kv_block, attended = lax.optimization_barrier((kv_block, attended))
        keys, values = kv_block[:, :width], kv_block[:, width:]
        group_attended, log_total = attend(group_queries, keys, values, key_mask)
        attended = lax.dynamic_update_slice_in_dim(attended, group_attended, start, 1)
        saved.append((group_queries, keys, values, key_mask, log_total, group_attended))
    att_branch = mm(attended, output_all).astype(bf16)
    att_back = exchange(att_branch.reshape(experts, capacity, -1))

    att_logits = mm(normed_one, att_all)
    att_gate, att_picks = gate_weights(att_logits, att_route, experts)
    att_place = placement_of(att_route, capacity, experts)
    att_picked = take_back(att_place, att_back)
    mixed_stream = inputs + jnp.sum(att_gate.T[:, :, None] * att_picked, 0)
    inverse_two = lax.rsqrt(jnp.mean(mixed_stream * mixed_stream, -1, keepdims=True) + norm_eps)
    normed_two = (mixed_stream * inverse_two * gain_second).astype(bf16)
    ffn_logits = mm(normed_two, ffn_all)
    ffn_gate, ffn_picks = gate_weights(ffn_logits, ffn_route, experts)
    ffn_place = placement_of(ffn_route, capacity, experts)
    ffn_rows = exchange(send_rows(ffn_place, normed_two, experts)).reshape(-1, model_width)
    grad_out = cotangent.astype(f32)
    ffn_rows, packed_grads = lax.optimization_barrier(
        (ffn_rows, send_grads(ffn_place, ffn_gate, grad_out, experts))
    )
    ffn_grad_rows = exchange(packed_grads).reshape(-1, model_width)
    gate_value = mm(ffn_rows, gate_all)
    up_value = mm(ffn_rows, up_all)
    sigmoid_gate = jax.nn.sigmoid(gate_value)
    hidden = (gate_value * sigmoid_gate * up_value).astype(bf16)
    down_part = mm_tn(hidden, ffn_grad_rows).astype(bf16)
    down_part, hidden, ffn_grad_rows = lax.optimization_barrier((down_part, hidden, ffn_grad_rows))
    down_sum = reduce_dp(down_part)
    ffn_branch = mm(hidden, down_all).astype(bf16)
    ffn_branch, ffn_grad_rows = lax.optimization_barrier((ffn_branch, ffn_grad_rows))
    ffn_back = exchange(ffn_branch.reshape(experts, capacity, -1))
    hidden_grad = mm_nt(ffn_grad_rows, down_all)
    gate_grad = (
        hidden_grad * up_value * sigmoid_gate * (1.0 + gate_value * (1.0 - sigmoid_gate))
    ).astype(bf16)
    up_grad = (hidden_grad * gate_value * sigmoid_gate).astype(bf16)
    ffn_rows_grad = (mm_nt(gate_grad, gate_all) + mm_nt(up_grad, up_all)).astype(bf16)
    ffn_rows_grad, gate_grad, up_grad, ffn_back = lax.optimization_barrier(
        (ffn_rows_grad, gate_grad, up_grad, ffn_back)
    )
    ffn_picked = take_back(ffn_place, ffn_back)
    result = mixed_stream + jnp.sum(ffn_gate.T[:, :, None] * ffn_picked, 0)
    ffn_logit_grad = router_back(ffn_gate, ffn_picks, ffn_picked, grad_out)
    ffn_rows_back = exchange(ffn_rows_grad.reshape(experts, capacity, -1)).reshape(
        experts * capacity, -1
    )
    gate_part = mm_tn(ffn_rows, gate_grad).astype(bf16)
    up_part = mm_tn(ffn_rows, up_grad).astype(bf16)
    gate_part, up_part, ffn_rows_back = lax.optimization_barrier(
        (gate_part, up_part, ffn_rows_back)
    )
    gate_sum = reduce_dp(gate_part)
    up_sum = reduce_dp(up_part)
    normed_two_grad = mm(ffn_place[0] + ffn_place[1], ffn_rows_back) + jnp.dot(
        ffn_logit_grad, ffn_all.astype(f32).T, precision=highest
    )
    gain_two_part = jnp.sum(normed_two_grad * mixed_stream * inverse_two, 0)
    mixed_grad = grad_out + norm_back(mixed_stream, inverse_two, gain_second, normed_two_grad)

    att_logit_grad = router_back(att_gate, att_picks, att_picked, mixed_grad)
    att_grad_rows = exchange(send_grads(att_place, att_gate, mixed_grad, experts)).reshape(
        -1, model_width
    )
    att_grad_rows, down_sum = lax.optimization_barrier((att_grad_rows, down_sum))
    attended_grad = mm_nt(att_grad_rows, output_all).astype(bf16)
    output_part = mm_tn(attended, att_grad_rows).astype(bf16)
    query_grad = jnp.zeros(queries.shape, f32)
    kv_grad = None
    for step in range(1, experts + 1):
        k = step % experts
        start = backs[k] * width
        group_grad = lax.dynamic_slice_in_dim(attended_grad, start, width, 1)
        group_query_grad, key_grad, value_grad = attend_back(*saved[k], group_grad)
        query_grad = lax.dynamic_update_slice_in_dim(query_grad, group_query_grad, start, 1)
        part = jnp.concatenate([key_grad, value_grad], 1)
        if step == 2:
            kv_grad, output_part = lax.optimization_barrier((kv_grad, output_part))
        if k == 0:
            query_raw_grad = rotate_back(query_grad, query_cos, query_sin).astype(bf16)
            query_part = mm_tn(query_rows, query_raw_grad).astype(bf16)
            kv_grad, query_part = lax.optimization_barrier((kv_grad, query_part))
        if kv_grad is not None:
            part = part + kv_grad.astype(f32)
        kv_grad = part if k == 0 else ring_step(part.astype(bf16), experts)
    output_sum = reduce_dp(output_part)
    query_sum = reduce_dp(query_part)
    att_rows_grad = mm_nt(query_raw_grad, query_all).astype(bf16)
    kv_raw_grad = jnp.concatenate(
        [rotate_back(kv_grad[:, :width], tree_cos, tree_sin), kv_grad[:, width:]], 1
    ).astype(bf16)
    tree_grad = mm_nt(kv_raw_grad, kv_all).reshape(experts, row_count, -1) + jnp.einsum(
        "ksr,ksd->krd",
        chosen,
        att_rows_grad.reshape(experts, capacity, -1),
        preferred_element_type=f32,
    )
    normed_one_grad = None
    for step in range(1, experts + 1):
        k = step % experts
        part = lax.dynamic_index_in_dim(tree_grad, backs[k], 0, keepdims=False)
        if normed_one_grad is not None:
            part = part + normed_one_grad.astype(f32)
        normed_one_grad = part if k == 0 else ring_step(part.astype(bf16), experts)
    normed_one_grad = normed_one_grad + jnp.dot(
        att_logit_grad, att_all.astype(f32).T, precision=highest
    )
    gain_one_part = jnp.sum(normed_one_grad * inputs * inverse_one, 0)
    input_grad = mixed_grad + norm_back(inputs, inverse_one, gain_first, normed_one_grad)
    att_router_part = lax.dot_general(
        normed_one.astype(f32), att_logit_grad, (((0,), (0,)), ((), ())), precision=highest
    )
    ffn_router_part = lax.dot_general(
        normed_two.astype(f32), ffn_logit_grad, (((0,), (0,)), ((), ())), precision=highest
    )
    shared_part = jnp.concatenate(
        [
            mm_tn(normed_tree, kv_raw_grad).astype(bf16),
            att_router_part.astype(bf16),
            ffn_router_part.astype(bf16),
            gain_one_part[:, None].astype(bf16),
            gain_two_part[:, None].astype(bf16),
            jnp.zeros((model_width, PAD - 2 * experts - 2), bf16),
        ],
        1,
    )
    shared_part, query_sum = lax.optimization_barrier((shared_part, query_sum))
    shared_sum = exchange(reduce_dp(shared_part).reshape(experts, shard_rows, -1)).astype(f32)
    kv_sum = (
        shared_sum[:, :, : 2 * width]
        .reshape(experts, shard_rows, 2, width)
        .transpose(1, 2, 0, 3)
        .reshape(shard_rows, 2 * head_width)
    )
    small_sum = jnp.sum(shared_sum[:, :, 2 * width :], 0)
    return (
        result.astype(bf16),
        input_grad,
        small_sum[:, 2 * experts],
        small_sum[:, 2 * experts + 1],
        kv_sum,
        small_sum[:, :experts],
        small_sum[:, experts : 2 * experts],
        query_sum.astype(f32)[None],
        output_sum.astype(f32)[None],
        gate_sum.astype(f32)[None],
        up_sum.astype(f32)[None],
        down_sum.astype(f32)[None],
    )

def solution(mesh):
    in_specs = (
        P(("dp", "expert"), None),
        P(("dp", "expert"), None),
        P(("dp", "expert")),
        P(("dp", "expert")),
        P(("dp", "expert"), None),
        P(("dp", "expert"), None),
        P(("dp", "expert"), None),
        P("expert", "dp", None),
        P("expert", "dp", None),
        P("expert", "dp", None),
        P("expert", "dp", None),
        P("expert", "dp", None),
        P("dp", None),
        P(("dp", "expert"), None),
        P(("dp", "expert"), None),
    )
    out_specs = (
        P(("dp", "expert"), None),
        P(("dp", "expert"), None),
        P(("dp", "expert")),
        P(("dp", "expert")),
        P(("dp", "expert"), None),
        P(("dp", "expert"), None),
        P(("dp", "expert"), None),
        P("expert", "dp", None),
        P("expert", "dp", None),
        P("expert", "dp", None),
        P("expert", "dp", None),
        P("expert", "dp", None),
    )
    return jax.shard_map(body, mesh=mesh, in_specs=in_specs, out_specs=out_specs, check_vma=False)
```

```python
import jax
import jax.numpy as jnp
from jax import lax
from jax.sharding import PartitionSpec as P

HEADS = 16
HEAD = 128
TRUNK = 512
BRANCH = 64
LEAF = 32
PAD = 128


norm_eps = 1e-05
highest = lax.Precision.HIGHEST
masked_score = -1e30
score_scale = HEAD ** (-0.5)
bf16 = jnp.bfloat16
f32 = jnp.float32


def layout(row_index):
    past_trunk = row_index - TRUNK
    in_branch = (row_index >= TRUNK) & (past_trunk < 4 * BRANCH)
    leaf_offset = past_trunk - 4 * BRANCH
    segment = jnp.where(
        row_index < TRUNK,
        0,
        jnp.where(in_branch, 1 + past_trunk // BRANCH, 5 + leaf_offset // LEAF),
    )
    position = jnp.where(
        row_index < TRUNK,
        row_index,
        jnp.where(in_branch, TRUNK + past_trunk % BRANCH, TRUNK + BRANCH + leaf_offset % LEAF),
    )
    return (segment, position)


def visible(query_index, query_segment, key_index, key_segment, parents):
    leaf_slot = query_segment - 5
    branch_of = jnp.sum(
        jnp.where(
            leaf_slot[:, None] == jnp.arange(8, dtype=jnp.int32)[None, :], parents[None, :], 0
        ),
        1,
    )
    ancestor = jnp.where(query_segment >= 5, branch_of, -1)
    same_segment = (key_segment[None, :] == query_segment[:, None]) & (
        key_index[None, :] <= query_index[:, None]
    )
    from_trunk = (key_segment[None, :] == 0) & (query_segment[:, None] > 0)
    from_branch = key_segment[None, :] == ancestor[:, None]
    return same_segment | from_trunk | from_branch


def rotary_tables(position):
    half_width = HEAD // 2
    frequency = 10000.0 ** (-2.0 * jnp.arange(half_width, dtype=f32) / HEAD)
    angle = position.astype(f32)[:, None] * frequency[None, :]
    return (jnp.cos(angle), jnp.sin(angle))


def rotate(vector, cosine, sine_table):
    length, width = vector.shape
    heads_view = vector.reshape(length, width // HEAD, HEAD)
    lead_half = heads_view[..., : HEAD // 2]
    tail_half = heads_view[..., HEAD // 2 :]
    cos_part = cosine[:, None, :]
    sin_part = sine_table[:, None, :]
    turned = jnp.concatenate(
        [lead_half * cos_part - tail_half * sin_part, tail_half * cos_part + lead_half * sin_part],
        -1,
    )
    return turned.reshape(length, width)


def rotate_back(grad_in, cosine, sine_table):
    return rotate(grad_in, cosine, -sine_table)


def mm(left, right):
    return jnp.dot(left, right, preferred_element_type=f32)


def mm_tn(left, right):
    return lax.dot_general(left, right, (((0,), (0,)), ((), ())), preferred_element_type=f32)


def mm_nt(left, right):
    return lax.dot_general(left, right, (((1,), (1,)), ((), ())), preferred_element_type=f32)


def earlier_count(named):
    rows = named.shape[0]
    before = jnp.tril(jnp.ones((rows, rows), bf16), -1)
    return mm(before, named.astype(bf16)).astype(jnp.int32)


def placement_of(routes, capacity, experts):
    picks = (routes[:, :, None] == jnp.arange(experts, dtype=jnp.int32)[None, None, :]).astype(
        jnp.int32
    )
    rank = earlier_count(jnp.sum(picks, 1))
    target = routes * capacity + jnp.sum(picks * rank[:, None, :], 2)
    slots_all = jnp.arange(experts * capacity, dtype=jnp.int32)
    return (target.T[:, :, None] == slots_all[None, None, :]).astype(bf16)


def gate_weights(logits, routes, experts):
    picks = (routes[:, :, None] == jnp.arange(experts, dtype=jnp.int32)[None, None, :]).astype(f32)
    chosen = jnp.sum(picks * logits[:, None, :], -1)
    return (jax.nn.softmax(chosen, -1), picks)


def router_back(gates, picks, picked, stream_grad):
    gate_grad = jnp.sum(picked * stream_grad[None], 2).T
    chosen_grad = gates * (gate_grad - jnp.sum(gates * gate_grad, 1, keepdims=True))
    return jnp.sum(picks * chosen_grad[:, :, None], 1)


def send_rows(place, values, experts):
    packed = mm_tn(place[0] + place[1], values).astype(bf16)
    return packed.reshape(experts, -1, values.shape[1])


def send_grads(place, gates, grad_in, experts):
    scaled = (gates.T[:, :, None] * grad_in[None]).astype(bf16)
    packed = (mm_tn(place[0], scaled[0]) + mm_tn(place[1], scaled[1])).astype(bf16)
    return packed.reshape(experts, -1, grad_in.shape[1])


def take_back(place, returned):
    flat_back = returned.reshape(place.shape[2], -1)
    return jnp.stack([mm(place[0], flat_back), mm(place[1], flat_back)])


def exchange(packed):
    return lax.all_to_all(packed, "expert", split_axis=0, concat_axis=0, tiled=True)


def exchange_direct(packed, experts, own):
    received = jnp.zeros(packed.shape, packed.dtype)
    for k in range(experts):
        block = lax.dynamic_index_in_dim(packed, (own + k) % experts, 0)
        if k:
            block = lax.ppermute(block, "expert", [(i, (i + k) % experts) for i in range(experts)])
        received = lax.dynamic_update_slice_in_dim(received, block, (own - k) % experts, 0)
    return received


def ring_step(block, experts):
    return lax.ppermute(block, "expert", [(i, (i + 1) % experts) for i in range(experts)])


def ring_gather(block, experts):
    blocks = [block]
    for _ in range(experts - 1):
        blocks.append(ring_step(blocks[-1], experts))
    return blocks


def norm_back(stream, inverse, gain, grad_in):
    scaled = grad_in * gain
    return inverse * scaled - stream * inverse**3 * jnp.mean(scaled * stream, -1, keepdims=True)


def group_scores(queries, keys):
    heads = queries.shape[1] // HEAD
    return (
        jnp.einsum(
            "qhd,khd->hqk",
            queries.reshape(-1, heads, HEAD),
            keys.reshape(-1, heads, HEAD),
            preferred_element_type=f32,
        )
        * score_scale
    )


def attend(queries, keys, values, key_mask):
    heads = queries.shape[1] // HEAD
    scores = jnp.where(key_mask[None], group_scores(queries, keys), masked_score)
    row_peak = jnp.max(scores, -1, keepdims=True)
    exponent = jnp.exp(scores - row_peak)
    row_total = jnp.sum(exponent, -1, keepdims=True)
    attended = jnp.einsum(
        "hqk,khd->qhd",
        (exponent / row_total).astype(bf16),
        values.reshape(-1, heads, HEAD),
        preferred_element_type=f32,
    ).reshape(queries.shape)
    return (attended.astype(bf16), row_peak + jnp.log(row_total))


def attend_back(queries, keys, values, key_mask, log_total, attended, attended_grad):
    heads = queries.shape[1] // HEAD
    scores = jnp.where(key_mask[None], group_scores(queries, keys), masked_score)
    probs = jnp.exp(scores - log_total)
    grad_heads = attended_grad.reshape(-1, heads, HEAD)
    value_heads = values.reshape(-1, heads, HEAD)
    prob_grad = jnp.einsum("qhd,khd->hqk", grad_heads, value_heads, preferred_element_type=f32)
    row_delta = jnp.sum(
        grad_heads.astype(f32) * attended.reshape(-1, heads, HEAD).astype(f32), -1
    ).T[:, :, None]
    score_grad = (probs * (prob_grad - row_delta)).astype(bf16)
    query_grad = jnp.einsum(
        "hqk,khd->qhd", score_grad, keys.reshape(-1, heads, HEAD), preferred_element_type=f32
    ).reshape(queries.shape)
    key_grad = jnp.einsum(
        "hqk,qhd->khd", score_grad, queries.reshape(-1, heads, HEAD), preferred_element_type=f32
    ).reshape(keys.shape)
    value_grad = jnp.einsum(
        "hqk,qhd->khd", probs.astype(bf16), grad_heads, preferred_element_type=f32
    ).reshape(values.shape)
    return (query_grad * score_scale, key_grad * score_scale, value_grad)


def gather_dp(weight):
    return lax.all_gather(weight[0], "dp", axis=0, tiled=True)


def reduce_dp(part):
    return lax.psum_scatter(part, "dp", scatter_dimension=0, tiled=True)


def swap(block, bit):
    return lax.ppermute(block, "dp", [(i, i ^ bit) for i in range(8)])


def bit_of(value, bit):
    return (value // bit) % 2


def halves(block, axis, bit):
    pick = bit_of(lax.axis_index("dp"), bit)
    kept = lax.dynamic_index_in_dim(block, pick, axis, keepdims=False)
    sent = lax.dynamic_index_in_dim(block, 1 - pick, axis, keepdims=False)
    return (kept.astype(f32), sent.astype(bf16))


def fold(block, axis, bit):
    kept, sent = halves(block, axis, bit)
    return kept + swap(sent, bit).astype(f32)


def reduce_swaps(part):
    if lax.axis_size("dp") != 8:
        return reduce_dp(part).astype(f32)
    rows, columns = part.shape
    grid = fold(part.reshape(2, 2, 2, rows // 8, columns), 2, 1).astype(bf16)
    left, right = grid[..., : columns // 2], grid[..., columns // 2 :]
    left = fold(fold(left, 1, 2).astype(bf16), 0, 4)
    right = fold(fold(right, 0, 4).astype(bf16), 0, 2)
    return jnp.concatenate([left, right], 1)


def body(
    tokens,
    cotangent,
    gain_one,
    gain_two,
    kv_weight,
    att_router,
    ffn_router,
    query_weight,
    output_weight,
    gate_weight,
    up_weight,
    down_weight,
    leaf_parent,
    att_route,
    ffn_route,
):
    row_count, model_width = tokens.shape
    experts = att_router.shape[1]
    capacity = row_count * 5 // (2 * experts)
    head_width = HEADS * HEAD
    width = head_width // experts
    shard_rows = kv_weight.shape[0]
    parents = leaf_parent[0]
    own = lax.axis_index("expert")
    backs = [(own - k) % experts for k in range(experts)]

    small = jnp.concatenate(
        [
            att_router,
            ffn_router,
            gain_one[:, None],
            gain_two[:, None],
            jnp.zeros((shard_rows, PAD - 2 * experts - 2), bf16),
        ],
        1,
    )
    bundle = jnp.concatenate(
        [
            kv_weight.reshape(shard_rows, 2, experts, width)
            .transpose(2, 0, 1, 3)
            .reshape(experts, shard_rows, 2 * width),
            jnp.broadcast_to(small[None], (experts, shard_rows, PAD)),
        ],
        2,
    )
    bundle = exchange_direct(bundle, experts, own).reshape(experts * shard_rows, 2 * width + PAD)
    bundle = lax.all_gather(bundle, "dp", axis=0, tiled=True)
    kv_all = bundle[:, : 2 * width]
    att_all = bundle[:, 2 * width : 2 * width + experts]
    ffn_all = bundle[:, 2 * width + experts : 2 * width + 2 * experts]
    gain_first = bundle[:, 2 * width + 2 * experts].astype(f32)
    gain_second = bundle[:, 2 * width + 2 * experts + 1].astype(f32)

    query_all = gather_dp(query_weight)
    output_all = gather_dp(output_weight)
    gate_all = gather_dp(gate_weight)
    up_all = gather_dp(up_weight)
    down_all = gather_dp(down_weight)

    tagged = jnp.concatenate(
        [tokens, att_route.astype(bf16), jnp.zeros((row_count, PAD - 2), bf16)], 1
    )
    tree = jnp.zeros((experts * row_count, model_width + PAD), bf16)
    for k, block in enumerate(ring_gather(tagged, experts)):
        tree = lax.dynamic_update_slice_in_dim(tree, block, backs[k] * row_count, 0)
    tree_tokens = tree[:, :model_width].astype(f32)
    tree_routes = tree[:, model_width : model_width + 2].astype(jnp.int32)
    tree_index = jnp.arange(experts * row_count, dtype=jnp.int32)
    tree_segment, tree_position = layout(tree_index)
    tree_cos, tree_sin = rotary_tables(tree_position)
    tree_inverse = lax.rsqrt(jnp.mean(tree_tokens * tree_tokens, -1, keepdims=True) + norm_eps)
    normed_tree = (tree_tokens * tree_inverse * gain_first).astype(bf16)
    inputs = tokens.astype(f32)
    own_start = own * row_count
    inverse_one = lax.dynamic_slice_in_dim(tree_inverse, own_start, row_count, 0)
    normed_one = lax.dynamic_slice_in_dim(normed_tree, own_start, row_count, 0)

    kv_raw = mm(normed_tree, kv_all)
    kv_own = jnp.concatenate(
        [rotate(kv_raw[:, :width], tree_cos, tree_sin), kv_raw[:, width:]], 1
    ).astype(bf16)
    kv_blocks = ring_gather(kv_own, experts)

    named = jnp.any(tree_routes == own, 1).reshape(experts, row_count)
    rank = earlier_count(named.T).T
    slots = jnp.arange(capacity, dtype=jnp.int32)
    chosen = named[:, None, :] & (rank[:, None, :] == slots[None, :, None])
    chosen_index = tree_index.reshape(experts, 1, row_count)
    query_index = jnp.sum(jnp.where(chosen, chosen_index, 0), 2).reshape(-1)
    chosen = chosen.astype(bf16)
    query_rows = (
        jnp.einsum(
            "ksr,krd->ksd",
            chosen,
            normed_tree.reshape(experts, row_count, model_width),
            preferred_element_type=f32,
        )
        .astype(bf16)
        .reshape(-1, model_width)
    )
    query_segment, query_position = layout(query_index)
    query_cos, query_sin = rotary_tables(query_position)
    key_mask = visible(query_index, query_segment, tree_index, tree_segment, parents)
    queries = rotate(mm(query_rows, query_all), query_cos, query_sin).astype(bf16)

    attended = jnp.zeros(queries.shape, bf16)
    saved = []
    for k in range(experts):
        start = backs[k] * width
        group_queries = lax.dynamic_slice_in_dim(queries, start, width, 1)
        kv_block = kv_blocks[k]
        if k:
            kv_block, attended = lax.optimization_barrier((kv_block, attended))
        keys, values = kv_block[:, :width], kv_block[:, width:]
        group_attended, log_total = attend(group_queries, keys, values, key_mask)
        attended = lax.dynamic_update_slice_in_dim(attended, group_attended, start, 1)
        saved.append((group_queries, keys, values, key_mask, log_total, group_attended))
    att_branch = mm(attended, output_all).astype(bf16)
    att_back = exchange(att_branch.reshape(experts, capacity, -1))

    att_logits = mm(normed_one, att_all)
    att_gate, att_picks = gate_weights(att_logits, att_route, experts)
    att_place = placement_of(att_route, capacity, experts)
    att_picked = take_back(att_place, att_back)
    mixed_stream = inputs + jnp.sum(att_gate.T[:, :, None] * att_picked, 0)
    inverse_two = lax.rsqrt(jnp.mean(mixed_stream * mixed_stream, -1, keepdims=True) + norm_eps)
    normed_two = (mixed_stream * inverse_two * gain_second).astype(bf16)
    ffn_logits = mm(normed_two, ffn_all)
    ffn_gate, ffn_picks = gate_weights(ffn_logits, ffn_route, experts)
    ffn_place = placement_of(ffn_route, capacity, experts)
    ffn_rows = exchange(send_rows(ffn_place, normed_two, experts)).reshape(-1, model_width)
    grad_out = cotangent.astype(f32)
    ffn_rows, packed_grads = lax.optimization_barrier(
        (ffn_rows, send_grads(ffn_place, ffn_gate, grad_out, experts))
    )
    ffn_grad_rows = exchange(packed_grads).reshape(-1, model_width)
    gate_value = mm(ffn_rows, gate_all)
    up_value = mm(ffn_rows, up_all)
    sigmoid_gate = jax.nn.sigmoid(gate_value)
    hidden = (gate_value * sigmoid_gate * up_value).astype(bf16)
    down_part = mm_tn(hidden, ffn_grad_rows).astype(bf16)
    down_part, hidden, ffn_grad_rows = lax.optimization_barrier((down_part, hidden, ffn_grad_rows))
    down_sum = reduce_dp(down_part)
    ffn_branch = mm(hidden, down_all).astype(bf16)
    ffn_branch, ffn_grad_rows = lax.optimization_barrier((ffn_branch, ffn_grad_rows))
    ffn_back = exchange(ffn_branch.reshape(experts, capacity, -1))
    hidden_grad = mm_nt(ffn_grad_rows, down_all)
    gate_grad = (
        hidden_grad * up_value * sigmoid_gate * (1.0 + gate_value * (1.0 - sigmoid_gate))
    ).astype(bf16)
    up_grad = (hidden_grad * gate_value * sigmoid_gate).astype(bf16)
    ffn_rows_grad = (mm_nt(gate_grad, gate_all) + mm_nt(up_grad, up_all)).astype(bf16)
    ffn_rows_grad, gate_grad, up_grad, ffn_back = lax.optimization_barrier(
        (ffn_rows_grad, gate_grad, up_grad, ffn_back)
    )
    ffn_picked = take_back(ffn_place, ffn_back)
    result = mixed_stream + jnp.sum(ffn_gate.T[:, :, None] * ffn_picked, 0)
    ffn_logit_grad = router_back(ffn_gate, ffn_picks, ffn_picked, grad_out)
    ffn_rows_back = exchange(ffn_rows_grad.reshape(experts, capacity, -1)).reshape(
        experts * capacity, -1
    )
    gate_part = mm_tn(ffn_rows, gate_grad).astype(bf16)
    up_part = mm_tn(ffn_rows, up_grad).astype(bf16)
    gate_part, up_part, ffn_rows_back = lax.optimization_barrier(
        (gate_part, up_part, ffn_rows_back)
    )
    gate_sum = reduce_dp(gate_part)
    up_sum = reduce_dp(up_part)
    normed_two_grad = mm(ffn_place[0] + ffn_place[1], ffn_rows_back) + jnp.dot(
        ffn_logit_grad, ffn_all.astype(f32).T, precision=highest
    )
    gain_two_part = jnp.sum(normed_two_grad * mixed_stream * inverse_two, 0)
    mixed_grad = grad_out + norm_back(mixed_stream, inverse_two, gain_second, normed_two_grad)

    att_logit_grad = router_back(att_gate, att_picks, att_picked, mixed_grad)
    att_grad_rows = exchange(send_grads(att_place, att_gate, mixed_grad, experts)).reshape(
        -1, model_width
    )
    att_grad_rows, down_sum = lax.optimization_barrier((att_grad_rows, down_sum))
    attended_grad = mm_nt(att_grad_rows, output_all).astype(bf16)
    output_part = mm_tn(attended, att_grad_rows).astype(bf16)
    query_grad = jnp.zeros(queries.shape, f32)
    kv_grad = None
    for step in range(1, experts + 1):
        k = step % experts
        start = backs[k] * width
        group_grad = lax.dynamic_slice_in_dim(attended_grad, start, width, 1)
        group_query_grad, key_grad, value_grad = attend_back(*saved[k], group_grad)
        query_grad = lax.dynamic_update_slice_in_dim(query_grad, group_query_grad, start, 1)
        part = jnp.concatenate([key_grad, value_grad], 1)
        if step == 2:
            kv_grad, output_part = lax.optimization_barrier((kv_grad, output_part))
            output_sum = reduce_swaps(output_part)
        if k == 0:
            query_raw_grad = rotate_back(query_grad, query_cos, query_sin).astype(bf16)
            query_part = mm_tn(query_rows, query_raw_grad).astype(bf16)
            kv_grad, query_part, output_sum = lax.optimization_barrier(
                (kv_grad, query_part, output_sum)
            )
            query_sum = reduce_swaps(query_part)
        if kv_grad is not None:
            part = part + kv_grad.astype(f32)
        kv_grad = part if k == 0 else ring_step(part.astype(bf16), experts)
    att_rows_grad = mm_nt(query_raw_grad, query_all).astype(bf16)
    kv_raw_grad = jnp.concatenate(
        [rotate_back(kv_grad[:, :width], tree_cos, tree_sin), kv_grad[:, width:]], 1
    ).astype(bf16)
    tree_grad = mm_nt(kv_raw_grad, kv_all).reshape(experts, row_count, -1) + jnp.einsum(
        "ksr,ksd->krd",
        chosen,
        att_rows_grad.reshape(experts, capacity, -1),
        preferred_element_type=f32,
    )
    normed_one_grad = None
    for step in range(1, experts + 1):
        k = step % experts
        part = lax.dynamic_index_in_dim(tree_grad, backs[k], 0, keepdims=False)
        if normed_one_grad is not None:
            part = part + normed_one_grad.astype(f32)
        normed_one_grad = part if k == 0 else ring_step(part.astype(bf16), experts)
    normed_one_grad, query_sum = lax.optimization_barrier((normed_one_grad, query_sum))
    normed_one_grad = normed_one_grad + jnp.dot(
        att_logit_grad, att_all.astype(f32).T, precision=highest
    )
    gain_one_part = jnp.sum(normed_one_grad * inputs * inverse_one, 0)
    input_grad = mixed_grad + norm_back(inputs, inverse_one, gain_first, normed_one_grad)
    att_router_part = lax.dot_general(
        att_logit_grad, normed_one.astype(f32), (((0,), (0,)), ((), ())), precision=highest
    )
    ffn_router_part = lax.dot_general(
        ffn_logit_grad, normed_two.astype(f32), (((0,), (0,)), ((), ())), precision=highest
    )
    small_part = jnp.concatenate(
        [
            att_router_part,
            ffn_router_part,
            gain_one_part[None],
            gain_two_part[None],
            jnp.zeros((PAD - 2 * experts - 2, model_width), f32),
        ],
        0,
    ).astype(bf16)
    shared_part = jnp.concatenate(
        [
            mm_tn(normed_tree, kv_raw_grad).astype(bf16),
            mm_tn(small_part, jnp.eye(PAD, dtype=bf16)).astype(bf16),
        ],
        1,
    )
    shared_sum = exchange(reduce_dp(shared_part).reshape(experts, shard_rows, -1)).astype(f32)
    kv_sum = (
        shared_sum[:, :, : 2 * width]
        .reshape(experts, shard_rows, 2, width)
        .transpose(1, 2, 0, 3)
        .reshape(shard_rows, 2 * head_width)
    )
    small_sum = jnp.sum(shared_sum[:, :, 2 * width :], 0)
    return (
        result.astype(bf16),
        input_grad,
        small_sum[:, 2 * experts],
        small_sum[:, 2 * experts + 1],
        kv_sum,
        small_sum[:, :experts],
        small_sum[:, experts : 2 * experts],
        query_sum.astype(f32)[None],
        output_sum.astype(f32)[None],
        gate_sum.astype(f32)[None],
        up_sum.astype(f32)[None],
        down_sum.astype(f32)[None],
    )

def solution(mesh):
    in_specs = (
        P(("dp", "expert"), None),
        P(("dp", "expert"), None),
        P(("dp", "expert")),
        P(("dp", "expert")),
        P(("dp", "expert"), None),
        P(("dp", "expert"), None),
        P(("dp", "expert"), None),
        P("expert", "dp", None),
        P("expert", "dp", None),
        P("expert", "dp", None),
        P("expert", "dp", None),
        P("expert", "dp", None),
        P("dp", None),
        P(("dp", "expert"), None),
        P(("dp", "expert"), None),
    )
    out_specs = (
        P(("dp", "expert"), None),
        P(("dp", "expert"), None),
        P(("dp", "expert")),
        P(("dp", "expert")),
        P(("dp", "expert"), None),
        P(("dp", "expert"), None),
        P(("dp", "expert"), None),
        P("expert", "dp", None),
        P("expert", "dp", None),
        P("expert", "dp", None),
        P("expert", "dp", None),
        P("expert", "dp", None),
    )
    return jax.shard_map(body, mesh=mesh, in_specs=in_specs, out_specs=out_specs, check_vma=False)
```

```python
import jax
import jax.numpy as jnp
from jax import lax
from jax.sharding import PartitionSpec as P

HEADS = 16
HEAD = 128
TRUNK = 512
BRANCH = 64
LEAF = 32
PAD = 128


norm_eps = 1e-05
highest = lax.Precision.HIGHEST
masked_score = -1e30
score_scale = HEAD ** (-0.5)
bf16 = jnp.bfloat16
f32 = jnp.float32


def layout(row_index):
    past_trunk = row_index - TRUNK
    in_branch = (row_index >= TRUNK) & (past_trunk < 4 * BRANCH)
    leaf_offset = past_trunk - 4 * BRANCH
    segment = jnp.where(
        row_index < TRUNK,
        0,
        jnp.where(in_branch, 1 + past_trunk // BRANCH, 5 + leaf_offset // LEAF),
    )
    position = jnp.where(
        row_index < TRUNK,
        row_index,
        jnp.where(in_branch, TRUNK + past_trunk % BRANCH, TRUNK + BRANCH + leaf_offset % LEAF),
    )
    return (segment, position)


def visible(query_index, query_segment, key_index, key_segment, parents):
    leaf_slot = query_segment - 5
    branch_of = jnp.sum(
        jnp.where(
            leaf_slot[:, None] == jnp.arange(8, dtype=jnp.int32)[None, :], parents[None, :], 0
        ),
        1,
    )
    ancestor = jnp.where(query_segment >= 5, branch_of, -1)
    same_segment = (key_segment[None, :] == query_segment[:, None]) & (
        key_index[None, :] <= query_index[:, None]
    )
    from_trunk = (key_segment[None, :] == 0) & (query_segment[:, None] > 0)
    from_branch = key_segment[None, :] == ancestor[:, None]
    return same_segment | from_trunk | from_branch


def rotary_tables(position):
    half_width = HEAD // 2
    frequency = 10000.0 ** (-2.0 * jnp.arange(half_width, dtype=f32) / HEAD)
    angle = position.astype(f32)[:, None] * frequency[None, :]
    return (jnp.cos(angle), jnp.sin(angle))


def rotate(vector, cosine, sine_table):
    length, width = vector.shape
    heads_view = vector.reshape(length, width // HEAD, HEAD)
    lead_half = heads_view[..., : HEAD // 2]
    tail_half = heads_view[..., HEAD // 2 :]
    cos_part = cosine[:, None, :]
    sin_part = sine_table[:, None, :]
    turned = jnp.concatenate(
        [lead_half * cos_part - tail_half * sin_part, tail_half * cos_part + lead_half * sin_part],
        -1,
    )
    return turned.reshape(length, width)


def rotate_back(grad_in, cosine, sine_table):
    return rotate(grad_in, cosine, -sine_table)


def mm(left, right):
    return jnp.dot(left, right, preferred_element_type=f32)


def mm_tn(left, right):
    return lax.dot_general(left, right, (((0,), (0,)), ((), ())), preferred_element_type=f32)


def mm_nt(left, right):
    return lax.dot_general(left, right, (((1,), (1,)), ((), ())), preferred_element_type=f32)


def earlier_count(named):
    rows = named.shape[0]
    before = jnp.tril(jnp.ones((rows, rows), bf16), -1)
    return mm(before, named.astype(bf16)).astype(jnp.int32)


def placement_of(routes, capacity, experts):
    picks = (routes[:, :, None] == jnp.arange(experts, dtype=jnp.int32)[None, None, :]).astype(
        jnp.int32
    )
    rank = earlier_count(jnp.sum(picks, 1))
    target = routes * capacity + jnp.sum(picks * rank[:, None, :], 2)
    slots_all = jnp.arange(experts * capacity, dtype=jnp.int32)
    return (target.T[:, :, None] == slots_all[None, None, :]).astype(bf16)


def gate_weights(logits, routes, experts):
    picks = (routes[:, :, None] == jnp.arange(experts, dtype=jnp.int32)[None, None, :]).astype(f32)
    chosen = jnp.sum(picks * logits[:, None, :], -1)
    return (jax.nn.softmax(chosen, -1), picks)


def router_back(gates, picks, gate_grad):
    chosen_grad = gates * (gate_grad - jnp.sum(gates * gate_grad, 1, keepdims=True))
    return jnp.sum(picks * chosen_grad[:, :, None], 1)


def send_rows(place, values, experts):
    packed = mm_tn(place[0] + place[1], values).astype(bf16)
    return packed.reshape(experts, -1, values.shape[1])


def send_grads(place, gates, grad_in, experts):
    scaled = (gates.T[:, :, None] * grad_in[None]).astype(bf16)
    packed = (mm_tn(place[0], scaled[0]) + mm_tn(place[1], scaled[1])).astype(bf16)
    return packed.reshape(experts, -1, grad_in.shape[1])


def as_columns(values):
    high = lax.reduce_precision(values, 8, 7)
    rest = values - high
    middle = lax.reduce_precision(rest, 8, 7)
    columns = jnp.stack([high, middle, rest - middle], 1).astype(bf16)
    return jnp.pad(columns, ((0, 0), (0, PAD - 3)))


def take_back(place, returned):
    flat_back = returned.reshape(place.shape[2], -1)
    return jnp.stack([mm(place[0], flat_back), mm(place[1], flat_back)])


def exchange(packed):
    return lax.all_to_all(packed, "expert", split_axis=0, concat_axis=0, tiled=True)


def exchange_direct(packed, experts, own):
    received = jnp.zeros(packed.shape, packed.dtype)
    for k in range(experts):
        block = lax.dynamic_index_in_dim(packed, (own + k) % experts, 0)
        if k:
            block = lax.ppermute(block, "expert", [(i, (i + k) % experts) for i in range(experts)])
        received = lax.dynamic_update_slice_in_dim(received, block, (own - k) % experts, 0)
    return received


def ring_step(block, experts):
    return lax.ppermute(block, "expert", [(i, (i + 1) % experts) for i in range(experts)])


def ring_gather(block, experts):
    blocks = [block]
    for _ in range(experts - 1):
        blocks.append(ring_step(blocks[-1], experts))
    return blocks


def norm_back(stream, inverse, gain, grad_in):
    scaled = grad_in * gain
    return inverse * scaled - stream * inverse**3 * jnp.mean(scaled * stream, -1, keepdims=True)


def group_scores(queries, keys):
    heads = queries.shape[1] // HEAD
    return (
        jnp.einsum(
            "qhd,khd->hqk",
            queries.reshape(-1, heads, HEAD),
            keys.reshape(-1, heads, HEAD),
            preferred_element_type=f32,
        )
        * score_scale
    )


def attend(queries, keys, values, key_mask):
    heads = queries.shape[1] // HEAD
    scores = jnp.where(key_mask[None], group_scores(queries, keys), masked_score)
    row_peak = jnp.max(scores, -1, keepdims=True)
    exponent = jnp.exp(scores - row_peak)
    row_total = jnp.sum(exponent, -1, keepdims=True)
    attended = jnp.einsum(
        "hqk,khd->qhd",
        (exponent / row_total).astype(bf16),
        values.reshape(-1, heads, HEAD),
        preferred_element_type=f32,
    ).reshape(queries.shape)
    return (attended.astype(bf16), row_peak + jnp.log(row_total))


def attend_back(queries, keys, values, key_mask, log_total, attended, attended_grad):
    heads = queries.shape[1] // HEAD
    scores = jnp.where(key_mask[None], group_scores(queries, keys), masked_score)
    probs = jnp.exp(scores - log_total)
    grad_heads = attended_grad.reshape(-1, heads, HEAD)
    value_heads = values.reshape(-1, heads, HEAD)
    prob_grad = jnp.einsum("qhd,khd->hqk", grad_heads, value_heads, preferred_element_type=f32)
    row_delta = jnp.sum(
        grad_heads.astype(f32) * attended.reshape(-1, heads, HEAD).astype(f32), -1
    ).T[:, :, None]
    score_grad = (probs * (prob_grad - row_delta)).astype(bf16)
    query_grad = jnp.einsum(
        "hqk,khd->qhd", score_grad, keys.reshape(-1, heads, HEAD), preferred_element_type=f32
    ).reshape(queries.shape)
    key_grad = jnp.einsum(
        "hqk,qhd->khd", score_grad, queries.reshape(-1, heads, HEAD), preferred_element_type=f32
    ).reshape(keys.shape)
    value_grad = jnp.einsum(
        "hqk,qhd->khd", probs.astype(bf16), grad_heads, preferred_element_type=f32
    ).reshape(values.shape)
    return (query_grad * score_scale, key_grad * score_scale, value_grad)


def gather_dp(weight):
    return lax.all_gather(weight[0], "dp", axis=0, tiled=True)


def reduce_dp(part):
    return lax.psum_scatter(part, "dp", scatter_dimension=0, tiled=True)


def swap(block, bit):
    return lax.ppermute(block, "dp", [(i, i ^ bit) for i in range(8)])


def bit_of(value, bit):
    return (value // bit) % 2


def halves(block, axis, bit):
    pick = bit_of(lax.axis_index("dp"), bit)
    kept = lax.dynamic_index_in_dim(block, pick, axis, keepdims=False)
    sent = lax.dynamic_index_in_dim(block, 1 - pick, axis, keepdims=False)
    return (kept.astype(f32), sent.astype(bf16))


def fold(block, axis, bit):
    kept, sent = halves(block, axis, bit)
    return kept + swap(sent, bit).astype(f32)


def reduce_swaps(part):
    if lax.axis_size("dp") != 8:
        return reduce_dp(part).astype(f32)
    rows, columns = part.shape
    grid = fold(part.reshape(2, 2, 2, rows // 8, columns), 2, 1).astype(bf16)
    left, right = grid[..., : columns // 2], grid[..., columns // 2 :]
    left = fold(fold(left, 1, 2).astype(bf16), 0, 4)
    right = fold(fold(right, 0, 4).astype(bf16), 0, 2)
    return jnp.concatenate([left, right], 1)


def body(
    tokens,
    cotangent,
    gain_one,
    gain_two,
    kv_weight,
    att_router,
    ffn_router,
    query_weight,
    output_weight,
    gate_weight,
    up_weight,
    down_weight,
    leaf_parent,
    att_route,
    ffn_route,
):
    row_count, model_width = tokens.shape
    experts = att_router.shape[1]
    capacity = row_count * 5 // (2 * experts)
    head_width = HEADS * HEAD
    width = head_width // experts
    shard_rows = kv_weight.shape[0]
    parents = leaf_parent[0]
    own = lax.axis_index("expert")
    backs = [(own - k) % experts for k in range(experts)]

    small = jnp.concatenate(
        [
            att_router,
            ffn_router,
            gain_one[:, None],
            gain_two[:, None],
            jnp.zeros((shard_rows, PAD - 2 * experts - 2), bf16),
        ],
        1,
    )
    bundle = jnp.concatenate(
        [
            kv_weight.reshape(shard_rows, 2, experts, width)
            .transpose(2, 0, 1, 3)
            .reshape(experts, shard_rows, 2 * width),
            jnp.broadcast_to(small[None], (experts, shard_rows, PAD)),
        ],
        2,
    )
    bundle = exchange_direct(bundle, experts, own).reshape(experts * shard_rows, 2 * width + PAD)
    bundle = lax.all_gather(bundle, "dp", axis=0, tiled=True)
    kv_all = bundle[:, : 2 * width]
    att_all = bundle[:, 2 * width : 2 * width + experts]
    ffn_all = bundle[:, 2 * width + experts : 2 * width + 2 * experts]
    gain_first = bundle[:, 2 * width + 2 * experts].astype(f32)
    gain_second = bundle[:, 2 * width + 2 * experts + 1].astype(f32)

    query_all = gather_dp(query_weight)
    output_all = gather_dp(output_weight)
    gate_all = gather_dp(gate_weight)
    up_all = gather_dp(up_weight)
    down_all = gather_dp(down_weight)

    tagged = jnp.concatenate(
        [tokens, att_route.astype(bf16), jnp.zeros((row_count, PAD - 2), bf16)], 1
    )
    tree = jnp.zeros((experts * row_count, model_width + PAD), bf16)
    for k, block in enumerate(ring_gather(tagged, experts)):
        tree = lax.dynamic_update_slice_in_dim(tree, block, backs[k] * row_count, 0)
    tree_tokens = tree[:, :model_width].astype(f32)
    tree_routes = tree[:, model_width : model_width + 2].astype(jnp.int32)
    tree_index = jnp.arange(experts * row_count, dtype=jnp.int32)
    tree_segment, tree_position = layout(tree_index)
    tree_cos, tree_sin = rotary_tables(tree_position)
    tree_inverse = lax.rsqrt(jnp.mean(tree_tokens * tree_tokens, -1, keepdims=True) + norm_eps)
    normed_tree = (tree_tokens * tree_inverse * gain_first).astype(bf16)
    inputs = tokens.astype(f32)
    own_start = own * row_count
    inverse_one = lax.dynamic_slice_in_dim(tree_inverse, own_start, row_count, 0)
    normed_one = lax.dynamic_slice_in_dim(normed_tree, own_start, row_count, 0)

    kv_raw = mm(normed_tree, kv_all)
    kv_own = jnp.concatenate(
        [rotate(kv_raw[:, :width], tree_cos, tree_sin), kv_raw[:, width:]], 1
    ).astype(bf16)

    named = jnp.any(tree_routes == own, 1).reshape(experts, row_count)
    rank = earlier_count(named.T).T
    slots = jnp.arange(capacity, dtype=jnp.int32)
    chosen = named[:, None, :] & (rank[:, None, :] == slots[None, :, None])
    chosen_index = tree_index.reshape(experts, 1, row_count)
    query_index = jnp.sum(jnp.where(chosen, chosen_index, 0), 2).reshape(-1)
    chosen = chosen.astype(bf16)
    query_rows = (
        jnp.einsum(
            "ksr,krd->ksd",
            chosen,
            normed_tree.reshape(experts, row_count, model_width),
            preferred_element_type=f32,
        )
        .astype(bf16)
        .reshape(-1, model_width)
    )
    query_segment, query_position = layout(query_index)
    query_cos, query_sin = rotary_tables(query_position)
    key_mask = visible(query_index, query_segment, tree_index, tree_segment, parents)
    queries = rotate(mm(query_rows, query_all), query_cos, query_sin).astype(bf16)

    attended = jnp.zeros(queries.shape, bf16)
    saved = []
    kv_block = kv_own
    kv_next = ring_step(kv_own, experts)
    for k in range(experts):
        if k:
            kv_block = kv_next
            if k == 1:
                kv_block, queries = lax.optimization_barrier((kv_block, queries))
            else:
                kv_block, attended = lax.optimization_barrier((kv_block, attended))
            if k < experts - 1:
                kv_next = ring_step(kv_block, experts)
        start = backs[k] * width
        group_queries = lax.dynamic_slice_in_dim(queries, start, width, 1)
        keys, values = kv_block[:, :width], kv_block[:, width:]
        group_attended, log_total = attend(group_queries, keys, values, key_mask)
        attended = lax.dynamic_update_slice_in_dim(attended, group_attended, start, 1)
        saved.append((group_queries, keys, values, key_mask, log_total, group_attended))
    att_branch = mm(attended, output_all).astype(bf16)
    att_back = exchange(att_branch.reshape(experts, capacity, -1))

    att_logits = mm(normed_one, att_all)
    att_gate, att_picks = gate_weights(att_logits, att_route, experts)
    att_place = placement_of(att_route, capacity, experts)
    att_picked = take_back(att_place, att_back)
    mixed_stream = inputs + jnp.sum(att_gate.T[:, :, None] * att_picked, 0)
    inverse_two = lax.rsqrt(jnp.mean(mixed_stream * mixed_stream, -1, keepdims=True) + norm_eps)
    normed_two = (mixed_stream * inverse_two * gain_second).astype(bf16)
    ffn_logits = mm(normed_two, ffn_all)
    ffn_gate, ffn_picks = gate_weights(ffn_logits, ffn_route, experts)
    ffn_place = placement_of(ffn_route, capacity, experts)
    ffn_rows = exchange(send_rows(ffn_place, normed_two, experts)).reshape(-1, model_width)
    grad_out = cotangent.astype(f32)
    slot_gate = jnp.sum(ffn_place.astype(f32) * ffn_gate.T[:, :, None], (0, 1))
    packed_grads = jnp.concatenate(
        [
            send_rows(ffn_place, cotangent, experts),
            as_columns(slot_gate).reshape(experts, capacity, PAD),
        ],
        2,
    )
    ffn_rows, packed_grads = lax.optimization_barrier((ffn_rows, packed_grads))
    received_grads = exchange(packed_grads).reshape(experts * capacity, -1)
    out_rows = received_grads[:, :model_width]
    row_gate = jnp.sum(received_grads[:, model_width:].astype(f32), 1, keepdims=True)
    ffn_grad_rows = (row_gate * out_rows.astype(f32)).astype(bf16)
    gate_value = mm(ffn_rows, gate_all)
    up_value = mm(ffn_rows, up_all)
    sigmoid_gate = jax.nn.sigmoid(gate_value)
    hidden = (gate_value * sigmoid_gate * up_value).astype(bf16)
    down_part = mm_tn(hidden, ffn_grad_rows).astype(bf16)
    down_part, hidden, out_rows = lax.optimization_barrier((down_part, hidden, out_rows))
    down_sum = reduce_dp(down_part)
    hidden_pull = mm_nt(out_rows, down_all)
    row_pull = jnp.sum(hidden.astype(f32) * hidden_pull, 1)
    hidden_grad = row_gate * hidden_pull
    gate_grad = (
        hidden_grad * up_value * sigmoid_gate * (1.0 + gate_value * (1.0 - sigmoid_gate))
    ).astype(bf16)
    up_grad = (hidden_grad * gate_value * sigmoid_gate).astype(bf16)
    ffn_rows_grad = (mm_nt(gate_grad, gate_all) + mm_nt(up_grad, up_all)).astype(bf16)
    ffn_rows_grad = jnp.concatenate([ffn_rows_grad, as_columns(row_pull)], 1)
    ffn_rows_grad, gate_grad, up_grad = lax.optimization_barrier(
        (ffn_rows_grad, gate_grad, up_grad)
    )
    ffn_rows_back = exchange(ffn_rows_grad.reshape(experts, capacity, -1)).reshape(
        experts * capacity, -1
    )
    gate_part = mm_tn(ffn_rows, gate_grad).astype(bf16)
    up_part = mm_tn(ffn_rows, up_grad).astype(bf16)
    gate_part, up_part, ffn_rows_back = lax.optimization_barrier(
        (gate_part, up_part, ffn_rows_back)
    )
    gate_sum = reduce_dp(gate_part)
    up_sum = reduce_dp(up_part)
    gate_pull = jnp.sum(take_back(ffn_place, ffn_rows_back[:, model_width:]), 2).T
    ffn_logit_grad = router_back(ffn_gate, ffn_picks, gate_pull)
    normed_two_grad = mm(ffn_place[0] + ffn_place[1], ffn_rows_back[:, :model_width]) + jnp.dot(
        ffn_logit_grad, ffn_all.astype(f32).T, precision=highest
    )
    gain_two_part = jnp.sum(normed_two_grad * mixed_stream * inverse_two, 0)
    mixed_grad = grad_out + norm_back(mixed_stream, inverse_two, gain_second, normed_two_grad)

    att_logit_grad = router_back(
        att_gate, att_picks, jnp.sum(att_picked * mixed_grad[None], 2).T
    )
    packed_grads, hidden = lax.optimization_barrier(
        (send_grads(att_place, att_gate, mixed_grad, experts), hidden)
    )
    ffn_branch = mm(hidden, down_all).astype(bf16)
    att_grad_rows, ffn_branch = lax.optimization_barrier((exchange(packed_grads), ffn_branch))
    att_grad_rows = att_grad_rows.reshape(-1, model_width)
    ffn_back = exchange(ffn_branch.reshape(experts, capacity, -1))
    att_grad_rows, down_sum = lax.optimization_barrier((att_grad_rows, down_sum))
    attended_grad = mm_nt(att_grad_rows, output_all).astype(bf16)
    query_grad = jnp.zeros(queries.shape, f32)
    kv_grad = None
    for step in range(1, experts + 1):
        k = step % experts
        start = backs[k] * width
        group_grad = lax.dynamic_slice_in_dim(attended_grad, start, width, 1)
        group_query_grad, key_grad, value_grad = attend_back(*saved[k], group_grad)
        query_grad = lax.dynamic_update_slice_in_dim(query_grad, group_query_grad, start, 1)
        part = jnp.concatenate([key_grad, value_grad], 1)
        if kv_grad is not None:
            part = part + kv_grad.astype(f32)
        if k == 0:
            kv_grad = part
            continue
        part = part.astype(bf16)
        if step == 2:
            part, att_grad_rows, ffn_back = lax.optimization_barrier(
                (part, att_grad_rows, ffn_back)
            )
        if step == experts - 1:
            part, query_rows = lax.optimization_barrier((part, query_rows))
        kv_grad = ring_step(part, experts)
    ffn_picked = take_back(ffn_place, ffn_back)
    result = mixed_stream + jnp.sum(ffn_gate.T[:, :, None] * ffn_picked, 0)
    output_sum = reduce_swaps(mm_tn(attended, att_grad_rows).astype(bf16))
    query_raw_grad = rotate_back(query_grad, query_cos, query_sin).astype(bf16)
    query_sum = reduce_swaps(mm_tn(query_rows, query_raw_grad).astype(bf16))
    att_rows_grad = mm_nt(query_raw_grad, query_all).astype(bf16)
    kv_raw_grad = jnp.concatenate(
        [rotate_back(kv_grad[:, :width], tree_cos, tree_sin), kv_grad[:, width:]], 1
    ).astype(bf16)
    tree_grad = mm_nt(kv_raw_grad, kv_all).reshape(experts, row_count, -1) + jnp.einsum(
        "ksr,ksd->krd",
        chosen,
        att_rows_grad.reshape(experts, capacity, -1),
        preferred_element_type=f32,
    )
    router_grad = jnp.dot(att_logit_grad, att_all.astype(f32).T, precision=highest)
    gain_one_part = jnp.sum(router_grad * inputs * inverse_one, 0) + jnp.sum(
        tree_grad.reshape(tree_tokens.shape) * tree_tokens * tree_inverse, 0
    )
    att_router_part = lax.dot_general(
        att_logit_grad, normed_one.astype(f32), (((0,), (0,)), ((), ())), precision=highest
    )
    ffn_router_part = lax.dot_general(
        ffn_logit_grad, normed_two.astype(f32), (((0,), (0,)), ((), ())), precision=highest
    )
    small_part = jnp.concatenate(
        [
            att_router_part,
            ffn_router_part,
            gain_one_part[None],
            gain_two_part[None],
            jnp.zeros((PAD - 2 * experts - 2, model_width), f32),
        ],
        0,
    ).astype(bf16)
    shared_part = jnp.concatenate(
        [
            mm_tn(normed_tree, kv_raw_grad).astype(bf16),
            mm_tn(small_part, jnp.eye(PAD, dtype=bf16)).astype(bf16),
        ],
        1,
    )
    normed_one_grad = None
    for step in range(1, experts + 1):
        k = step % experts
        part = lax.dynamic_index_in_dim(tree_grad, backs[k], 0, keepdims=False)
        if normed_one_grad is not None:
            part = part + normed_one_grad.astype(f32)
        normed_one_grad = part if k == 0 else ring_step(part.astype(bf16), experts)
        if step == 1:
            normed_one_grad, output_sum = lax.optimization_barrier((normed_one_grad, output_sum))
    normed_one_grad, query_sum, shared_part = lax.optimization_barrier(
        (normed_one_grad, query_sum, shared_part)
    )
    normed_one_grad = normed_one_grad + router_grad
    input_grad = mixed_grad + norm_back(inputs, inverse_one, gain_first, normed_one_grad)
    shared_sum = exchange(reduce_dp(shared_part).reshape(experts, shard_rows, -1)).astype(f32)
    kv_sum = (
        shared_sum[:, :, : 2 * width]
        .reshape(experts, shard_rows, 2, width)
        .transpose(1, 2, 0, 3)
        .reshape(shard_rows, 2 * head_width)
    )
    small_sum = jnp.sum(shared_sum[:, :, 2 * width :], 0)
    return (
        result.astype(bf16),
        input_grad,
        small_sum[:, 2 * experts],
        small_sum[:, 2 * experts + 1],
        kv_sum,
        small_sum[:, :experts],
        small_sum[:, experts : 2 * experts],
        query_sum.astype(f32)[None],
        output_sum.astype(f32)[None],
        gate_sum.astype(f32)[None],
        up_sum.astype(f32)[None],
        down_sum.astype(f32)[None],
    )

def solution(mesh):
    in_specs = (
        P(("dp", "expert"), None),
        P(("dp", "expert"), None),
        P(("dp", "expert")),
        P(("dp", "expert")),
        P(("dp", "expert"), None),
        P(("dp", "expert"), None),
        P(("dp", "expert"), None),
        P("expert", "dp", None),
        P("expert", "dp", None),
        P("expert", "dp", None),
        P("expert", "dp", None),
        P("expert", "dp", None),
        P("dp", None),
        P(("dp", "expert"), None),
        P(("dp", "expert"), None),
    )
    out_specs = (
        P(("dp", "expert"), None),
        P(("dp", "expert"), None),
        P(("dp", "expert")),
        P(("dp", "expert")),
        P(("dp", "expert"), None),
        P(("dp", "expert"), None),
        P(("dp", "expert"), None),
        P("expert", "dp", None),
        P("expert", "dp", None),
        P("expert", "dp", None),
        P("expert", "dp", None),
        P("expert", "dp", None),
    )
    return jax.shard_map(body, mesh=mesh, in_specs=in_specs, out_specs=out_specs, check_vma=False)
```

```python
import jax
import jax.numpy as jnp
from jax import lax
from jax.sharding import PartitionSpec as P

HEADS = 16
HEAD = 128
TRUNK = 512
BRANCH = 64
LEAF = 32
PAD = 128


norm_eps = 1e-05
highest = lax.Precision.HIGHEST
masked_score = -1e30
score_scale = HEAD ** (-0.5)
bf16 = jnp.bfloat16
f32 = jnp.float32


def layout(row_index):
    past_trunk = row_index - TRUNK
    in_branch = (row_index >= TRUNK) & (past_trunk < 4 * BRANCH)
    leaf_offset = past_trunk - 4 * BRANCH
    segment = jnp.where(
        row_index < TRUNK,
        0,
        jnp.where(in_branch, 1 + past_trunk // BRANCH, 5 + leaf_offset // LEAF),
    )
    position = jnp.where(
        row_index < TRUNK,
        row_index,
        jnp.where(in_branch, TRUNK + past_trunk % BRANCH, TRUNK + BRANCH + leaf_offset % LEAF),
    )
    return (segment, position)


def visible(query_index, query_segment, key_index, key_segment, parents):
    leaf_slot = query_segment - 5
    branch_of = jnp.sum(
        jnp.where(
            leaf_slot[:, None] == jnp.arange(8, dtype=jnp.int32)[None, :], parents[None, :], 0
        ),
        1,
    )
    ancestor = jnp.where(query_segment >= 5, branch_of, -1)
    same_segment = (key_segment[None, :] == query_segment[:, None]) & (
        key_index[None, :] <= query_index[:, None]
    )
    from_trunk = (key_segment[None, :] == 0) & (query_segment[:, None] > 0)
    from_branch = key_segment[None, :] == ancestor[:, None]
    return same_segment | from_trunk | from_branch


def rotary_tables(position):
    half_width = HEAD // 2
    frequency = 10000.0 ** (-2.0 * jnp.arange(half_width, dtype=f32) / HEAD)
    angle = position.astype(f32)[:, None] * frequency[None, :]
    return (jnp.cos(angle), jnp.sin(angle))


def rotate(vector, cosine, sine_table):
    length, width = vector.shape
    heads_view = vector.reshape(length, width // HEAD, HEAD)
    lead_half = heads_view[..., : HEAD // 2]
    tail_half = heads_view[..., HEAD // 2 :]
    cos_part = cosine[:, None, :]
    sin_part = sine_table[:, None, :]
    turned = jnp.concatenate(
        [lead_half * cos_part - tail_half * sin_part, tail_half * cos_part + lead_half * sin_part],
        -1,
    )
    return turned.reshape(length, width)


def rotate_back(grad_in, cosine, sine_table):
    return rotate(grad_in, cosine, -sine_table)


def mm(left, right):
    return jnp.dot(left, right, preferred_element_type=f32)


def mm_tn(left, right):
    return lax.dot_general(left, right, (((0,), (0,)), ((), ())), preferred_element_type=f32)


def mm_nt(left, right):
    return lax.dot_general(left, right, (((1,), (1,)), ((), ())), preferred_element_type=f32)


def earlier_count(named):
    rows = named.shape[0]
    before = jnp.tril(jnp.ones((rows, rows), bf16), -1)
    return mm(before, named.astype(bf16)).astype(jnp.int32)


def placement_of(routes, capacity, experts):
    picks = (routes[:, :, None] == jnp.arange(experts, dtype=jnp.int32)[None, None, :]).astype(
        jnp.int32
    )
    rank = earlier_count(jnp.sum(picks, 1))
    target = routes * capacity + jnp.sum(picks * rank[:, None, :], 2)
    slots_all = jnp.arange(experts * capacity, dtype=jnp.int32)
    return (target.T[:, :, None] == slots_all[None, None, :]).astype(bf16)


def gate_weights(logits, routes, experts):
    picks = (routes[:, :, None] == jnp.arange(experts, dtype=jnp.int32)[None, None, :]).astype(f32)
    chosen = jnp.sum(picks * logits[:, None, :], -1)
    return (jax.nn.softmax(chosen, -1), picks)


def router_back(gates, picks, gate_grad):
    chosen_grad = gates * (gate_grad - jnp.sum(gates * gate_grad, 1, keepdims=True))
    return jnp.sum(picks * chosen_grad[:, :, None], 1)


def send_rows(place, values, experts):
    packed = mm_tn(place[0] + place[1], values).astype(bf16)
    return packed.reshape(experts, -1, values.shape[1])


def send_grads(place, gates, grad_in, experts):
    scaled = (gates.T[:, :, None] * grad_in[None]).astype(bf16)
    packed = (mm_tn(place[0], scaled[0]) + mm_tn(place[1], scaled[1])).astype(bf16)
    return packed.reshape(experts, -1, grad_in.shape[1])


def as_columns(values):
    high = lax.reduce_precision(values, 8, 7)
    rest = values - high
    middle = lax.reduce_precision(rest, 8, 7)
    columns = jnp.stack([high, middle, rest - middle], 1).astype(bf16)
    return jnp.pad(columns, ((0, 0), (0, PAD - 3)))


def take_back(place, returned):
    flat_back = returned.reshape(place.shape[2], -1)
    return jnp.stack([mm(place[0], flat_back), mm(place[1], flat_back)])


def exchange(packed):
    return lax.all_to_all(packed, "expert", split_axis=0, concat_axis=0, tiled=True)


def exchange_direct(packed, experts, own):
    received = jnp.zeros(packed.shape, packed.dtype)
    for k in range(experts):
        block = lax.dynamic_index_in_dim(packed, (own + k) % experts, 0)
        if k:
            block = lax.ppermute(block, "expert", [(i, (i + k) % experts) for i in range(experts)])
        received = lax.dynamic_update_slice_in_dim(received, block, (own - k) % experts, 0)
    return received


def ring_step(block, experts):
    return lax.ppermute(block, "expert", [(i, (i + 1) % experts) for i in range(experts)])


def ring_gather(block, experts):
    blocks = [block]
    for _ in range(experts - 1):
        blocks.append(ring_step(blocks[-1], experts))
    return blocks


def norm_back(stream, inverse, gain, grad_in):
    scaled = grad_in * gain
    return inverse * scaled - stream * inverse**3 * jnp.mean(scaled * stream, -1, keepdims=True)


def group_scores(queries, keys):
    heads = queries.shape[1] // HEAD
    return (
        jnp.einsum(
            "qhd,khd->hqk",
            queries.reshape(-1, heads, HEAD),
            keys.reshape(-1, heads, HEAD),
            preferred_element_type=f32,
        )
        * score_scale
    )


def attend(queries, keys, values, key_mask):
    heads = queries.shape[1] // HEAD
    scores = jnp.where(key_mask[None], group_scores(queries, keys), masked_score)
    row_peak = jnp.max(scores, -1, keepdims=True)
    exponent = jnp.exp(scores - row_peak)
    row_total = jnp.sum(exponent, -1, keepdims=True)
    attended = jnp.einsum(
        "hqk,khd->qhd",
        (exponent / row_total).astype(bf16),
        values.reshape(-1, heads, HEAD),
        preferred_element_type=f32,
    ).reshape(queries.shape)
    return (attended.astype(bf16), row_peak + jnp.log(row_total))


def attend_back(queries, keys, values, key_mask, log_total, attended, attended_grad):
    heads = queries.shape[1] // HEAD
    scores = jnp.where(key_mask[None], group_scores(queries, keys), masked_score)
    probs = jnp.exp(scores - log_total)
    grad_heads = attended_grad.reshape(-1, heads, HEAD)
    value_heads = values.reshape(-1, heads, HEAD)
    prob_grad = jnp.einsum("qhd,khd->hqk", grad_heads, value_heads, preferred_element_type=f32)
    row_delta = jnp.sum(
        grad_heads.astype(f32) * attended.reshape(-1, heads, HEAD).astype(f32), -1
    ).T[:, :, None]
    score_grad = (probs * (prob_grad - row_delta)).astype(bf16)
    query_grad = jnp.einsum(
        "hqk,khd->qhd", score_grad, keys.reshape(-1, heads, HEAD), preferred_element_type=f32
    ).reshape(queries.shape)
    key_grad = jnp.einsum(
        "hqk,qhd->khd", score_grad, queries.reshape(-1, heads, HEAD), preferred_element_type=f32
    ).reshape(keys.shape)
    value_grad = jnp.einsum(
        "hqk,qhd->khd", probs.astype(bf16), grad_heads, preferred_element_type=f32
    ).reshape(values.shape)
    return (query_grad * score_scale, key_grad * score_scale, value_grad)


def gather_dp(weight):
    return lax.all_gather(weight[0], "dp", axis=0, tiled=True)


def reduce_dp(part):
    return lax.psum_scatter(part, "dp", scatter_dimension=0, tiled=True)


def swap(block, bit):
    return lax.ppermute(block, "dp", [(i, i ^ bit) for i in range(8)])


def bit_of(value, bit):
    return (value // bit) % 2


def halves(block, axis, bit):
    pick = bit_of(lax.axis_index("dp"), bit)
    kept = lax.dynamic_index_in_dim(block, pick, axis, keepdims=False)
    sent = lax.dynamic_index_in_dim(block, 1 - pick, axis, keepdims=False)
    return (kept.astype(f32), sent.astype(bf16))


def fold(block, axis, bit):
    kept, sent = halves(block, axis, bit)
    return kept + swap(sent, bit).astype(f32)


def reduce_swaps(part):
    if lax.axis_size("dp") != 8:
        return reduce_dp(part).astype(f32)
    rows, columns = part.shape
    grid = fold(part.reshape(2, 2, 2, rows // 8, columns), 2, 1).astype(bf16)
    left, right = grid[..., : columns // 2], grid[..., columns // 2 :]
    left = fold(fold(left, 1, 2).astype(bf16), 0, 4)
    right = fold(fold(right, 0, 4).astype(bf16), 0, 2)
    return jnp.concatenate([left, right], 1)


def body(
    tokens,
    cotangent,
    gain_one,
    gain_two,
    kv_weight,
    att_router,
    ffn_router,
    query_weight,
    output_weight,
    gate_weight,
    up_weight,
    down_weight,
    leaf_parent,
    att_route,
    ffn_route,
):
    row_count, model_width = tokens.shape
    experts = att_router.shape[1]
    capacity = row_count * 5 // (2 * experts)
    head_width = HEADS * HEAD
    width = head_width // experts
    shard_rows = kv_weight.shape[0]
    parents = leaf_parent[0]
    own = lax.axis_index("expert")
    backs = [(own - k) % experts for k in range(experts)]

    small = jnp.concatenate(
        [
            att_router,
            ffn_router,
            gain_one[:, None],
            gain_two[:, None],
            jnp.zeros((shard_rows, PAD - 2 * experts - 2), bf16),
        ],
        1,
    )
    bundle = jnp.concatenate(
        [
            kv_weight.reshape(shard_rows, 2, experts, width)
            .transpose(2, 0, 1, 3)
            .reshape(experts, shard_rows, 2 * width),
            jnp.broadcast_to(small[None], (experts, shard_rows, PAD)),
        ],
        2,
    )
    bundle = exchange_direct(bundle, experts, own).reshape(experts * shard_rows, 2 * width + PAD)
    bundle = lax.all_gather(bundle, "dp", axis=0, tiled=True)
    kv_all = bundle[:, : 2 * width]
    att_all = bundle[:, 2 * width : 2 * width + experts]
    ffn_all = bundle[:, 2 * width + experts : 2 * width + 2 * experts]
    gain_first = bundle[:, 2 * width + 2 * experts].astype(f32)
    gain_second = bundle[:, 2 * width + 2 * experts + 1].astype(f32)

    query_all = gather_dp(query_weight)
    output_all = gather_dp(output_weight)
    gate_all = gather_dp(gate_weight)
    up_all = gather_dp(up_weight)
    down_all = gather_dp(down_weight)

    tagged = jnp.concatenate(
        [tokens, att_route.astype(bf16), jnp.zeros((row_count, PAD - 2), bf16)], 1
    )
    tree = jnp.zeros((experts * row_count, model_width + PAD), bf16)
    for k, block in enumerate(ring_gather(tagged, experts)):
        tree = lax.dynamic_update_slice_in_dim(tree, block, backs[k] * row_count, 0)
    tree_tokens = tree[:, :model_width].astype(f32)
    tree_routes = tree[:, model_width : model_width + 2].astype(jnp.int32)
    tree_index = jnp.arange(experts * row_count, dtype=jnp.int32)
    tree_segment, tree_position = layout(tree_index)
    tree_cos, tree_sin = rotary_tables(tree_position)
    tree_inverse = lax.rsqrt(jnp.mean(tree_tokens * tree_tokens, -1, keepdims=True) + norm_eps)
    normed_tree = (tree_tokens * tree_inverse * gain_first).astype(bf16)
    inputs = tokens.astype(f32)
    own_start = own * row_count
    inverse_one = lax.dynamic_slice_in_dim(tree_inverse, own_start, row_count, 0)
    normed_one = lax.dynamic_slice_in_dim(normed_tree, own_start, row_count, 0)

    kv_raw = mm(normed_tree, kv_all)
    kv_own = jnp.concatenate(
        [rotate(kv_raw[:, :width], tree_cos, tree_sin), kv_raw[:, width:]], 1
    ).astype(bf16)

    named = jnp.any(tree_routes == own, 1).reshape(experts, row_count)
    rank = earlier_count(named.T).T
    slots = jnp.arange(capacity, dtype=jnp.int32)
    chosen = named[:, None, :] & (rank[:, None, :] == slots[None, :, None])
    chosen_index = tree_index.reshape(experts, 1, row_count)
    query_index = jnp.sum(jnp.where(chosen, chosen_index, 0), 2).reshape(-1)
    chosen = chosen.astype(bf16)
    query_rows = (
        jnp.einsum(
            "ksr,krd->ksd",
            chosen,
            normed_tree.reshape(experts, row_count, model_width),
            preferred_element_type=f32,
        )
        .astype(bf16)
        .reshape(-1, model_width)
    )
    query_segment, query_position = layout(query_index)
    query_cos, query_sin = rotary_tables(query_position)
    key_mask = visible(query_index, query_segment, tree_index, tree_segment, parents)
    queries = rotate(mm(query_rows, query_all), query_cos, query_sin).astype(bf16)

    attended = jnp.zeros(queries.shape, bf16)
    saved = []
    kv_block = kv_own
    kv_next = ring_step(kv_own, experts)
    for k in range(experts):
        if k:
            kv_block = kv_next
            if k == 1:
                kv_block, queries = lax.optimization_barrier((kv_block, queries))
            else:
                kv_block, attended = lax.optimization_barrier((kv_block, attended))
            if k < experts - 1:
                kv_next = ring_step(kv_block, experts)
        start = backs[k] * width
        group_queries = lax.dynamic_slice_in_dim(queries, start, width, 1)
        keys, values = kv_block[:, :width], kv_block[:, width:]
        group_attended, log_total = attend(group_queries, keys, values, key_mask)
        attended = lax.dynamic_update_slice_in_dim(attended, group_attended, start, 1)
        saved.append((group_queries, keys, values, key_mask, log_total, group_attended))
    att_branch = mm(attended, output_all).astype(bf16)
    att_back = exchange(att_branch.reshape(experts, capacity, -1))

    att_logits = mm(normed_one, att_all)
    att_gate, att_picks = gate_weights(att_logits, att_route, experts)
    att_place = placement_of(att_route, capacity, experts)
    att_picked = take_back(att_place, att_back)
    mixed_stream = inputs + jnp.sum(att_gate.T[:, :, None] * att_picked, 0)
    inverse_two = lax.rsqrt(jnp.mean(mixed_stream * mixed_stream, -1, keepdims=True) + norm_eps)
    normed_two = (mixed_stream * inverse_two * gain_second).astype(bf16)
    ffn_logits = mm(normed_two, ffn_all)
    ffn_gate, ffn_picks = gate_weights(ffn_logits, ffn_route, experts)
    ffn_place = placement_of(ffn_route, capacity, experts)
    ffn_rows = exchange(send_rows(ffn_place, normed_two, experts)).reshape(-1, model_width)
    grad_out = cotangent.astype(f32)
    slot_gate = jnp.sum(ffn_place.astype(f32) * ffn_gate.T[:, :, None], (0, 1))
    packed_grads = jnp.concatenate(
        [
            send_rows(ffn_place, cotangent, experts),
            as_columns(slot_gate).reshape(experts, capacity, PAD),
        ],
        2,
    )
    ffn_rows, packed_grads = lax.optimization_barrier((ffn_rows, packed_grads))
    gate_value = mm(ffn_rows, gate_all)
    up_value = mm(ffn_rows, up_all)
    sigmoid_gate = jax.nn.sigmoid(gate_value)
    hidden = (gate_value * sigmoid_gate * up_value).astype(bf16)
    received_grads, hidden = lax.optimization_barrier((exchange(packed_grads), hidden))
    received_grads = received_grads.reshape(experts * capacity, -1)
    out_rows = received_grads[:, :model_width]
    row_gate = jnp.sum(received_grads[:, model_width:].astype(f32), 1, keepdims=True)
    ffn_grad_rows = (row_gate * out_rows.astype(f32)).astype(bf16)
    down_part = mm_tn(hidden, ffn_grad_rows).astype(bf16)
    down_part, hidden, out_rows = lax.optimization_barrier((down_part, hidden, out_rows))
    down_sum = reduce_dp(down_part)
    hidden_pull = mm_nt(out_rows, down_all)
    row_pull = jnp.sum(hidden.astype(f32) * hidden_pull, 1)
    hidden_grad = row_gate * hidden_pull
    gate_grad = (
        hidden_grad * up_value * sigmoid_gate * (1.0 + gate_value * (1.0 - sigmoid_gate))
    ).astype(bf16)
    up_grad = (hidden_grad * gate_value * sigmoid_gate).astype(bf16)
    ffn_rows_grad = (mm_nt(gate_grad, gate_all) + mm_nt(up_grad, up_all)).astype(bf16)
    ffn_rows_grad = jnp.concatenate([ffn_rows_grad, as_columns(row_pull)], 1)
    ffn_rows_grad, gate_grad, up_grad = lax.optimization_barrier(
        (ffn_rows_grad, gate_grad, up_grad)
    )
    ffn_rows_back = exchange(ffn_rows_grad.reshape(experts, capacity, -1)).reshape(
        experts * capacity, -1
    )
    gate_part = mm_tn(ffn_rows, gate_grad).astype(bf16)
    up_part = mm_tn(ffn_rows, up_grad).astype(bf16)
    gate_part, up_part, ffn_rows_back = lax.optimization_barrier(
        (gate_part, up_part, ffn_rows_back)
    )
    gate_sum = reduce_dp(gate_part)
    up_sum = reduce_dp(up_part)
    gate_pull = jnp.sum(take_back(ffn_place, ffn_rows_back[:, model_width:]), 2).T
    ffn_logit_grad = router_back(ffn_gate, ffn_picks, gate_pull)
    normed_two_grad = mm(ffn_place[0] + ffn_place[1], ffn_rows_back[:, :model_width]) + jnp.dot(
        ffn_logit_grad, ffn_all.astype(f32).T, precision=highest
    )
    gain_two_part = jnp.sum(normed_two_grad * mixed_stream * inverse_two, 0)
    mixed_grad = grad_out + norm_back(mixed_stream, inverse_two, gain_second, normed_two_grad)

    att_logit_grad = router_back(
        att_gate, att_picks, jnp.sum(att_picked * mixed_grad[None], 2).T
    )
    packed_grads, hidden = lax.optimization_barrier(
        (send_grads(att_place, att_gate, mixed_grad, experts), hidden)
    )
    ffn_branch = mm(hidden, down_all).astype(bf16)
    att_grad_rows, ffn_branch = lax.optimization_barrier((exchange(packed_grads), ffn_branch))
    att_grad_rows = att_grad_rows.reshape(-1, model_width)
    ffn_back = exchange(ffn_branch.reshape(experts, capacity, -1))
    att_grad_rows, down_sum = lax.optimization_barrier((att_grad_rows, down_sum))
    attended_grad = mm_nt(att_grad_rows, output_all).astype(bf16)
    query_grad = jnp.zeros(queries.shape, f32)
    kv_grad = None
    for step in range(1, experts + 1):
        k = step % experts
        start = backs[k] * width
        group_grad = lax.dynamic_slice_in_dim(
            attended_grad if step < 4 else late_grad, start, width, 1
        )
        group_query_grad, key_grad, value_grad = attend_back(*saved[k], group_grad)
        query_grad = lax.dynamic_update_slice_in_dim(query_grad, group_query_grad, start, 1)
        part = jnp.concatenate([key_grad, value_grad], 1)
        if kv_grad is not None:
            part = part + kv_grad.astype(f32)
        if k == 0:
            kv_grad = part
            continue
        part = part.astype(bf16)
        if step == 2:
            part, att_grad_rows, ffn_back, late_grad = lax.optimization_barrier(
                (part, att_grad_rows, ffn_back, attended_grad)
            )
        if step == experts - 1:
            part, query_rows = lax.optimization_barrier((part, query_rows))
        kv_grad = ring_step(part, experts)
    ffn_picked = take_back(ffn_place, ffn_back)
    result = mixed_stream + jnp.sum(ffn_gate.T[:, :, None] * ffn_picked, 0)
    output_sum = reduce_swaps(mm_tn(attended, att_grad_rows).astype(bf16))
    query_raw_grad = rotate_back(query_grad, query_cos, query_sin).astype(bf16)
    query_sum = reduce_swaps(mm_tn(query_rows, query_raw_grad).astype(bf16))
    att_rows_grad = mm_nt(query_raw_grad, query_all).astype(bf16)
    kv_raw_grad = jnp.concatenate(
        [rotate_back(kv_grad[:, :width], tree_cos, tree_sin), kv_grad[:, width:]], 1
    ).astype(bf16)
    tree_grad = mm_nt(kv_raw_grad, kv_all).reshape(experts, row_count, -1) + jnp.einsum(
        "ksr,ksd->krd",
        chosen,
        att_rows_grad.reshape(experts, capacity, -1),
        preferred_element_type=f32,
    )
    router_grad = jnp.dot(att_logit_grad, att_all.astype(f32).T, precision=highest)
    gain_one_part = jnp.sum(router_grad * inputs * inverse_one, 0) + jnp.sum(
        tree_grad.reshape(tree_tokens.shape) * tree_tokens * tree_inverse, 0
    )
    att_router_part = lax.dot_general(
        att_logit_grad, normed_one.astype(f32), (((0,), (0,)), ((), ())), precision=highest
    )
    ffn_router_part = lax.dot_general(
        ffn_logit_grad, normed_two.astype(f32), (((0,), (0,)), ((), ())), precision=highest
    )
    small_part = jnp.concatenate(
        [
            att_router_part,
            ffn_router_part,
            gain_one_part[None],
            gain_two_part[None],
            jnp.zeros((PAD - 2 * experts - 2, model_width), f32),
        ],
        0,
    ).astype(bf16)
    shared_part = jnp.concatenate(
        [
            mm_tn(normed_tree, kv_raw_grad).astype(bf16),
            mm_tn(small_part, jnp.eye(PAD, dtype=bf16)).astype(bf16),
        ],
        1,
    )
    normed_one_grad = None
    for step in range(1, experts + 1):
        k = step % experts
        part = lax.dynamic_index_in_dim(tree_grad, backs[k], 0, keepdims=False)
        if normed_one_grad is not None:
            part = part + normed_one_grad.astype(f32)
        normed_one_grad = part if k == 0 else ring_step(part.astype(bf16), experts)
        if step == experts - 1:
            normed_one_grad, shared_part = lax.optimization_barrier(
                (normed_one_grad, reduce_dp(shared_part))
            )
        if step == 1:
            normed_one_grad, output_sum = lax.optimization_barrier((normed_one_grad, output_sum))
    normed_one_grad, query_sum = lax.optimization_barrier((normed_one_grad, query_sum))
    normed_one_grad = normed_one_grad + router_grad
    input_grad = mixed_grad + norm_back(inputs, inverse_one, gain_first, normed_one_grad)
    shared_sum = exchange(shared_part.reshape(experts, shard_rows, -1)).astype(f32)
    kv_sum = (
        shared_sum[:, :, : 2 * width]
        .reshape(experts, shard_rows, 2, width)
        .transpose(1, 2, 0, 3)
        .reshape(shard_rows, 2 * head_width)
    )
    small_sum = jnp.sum(shared_sum[:, :, 2 * width :], 0)
    return (
        result.astype(bf16),
        input_grad,
        small_sum[:, 2 * experts],
        small_sum[:, 2 * experts + 1],
        kv_sum,
        small_sum[:, :experts],
        small_sum[:, experts : 2 * experts],
        query_sum.astype(f32)[None],
        output_sum.astype(f32)[None],
        gate_sum.astype(f32)[None],
        up_sum.astype(f32)[None],
        down_sum.astype(f32)[None],
    )

def solution(mesh):
    in_specs = (
        P(("dp", "expert"), None),
        P(("dp", "expert"), None),
        P(("dp", "expert")),
        P(("dp", "expert")),
        P(("dp", "expert"), None),
        P(("dp", "expert"), None),
        P(("dp", "expert"), None),
        P("expert", "dp", None),
        P("expert", "dp", None),
        P("expert", "dp", None),
        P("expert", "dp", None),
        P("expert", "dp", None),
        P("dp", None),
        P(("dp", "expert"), None),
        P(("dp", "expert"), None),
    )
    out_specs = (
        P(("dp", "expert"), None),
        P(("dp", "expert"), None),
        P(("dp", "expert")),
        P(("dp", "expert")),
        P(("dp", "expert"), None),
        P(("dp", "expert"), None),
        P(("dp", "expert"), None),
        P("expert", "dp", None),
        P("expert", "dp", None),
        P("expert", "dp", None),
        P("expert", "dp", None),
        P("expert", "dp", None),
    )
    return jax.shard_map(body, mesh=mesh, in_specs=in_specs, out_specs=out_specs, check_vma=False)
```

```python
import jax
import jax.numpy as jnp
from jax import lax
from jax.sharding import PartitionSpec as P

HEADS = 16
HEAD = 128
TRUNK = 512
BRANCH = 64
LEAF = 32
PAD = 128


norm_eps = 1e-05
highest = lax.Precision.HIGHEST
masked_score = -1e30
score_scale = HEAD ** (-0.5)
bf16 = jnp.bfloat16
f32 = jnp.float32


def layout(row_index):
    past_trunk = row_index - TRUNK
    in_branch = (row_index >= TRUNK) & (past_trunk < 4 * BRANCH)
    leaf_offset = past_trunk - 4 * BRANCH
    segment = jnp.where(
        row_index < TRUNK,
        0,
        jnp.where(in_branch, 1 + past_trunk // BRANCH, 5 + leaf_offset // LEAF),
    )
    position = jnp.where(
        row_index < TRUNK,
        row_index,
        jnp.where(in_branch, TRUNK + past_trunk % BRANCH, TRUNK + BRANCH + leaf_offset % LEAF),
    )
    return (segment, position)


def visible(query_index, query_segment, key_index, key_segment, parents):
    leaf_slot = query_segment - 5
    branch_of = jnp.sum(
        jnp.where(
            leaf_slot[:, None] == jnp.arange(8, dtype=jnp.int32)[None, :], parents[None, :], 0
        ),
        1,
    )
    ancestor = jnp.where(query_segment >= 5, branch_of, -1)
    same_segment = (key_segment[None, :] == query_segment[:, None]) & (
        key_index[None, :] <= query_index[:, None]
    )
    from_trunk = (key_segment[None, :] == 0) & (query_segment[:, None] > 0)
    from_branch = key_segment[None, :] == ancestor[:, None]
    return same_segment | from_trunk | from_branch


def rotary_tables(position):
    half_width = HEAD // 2
    frequency = 10000.0 ** (-2.0 * jnp.arange(half_width, dtype=f32) / HEAD)
    angle = position.astype(f32)[:, None] * frequency[None, :]
    return (jnp.cos(angle), jnp.sin(angle))


def rotate(vector, cosine, sine_table):
    length, width = vector.shape
    heads_view = vector.reshape(length, width // HEAD, HEAD)
    lead_half = heads_view[..., : HEAD // 2]
    tail_half = heads_view[..., HEAD // 2 :]
    cos_part = cosine[:, None, :]
    sin_part = sine_table[:, None, :]
    turned = jnp.concatenate(
        [lead_half * cos_part - tail_half * sin_part, tail_half * cos_part + lead_half * sin_part],
        -1,
    )
    return turned.reshape(length, width)


def rotate_back(grad_in, cosine, sine_table):
    return rotate(grad_in, cosine, -sine_table)


def mm(left, right):
    return jnp.dot(left, right, preferred_element_type=f32)


def mm_tn(left, right):
    return lax.dot_general(left, right, (((0,), (0,)), ((), ())), preferred_element_type=f32)


def mm_nt(left, right):
    return lax.dot_general(left, right, (((1,), (1,)), ((), ())), preferred_element_type=f32)


def earlier_count(named):
    rows = named.shape[0]
    before = jnp.tril(jnp.ones((rows, rows), bf16), -1)
    return mm(before, named.astype(bf16)).astype(jnp.int32)


def placement_of(routes, capacity, experts):
    picks = (routes[:, :, None] == jnp.arange(experts, dtype=jnp.int32)[None, None, :]).astype(
        jnp.int32
    )
    rank = earlier_count(jnp.sum(picks, 1))
    target = routes * capacity + jnp.sum(picks * rank[:, None, :], 2)
    slots_all = jnp.arange(experts * capacity, dtype=jnp.int32)
    return (target.T[:, :, None] == slots_all[None, None, :]).astype(bf16)


def gate_weights(logits, routes, experts):
    picks = (routes[:, :, None] == jnp.arange(experts, dtype=jnp.int32)[None, None, :]).astype(f32)
    chosen = jnp.sum(picks * logits[:, None, :], -1)
    return (jax.nn.softmax(chosen, -1), picks)


def router_back(gates, picks, gate_grad):
    chosen_grad = gates * (gate_grad - jnp.sum(gates * gate_grad, 1, keepdims=True))
    return jnp.sum(picks * chosen_grad[:, :, None], 1)


def send_rows(place, values, experts):
    packed = mm_tn(place[0] + place[1], values).astype(bf16)
    return packed.reshape(experts, -1, values.shape[1])


def send_grads(place, gates, grad_in, experts):
    scaled = (gates.T[:, :, None] * grad_in[None]).astype(bf16)
    packed = (mm_tn(place[0], scaled[0]) + mm_tn(place[1], scaled[1])).astype(bf16)
    return packed.reshape(experts, -1, grad_in.shape[1])


def as_columns(values):
    high = lax.reduce_precision(values, 8, 7)
    rest = values - high
    middle = lax.reduce_precision(rest, 8, 7)
    columns = jnp.stack([high, middle, rest - middle], 1).astype(bf16)
    return jnp.pad(columns, ((0, 0), (0, PAD - 3)))


def take_back(place, returned):
    flat_back = returned.reshape(place.shape[2], -1)
    return jnp.stack([mm(place[0], flat_back), mm(place[1], flat_back)])


def exchange(packed):
    return lax.all_to_all(packed, "expert", split_axis=0, concat_axis=0, tiled=True)


def exchange_direct(packed, experts, own):
    received = jnp.zeros(packed.shape, packed.dtype)
    for k in range(experts):
        block = lax.dynamic_index_in_dim(packed, (own + k) % experts, 0)
        if k:
            block = lax.ppermute(block, "expert", [(i, (i + k) % experts) for i in range(experts)])
        received = lax.dynamic_update_slice_in_dim(received, block, (own - k) % experts, 0)
    return received


def ring_step(block, experts):
    return lax.ppermute(block, "expert", [(i, (i + 1) % experts) for i in range(experts)])


def ring_gather(block, experts):
    blocks = [block]
    for _ in range(experts - 1):
        blocks.append(ring_step(blocks[-1], experts))
    return blocks


def norm_back(stream, inverse, gain, grad_in):
    scaled = grad_in * gain
    return inverse * scaled - stream * inverse**3 * jnp.mean(scaled * stream, -1, keepdims=True)


def group_scores(queries, keys):
    heads = queries.shape[1] // HEAD
    return (
        jnp.einsum(
            "qhd,khd->hqk",
            queries.reshape(-1, heads, HEAD),
            keys.reshape(-1, heads, HEAD),
            preferred_element_type=f32,
        )
        * score_scale
    )


def attend(queries, keys, values, key_mask):
    heads = queries.shape[1] // HEAD
    scores = jnp.where(key_mask[None], group_scores(queries, keys), masked_score)
    row_peak = jnp.max(scores, -1, keepdims=True)
    exponent = jnp.exp(scores - row_peak)
    row_total = jnp.sum(exponent, -1, keepdims=True)
    attended = jnp.einsum(
        "hqk,khd->qhd",
        (exponent / row_total).astype(bf16),
        values.reshape(-1, heads, HEAD),
        preferred_element_type=f32,
    ).reshape(queries.shape)
    return (attended.astype(bf16), row_peak + jnp.log(row_total))


def attend_back(queries, keys, values, key_mask, log_total, attended, attended_grad):
    heads = queries.shape[1] // HEAD
    scores = jnp.where(key_mask[None], group_scores(queries, keys), masked_score)
    probs = jnp.exp(scores - log_total)
    grad_heads = attended_grad.reshape(-1, heads, HEAD)
    value_heads = values.reshape(-1, heads, HEAD)
    prob_grad = jnp.einsum("qhd,khd->hqk", grad_heads, value_heads, preferred_element_type=f32)
    row_delta = jnp.sum(
        grad_heads.astype(f32) * attended.reshape(-1, heads, HEAD).astype(f32), -1
    ).T[:, :, None]
    score_grad = (probs * (prob_grad - row_delta)).astype(bf16)
    query_grad = jnp.einsum(
        "hqk,khd->qhd", score_grad, keys.reshape(-1, heads, HEAD), preferred_element_type=f32
    ).reshape(queries.shape)
    key_grad = jnp.einsum(
        "hqk,qhd->khd", score_grad, queries.reshape(-1, heads, HEAD), preferred_element_type=f32
    ).reshape(keys.shape)
    value_grad = jnp.einsum(
        "hqk,qhd->khd", probs.astype(bf16), grad_heads, preferred_element_type=f32
    ).reshape(values.shape)
    return (query_grad * score_scale, key_grad * score_scale, value_grad)


def gather_dp(weight):
    return lax.all_gather(weight[0], "dp", axis=0, tiled=True)


def reduce_dp(part):
    return lax.psum_scatter(part, "dp", scatter_dimension=0, tiled=True)


def swap(block, bit):
    return lax.ppermute(block, "dp", [(i, i ^ bit) for i in range(8)])


def bit_of(value, bit):
    return (value // bit) % 2


def halves(block, axis, bit):
    pick = bit_of(lax.axis_index("dp"), bit)
    kept = lax.dynamic_index_in_dim(block, pick, axis, keepdims=False)
    sent = lax.dynamic_index_in_dim(block, 1 - pick, axis, keepdims=False)
    return (kept.astype(f32), sent.astype(bf16))


def fold(block, axis, bit):
    kept, sent = halves(block, axis, bit)
    return kept + swap(sent, bit).astype(f32)


def reduce_swaps(part):
    if lax.axis_size("dp") != 8:
        return reduce_dp(part).astype(f32)
    rows, columns = part.shape
    grid = fold(part.reshape(2, 2, 2, rows // 8, columns), 2, 1).astype(bf16)
    left, right = grid[..., : columns // 2], grid[..., columns // 2 :]
    left = fold(fold(left, 1, 2).astype(bf16), 0, 4)
    right = fold(fold(right, 0, 4).astype(bf16), 0, 2)
    return jnp.concatenate([left, right], 1)


def body(
    tokens,
    cotangent,
    gain_one,
    gain_two,
    kv_weight,
    att_router,
    ffn_router,
    query_weight,
    output_weight,
    gate_weight,
    up_weight,
    down_weight,
    leaf_parent,
    att_route,
    ffn_route,
):
    row_count, model_width = tokens.shape
    experts = att_router.shape[1]
    capacity = row_count * 5 // (2 * experts)
    head_width = HEADS * HEAD
    width = head_width // experts
    shard_rows = kv_weight.shape[0]
    parents = leaf_parent[0]
    own = lax.axis_index("expert")
    backs = [(own - k) % experts for k in range(experts)]

    small = jnp.concatenate(
        [
            att_router,
            ffn_router,
            gain_one[:, None],
            gain_two[:, None],
            jnp.zeros((shard_rows, PAD - 2 * experts - 2), bf16),
        ],
        1,
    )
    bundle = jnp.concatenate(
        [
            kv_weight.reshape(shard_rows, 2, experts, width)
            .transpose(2, 0, 1, 3)
            .reshape(experts, shard_rows, 2 * width),
            jnp.broadcast_to(small[None], (experts, shard_rows, PAD)),
        ],
        2,
    )
    bundle = exchange_direct(bundle, experts, own).reshape(experts * shard_rows, 2 * width + PAD)
    bundle = lax.all_gather(bundle, "dp", axis=0, tiled=True)
    kv_all = bundle[:, : 2 * width]
    att_all = bundle[:, 2 * width : 2 * width + experts]
    ffn_all = bundle[:, 2 * width + experts : 2 * width + 2 * experts]
    gain_first = bundle[:, 2 * width + 2 * experts].astype(f32)
    gain_second = bundle[:, 2 * width + 2 * experts + 1].astype(f32)

    query_all = gather_dp(query_weight)
    output_all = gather_dp(output_weight)
    gate_all = gather_dp(gate_weight)
    up_all = gather_dp(up_weight)
    down_all = gather_dp(down_weight)

    tagged = jnp.concatenate(
        [tokens, att_route.astype(bf16), jnp.zeros((row_count, PAD - 2), bf16)], 1
    )
    tree = jnp.zeros((experts * row_count, model_width + PAD), bf16)
    for k, block in enumerate(ring_gather(tagged, experts)):
        tree = lax.dynamic_update_slice_in_dim(tree, block, backs[k] * row_count, 0)
    tree_tokens = tree[:, :model_width].astype(f32)
    tree_routes = tree[:, model_width : model_width + 2].astype(jnp.int32)
    tree_index = jnp.arange(experts * row_count, dtype=jnp.int32)
    tree_segment, tree_position = layout(tree_index)
    tree_cos, tree_sin = rotary_tables(tree_position)
    tree_inverse = lax.rsqrt(jnp.mean(tree_tokens * tree_tokens, -1, keepdims=True) + norm_eps)
    normed_tree = (tree_tokens * tree_inverse * gain_first).astype(bf16)
    inputs = tokens.astype(f32)
    own_start = own * row_count
    inverse_one = lax.dynamic_slice_in_dim(tree_inverse, own_start, row_count, 0)
    normed_one = lax.dynamic_slice_in_dim(normed_tree, own_start, row_count, 0)

    kv_raw = mm(normed_tree, kv_all)
    kv_own = jnp.concatenate(
        [rotate(kv_raw[:, :width], tree_cos, tree_sin), kv_raw[:, width:]], 1
    ).astype(bf16)

    named = jnp.any(tree_routes == own, 1).reshape(experts, row_count)
    rank = earlier_count(named.T).T
    slots = jnp.arange(capacity, dtype=jnp.int32)
    chosen = named[:, None, :] & (rank[:, None, :] == slots[None, :, None])
    chosen_index = tree_index.reshape(experts, 1, row_count)
    query_index = jnp.sum(jnp.where(chosen, chosen_index, 0), 2).reshape(-1)
    chosen = chosen.astype(bf16)
    query_rows = (
        jnp.einsum(
            "ksr,krd->ksd",
            chosen,
            normed_tree.reshape(experts, row_count, model_width),
            preferred_element_type=f32,
        )
        .astype(bf16)
        .reshape(-1, model_width)
    )
    query_segment, query_position = layout(query_index)
    query_cos, query_sin = rotary_tables(query_position)
    key_mask = visible(query_index, query_segment, tree_index, tree_segment, parents)
    queries = rotate(mm(query_rows, query_all), query_cos, query_sin).astype(bf16)

    attended = jnp.zeros(queries.shape, bf16)
    saved = []
    kv_block = kv_own
    kv_next = ring_step(kv_own, experts)
    for k in range(experts):
        if k:
            kv_block = kv_next
            if k == 1:
                kv_block, queries = lax.optimization_barrier((kv_block, queries))
            else:
                kv_block, attended = lax.optimization_barrier((kv_block, attended))
            if k < experts - 1:
                kv_next = ring_step(kv_block, experts)
        start = backs[k] * width
        group_queries = lax.dynamic_slice_in_dim(queries, start, width, 1)
        keys, values = kv_block[:, :width], kv_block[:, width:]
        group_attended, log_total = attend(group_queries, keys, values, key_mask)
        attended = lax.dynamic_update_slice_in_dim(attended, group_attended, start, 1)
        saved.append((group_queries, keys, values, key_mask, log_total, group_attended))
    att_branch = mm(attended, output_all).astype(bf16)
    att_back = exchange(att_branch.reshape(experts, capacity, -1))

    att_logits = mm(normed_one, att_all)
    att_gate, att_picks = gate_weights(att_logits, att_route, experts)
    att_place = placement_of(att_route, capacity, experts)
    att_picked = take_back(att_place, att_back)
    mixed_stream = inputs + jnp.sum(att_gate.T[:, :, None] * att_picked, 0)
    inverse_two = lax.rsqrt(jnp.mean(mixed_stream * mixed_stream, -1, keepdims=True) + norm_eps)
    normed_two = (mixed_stream * inverse_two * gain_second).astype(bf16)
    ffn_logits = mm(normed_two, ffn_all)
    ffn_gate, ffn_picks = gate_weights(ffn_logits, ffn_route, experts)
    ffn_place = placement_of(ffn_route, capacity, experts)
    ffn_rows = exchange(send_rows(ffn_place, normed_two, experts)).reshape(-1, model_width)
    grad_out = cotangent.astype(f32)
    slot_gate = jnp.sum(ffn_place.astype(f32) * ffn_gate.T[:, :, None], (0, 1))
    packed_grads = jnp.concatenate(
        [
            send_rows(ffn_place, cotangent, experts),
            as_columns(slot_gate).reshape(experts, capacity, PAD),
        ],
        2,
    )
    ffn_rows, packed_grads = lax.optimization_barrier((ffn_rows, packed_grads))
    gate_value = mm(ffn_rows, gate_all)
    up_value = mm(ffn_rows, up_all)
    sigmoid_gate = jax.nn.sigmoid(gate_value)
    hidden = (gate_value * sigmoid_gate * up_value).astype(bf16)
    received_grads, hidden = lax.optimization_barrier((exchange(packed_grads), hidden))
    received_grads = received_grads.reshape(experts * capacity, -1)
    out_rows = received_grads[:, :model_width]
    row_gate = jnp.sum(received_grads[:, model_width:].astype(f32), 1, keepdims=True)
    ffn_grad_rows = (row_gate * out_rows.astype(f32)).astype(bf16)
    down_part = mm_tn(hidden, ffn_grad_rows).astype(bf16)
    down_part, hidden, out_rows = lax.optimization_barrier((down_part, hidden, out_rows))
    down_sum = reduce_dp(down_part)
    hidden_pull = mm_nt(out_rows, down_all)
    row_pull = jnp.sum(hidden.astype(f32) * hidden_pull, 1)
    hidden_grad = row_gate * hidden_pull
    gate_grad = (
        hidden_grad * up_value * sigmoid_gate * (1.0 + gate_value * (1.0 - sigmoid_gate))
    ).astype(bf16)
    up_grad = (hidden_grad * gate_value * sigmoid_gate).astype(bf16)
    ffn_rows_grad = (mm_nt(gate_grad, gate_all) + mm_nt(up_grad, up_all)).astype(bf16)
    ffn_rows_grad = jnp.concatenate([ffn_rows_grad, as_columns(row_pull)], 1)
    ffn_rows_grad, gate_grad, up_grad = lax.optimization_barrier(
        (ffn_rows_grad, gate_grad, up_grad)
    )
    ffn_rows_back = exchange(ffn_rows_grad.reshape(experts, capacity, -1)).reshape(
        experts * capacity, -1
    )
    ffn_rows_grad, hidden = lax.optimization_barrier((ffn_rows_grad, hidden))
    ffn_branch = mm(hidden, down_all).astype(bf16)
    ffn_branch, ffn_rows, gate_grad = lax.optimization_barrier((ffn_branch, ffn_rows, gate_grad))
    ffn_back = exchange_direct(ffn_branch.reshape(experts, capacity, -1), experts, own)
    gate_part = mm_tn(ffn_rows, gate_grad).astype(bf16)
    gate_part, ffn_rows_back = lax.optimization_barrier((gate_part, ffn_rows_back))
    gate_sum = reduce_dp(gate_part)
    gate_pull = jnp.sum(take_back(ffn_place, ffn_rows_back[:, model_width:]), 2).T
    ffn_logit_grad = router_back(ffn_gate, ffn_picks, gate_pull)
    normed_two_grad = mm(ffn_place[0] + ffn_place[1], ffn_rows_back[:, :model_width]) + jnp.dot(
        ffn_logit_grad, ffn_all.astype(f32).T, precision=highest
    )
    gain_two_part = jnp.sum(normed_two_grad * mixed_stream * inverse_two, 0)
    mixed_grad = grad_out + norm_back(mixed_stream, inverse_two, gain_second, normed_two_grad)

    att_logit_grad = router_back(
        att_gate, att_picks, jnp.sum(att_picked * mixed_grad[None], 2).T
    )
    packed_grads, up_grad = lax.optimization_barrier(
        (send_grads(att_place, att_gate, mixed_grad, experts), up_grad)
    )
    up_part = mm_tn(ffn_rows, up_grad).astype(bf16)
    att_grad_rows, up_part, ffn_back = lax.optimization_barrier(
        (exchange(packed_grads), up_part, ffn_back)
    )
    up_sum = reduce_dp(up_part)
    att_grad_rows = att_grad_rows.reshape(-1, model_width)
    ffn_picked = take_back(ffn_place, ffn_back)
    result = mixed_stream + jnp.sum(ffn_gate.T[:, :, None] * ffn_picked, 0)
    att_grad_rows, down_sum = lax.optimization_barrier((att_grad_rows, down_sum))
    attended_grad = mm_nt(att_grad_rows, output_all).astype(bf16)
    query_grad = jnp.zeros(queries.shape, f32)
    kv_grad = None
    for step in range(1, experts + 1):
        k = step % experts
        start = backs[k] * width
        group_grad = lax.dynamic_slice_in_dim(
            late_grad if k == 0 else attended_grad, start, width, 1
        )
        group_query_grad, key_grad, value_grad = attend_back(*saved[k], group_grad)
        query_grad = lax.dynamic_update_slice_in_dim(query_grad, group_query_grad, start, 1)
        part = jnp.concatenate([key_grad, value_grad], 1)
        if k == 0:
            output_sum = reduce_swaps(mm_tn(attended, att_grad_rows).astype(bf16))
            kv_grad, query_rows = lax.optimization_barrier((kv_grad, query_rows))
        if kv_grad is not None:
            part = part + kv_grad.astype(f32)
        if k == 0:
            kv_grad = part
            continue
        part = part.astype(bf16)
        if step == experts - 1:
            part, late_grad, att_grad_rows = lax.optimization_barrier(
                (part, attended_grad, att_grad_rows)
            )
        kv_grad = ring_step(part, experts)
    query_raw_grad = rotate_back(query_grad, query_cos, query_sin).astype(bf16)
    query_sum = reduce_swaps(mm_tn(query_rows, query_raw_grad).astype(bf16))
    att_rows_grad = mm_nt(query_raw_grad, query_all).astype(bf16)
    kv_raw_grad = jnp.concatenate(
        [rotate_back(kv_grad[:, :width], tree_cos, tree_sin), kv_grad[:, width:]], 1
    ).astype(bf16)
    tree_grad = mm_nt(kv_raw_grad, kv_all).reshape(experts, row_count, -1) + jnp.einsum(
        "ksr,ksd->krd",
        chosen,
        att_rows_grad.reshape(experts, capacity, -1),
        preferred_element_type=f32,
    )
    router_grad = jnp.dot(att_logit_grad, att_all.astype(f32).T, precision=highest)
    gain_one_part = jnp.sum(router_grad * inputs * inverse_one, 0) + jnp.sum(
        tree_grad.reshape(tree_tokens.shape) * tree_tokens * tree_inverse, 0
    )
    att_router_part = lax.dot_general(
        att_logit_grad, normed_one.astype(f32), (((0,), (0,)), ((), ())), precision=highest
    )
    ffn_router_part = lax.dot_general(
        ffn_logit_grad, normed_two.astype(f32), (((0,), (0,)), ((), ())), precision=highest
    )
    small_part = jnp.concatenate(
        [
            att_router_part,
            ffn_router_part,
            gain_one_part[None],
            gain_two_part[None],
            jnp.zeros((PAD - 2 * experts - 2, model_width), f32),
        ],
        0,
    ).astype(bf16)
    shared_part = jnp.concatenate(
        [
            mm_tn(normed_tree, kv_raw_grad).astype(bf16),
            mm_tn(small_part, jnp.eye(PAD, dtype=bf16)).astype(bf16),
        ],
        1,
    )
    normed_one_grad = None
    for step in range(1, experts + 1):
        k = step % experts
        part = lax.dynamic_index_in_dim(tree_grad, backs[k], 0, keepdims=False)
        if normed_one_grad is not None:
            part = part + normed_one_grad.astype(f32)
        normed_one_grad = part if k == 0 else ring_step(part.astype(bf16), experts)
        if step == experts - 1:
            normed_one_grad, shared_part = lax.optimization_barrier(
                (normed_one_grad, reduce_dp(shared_part))
            )
        if k == 0:
            normed_one_grad, query_sum, output_sum = lax.optimization_barrier(
                (normed_one_grad, query_sum, output_sum)
            )
    normed_one_grad = normed_one_grad + router_grad
    input_grad = mixed_grad + norm_back(inputs, inverse_one, gain_first, normed_one_grad)
    shared_sum = exchange(shared_part.reshape(experts, shard_rows, -1)).astype(f32)
    kv_sum = (
        shared_sum[:, :, : 2 * width]
        .reshape(experts, shard_rows, 2, width)
        .transpose(1, 2, 0, 3)
        .reshape(shard_rows, 2 * head_width)
    )
    small_sum = jnp.sum(shared_sum[:, :, 2 * width :], 0)
    return (
        result.astype(bf16),
        input_grad,
        small_sum[:, 2 * experts],
        small_sum[:, 2 * experts + 1],
        kv_sum,
        small_sum[:, :experts],
        small_sum[:, experts : 2 * experts],
        query_sum.astype(f32)[None],
        output_sum.astype(f32)[None],
        gate_sum.astype(f32)[None],
        up_sum.astype(f32)[None],
        down_sum.astype(f32)[None],
    )

def solution(mesh):
    in_specs = (
        P(("dp", "expert"), None),
        P(("dp", "expert"), None),
        P(("dp", "expert")),
        P(("dp", "expert")),
        P(("dp", "expert"), None),
        P(("dp", "expert"), None),
        P(("dp", "expert"), None),
        P("expert", "dp", None),
        P("expert", "dp", None),
        P("expert", "dp", None),
        P("expert", "dp", None),
        P("expert", "dp", None),
        P("dp", None),
        P(("dp", "expert"), None),
        P(("dp", "expert"), None),
    )
    out_specs = (
        P(("dp", "expert"), None),
        P(("dp", "expert"), None),
        P(("dp", "expert")),
        P(("dp", "expert")),
        P(("dp", "expert"), None),
        P(("dp", "expert"), None),
        P(("dp", "expert"), None),
        P("expert", "dp", None),
        P("expert", "dp", None),
        P("expert", "dp", None),
        P("expert", "dp", None),
        P("expert", "dp", None),
    )
    return jax.shard_map(body, mesh=mesh, in_specs=in_specs, out_specs=out_specs, check_vma=False)
```

```python
import jax
import jax.numpy as jnp
from jax import lax
from jax.sharding import PartitionSpec as P

HEADS = 16
HEAD = 128
TRUNK = 512
BRANCH = 64
LEAF = 32
PAD = 128


norm_eps = 1e-05
highest = lax.Precision.HIGHEST
masked_score = -1e30
score_scale = HEAD ** (-0.5)
bf16 = jnp.bfloat16
f32 = jnp.float32


def layout(row_index):
    past_trunk = row_index - TRUNK
    in_branch = (row_index >= TRUNK) & (past_trunk < 4 * BRANCH)
    leaf_offset = past_trunk - 4 * BRANCH
    segment = jnp.where(
        row_index < TRUNK,
        0,
        jnp.where(in_branch, 1 + past_trunk // BRANCH, 5 + leaf_offset // LEAF),
    )
    position = jnp.where(
        row_index < TRUNK,
        row_index,
        jnp.where(in_branch, TRUNK + past_trunk % BRANCH, TRUNK + BRANCH + leaf_offset % LEAF),
    )
    return (segment, position)


def visible(query_index, query_segment, key_index, key_segment, parents):
    leaf_slot = query_segment - 5
    branch_of = jnp.sum(
        jnp.where(
            leaf_slot[:, None] == jnp.arange(8, dtype=jnp.int32)[None, :], parents[None, :], 0
        ),
        1,
    )
    ancestor = jnp.where(query_segment >= 5, branch_of, -1)
    same_segment = (key_segment[None, :] == query_segment[:, None]) & (
        key_index[None, :] <= query_index[:, None]
    )
    from_trunk = (key_segment[None, :] == 0) & (query_segment[:, None] > 0)
    from_branch = key_segment[None, :] == ancestor[:, None]
    return same_segment | from_trunk | from_branch


def rotary_tables(position):
    half_width = HEAD // 2
    frequency = 10000.0 ** (-2.0 * jnp.arange(half_width, dtype=f32) / HEAD)
    angle = position.astype(f32)[:, None] * frequency[None, :]
    return (jnp.cos(angle), jnp.sin(angle))


def rotate(vector, cosine, sine_table):
    length, width = vector.shape
    heads_view = vector.reshape(length, width // HEAD, HEAD)
    lead_half = heads_view[..., : HEAD // 2]
    tail_half = heads_view[..., HEAD // 2 :]
    cos_part = cosine[:, None, :]
    sin_part = sine_table[:, None, :]
    turned = jnp.concatenate(
        [lead_half * cos_part - tail_half * sin_part, tail_half * cos_part + lead_half * sin_part],
        -1,
    )
    return turned.reshape(length, width)


def rotate_back(grad_in, cosine, sine_table):
    return rotate(grad_in, cosine, -sine_table)


def mm(left, right):
    return jnp.dot(left, right, preferred_element_type=f32)


def mm_tn(left, right):
    return lax.dot_general(left, right, (((0,), (0,)), ((), ())), preferred_element_type=f32)


def mm_nt(left, right):
    return lax.dot_general(left, right, (((1,), (1,)), ((), ())), preferred_element_type=f32)


def earlier_count(named):
    rows = named.shape[0]
    before = jnp.tril(jnp.ones((rows, rows), bf16), -1)
    return mm(before, named.astype(bf16)).astype(jnp.int32)


def placement_of(routes, capacity, experts):
    picks = (routes[:, :, None] == jnp.arange(experts, dtype=jnp.int32)[None, None, :]).astype(
        jnp.int32
    )
    rank = earlier_count(jnp.sum(picks, 1))
    target = routes * capacity + jnp.sum(picks * rank[:, None, :], 2)
    slots_all = jnp.arange(experts * capacity, dtype=jnp.int32)
    return (target.T[:, :, None] == slots_all[None, None, :]).astype(bf16)


def gate_weights(logits, routes, experts):
    picks = (routes[:, :, None] == jnp.arange(experts, dtype=jnp.int32)[None, None, :]).astype(f32)
    chosen = jnp.sum(picks * logits[:, None, :], -1)
    return (jax.nn.softmax(chosen, -1), picks)


def router_back(gates, picks, gate_grad):
    chosen_grad = gates * (gate_grad - jnp.sum(gates * gate_grad, 1, keepdims=True))
    return jnp.sum(picks * chosen_grad[:, :, None], 1)


def send_rows(place, values, experts):
    packed = mm_tn(place[0] + place[1], values).astype(bf16)
    return packed.reshape(experts, -1, values.shape[1])


def send_grads(place, gates, grad_in, experts):
    scaled = (gates.T[:, :, None] * grad_in[None]).astype(bf16)
    packed = (mm_tn(place[0], scaled[0]) + mm_tn(place[1], scaled[1])).astype(bf16)
    return packed.reshape(experts, -1, grad_in.shape[1])


def as_columns(values):
    high = lax.reduce_precision(values, 8, 7)
    rest = values - high
    middle = lax.reduce_precision(rest, 8, 7)
    columns = jnp.stack([high, middle, rest - middle], 1).astype(bf16)
    return jnp.pad(columns, ((0, 0), (0, PAD - 3)))


def take_back(place, returned):
    flat_back = returned.reshape(place.shape[2], -1)
    return jnp.stack([mm(place[0], flat_back), mm(place[1], flat_back)])


def exchange(packed):
    return lax.all_to_all(packed, "expert", split_axis=0, concat_axis=0, tiled=True)


def exchange_direct(packed, experts, own):
    received = jnp.zeros(packed.shape, packed.dtype)
    for k in range(experts):
        block = lax.dynamic_index_in_dim(packed, (own + k) % experts, 0)
        if k:
            block = lax.ppermute(block, "expert", [(i, (i + k) % experts) for i in range(experts)])
        received = lax.dynamic_update_slice_in_dim(received, block, (own - k) % experts, 0)
    return received


def ring_step(block, experts):
    return lax.ppermute(block, "expert", [(i, (i + 1) % experts) for i in range(experts)])


def ring_gather(block, experts):
    blocks = [block]
    for _ in range(experts - 1):
        blocks.append(ring_step(blocks[-1], experts))
    return blocks


def norm_back(stream, inverse, gain, grad_in):
    scaled = grad_in * gain
    return inverse * scaled - stream * inverse**3 * jnp.mean(scaled * stream, -1, keepdims=True)


def group_scores(queries, keys):
    heads = queries.shape[1] // HEAD
    return (
        jnp.einsum(
            "qhd,khd->hqk",
            queries.reshape(-1, heads, HEAD),
            keys.reshape(-1, heads, HEAD),
            preferred_element_type=f32,
        )
        * score_scale
    )


def attend(queries, keys, values, key_mask):
    heads = queries.shape[1] // HEAD
    scores = jnp.where(key_mask[None], group_scores(queries, keys), masked_score)
    row_peak = jnp.max(scores, -1, keepdims=True)
    exponent = jnp.exp(scores - row_peak)
    row_total = jnp.sum(exponent, -1, keepdims=True)
    attended = jnp.einsum(
        "hqk,khd->qhd",
        (exponent / row_total).astype(bf16),
        values.reshape(-1, heads, HEAD),
        preferred_element_type=f32,
    ).reshape(queries.shape)
    return (attended.astype(bf16), row_peak + jnp.log(row_total))


def attend_back(queries, keys, values, key_mask, log_total, attended, attended_grad):
    heads = queries.shape[1] // HEAD
    scores = jnp.where(key_mask[None], group_scores(queries, keys), masked_score)
    probs = jnp.exp(scores - log_total)
    grad_heads = attended_grad.reshape(-1, heads, HEAD)
    value_heads = values.reshape(-1, heads, HEAD)
    prob_grad = jnp.einsum("qhd,khd->hqk", grad_heads, value_heads, preferred_element_type=f32)
    row_delta = jnp.sum(
        grad_heads.astype(f32) * attended.reshape(-1, heads, HEAD).astype(f32), -1
    ).T[:, :, None]
    score_grad = (probs * (prob_grad - row_delta)).astype(bf16)
    query_grad = jnp.einsum(
        "hqk,khd->qhd", score_grad, keys.reshape(-1, heads, HEAD), preferred_element_type=f32
    ).reshape(queries.shape)
    key_grad = jnp.einsum(
        "hqk,qhd->khd", score_grad, queries.reshape(-1, heads, HEAD), preferred_element_type=f32
    ).reshape(keys.shape)
    value_grad = jnp.einsum(
        "hqk,qhd->khd", probs.astype(bf16), grad_heads, preferred_element_type=f32
    ).reshape(values.shape)
    return (query_grad * score_scale, key_grad * score_scale, value_grad)


def gather_dp(weight):
    return lax.all_gather(weight[0], "dp", axis=0, tiled=True)


def reduce_dp(part):
    return lax.psum_scatter(part, "dp", scatter_dimension=0, tiled=True)


def swap(block, bit):
    return lax.ppermute(block, "dp", [(i, i ^ bit) for i in range(8)])


def bit_of(value, bit):
    return (value // bit) % 2


def halves(block, axis, bit):
    pick = bit_of(lax.axis_index("dp"), bit)
    kept = lax.dynamic_index_in_dim(block, pick, axis, keepdims=False)
    sent = lax.dynamic_index_in_dim(block, 1 - pick, axis, keepdims=False)
    return (kept.astype(f32), sent.astype(bf16))


def fold(block, axis, bit):
    kept, sent = halves(block, axis, bit)
    return kept + swap(sent, bit).astype(f32)


def reduce_swaps(part):
    if lax.axis_size("dp") != 8:
        return reduce_dp(part).astype(f32)
    rows, columns = part.shape
    grid = fold(part.reshape(2, 2, 2, rows // 8, columns), 2, 1).astype(bf16)
    left, right = grid[..., : columns // 2], grid[..., columns // 2 :]
    left = fold(fold(left, 1, 2).astype(bf16), 0, 4)
    right = fold(fold(right, 0, 4).astype(bf16), 0, 2)
    return jnp.concatenate([left, right], 1)


def body(
    tokens,
    cotangent,
    gain_one,
    gain_two,
    kv_weight,
    att_router,
    ffn_router,
    query_weight,
    output_weight,
    gate_weight,
    up_weight,
    down_weight,
    leaf_parent,
    att_route,
    ffn_route,
):
    row_count, model_width = tokens.shape
    experts = att_router.shape[1]
    capacity = row_count * 5 // (2 * experts)
    head_width = HEADS * HEAD
    width = head_width // experts
    shard_rows = kv_weight.shape[0]
    parents = leaf_parent[0]
    own = lax.axis_index("expert")
    backs = [(own - k) % experts for k in range(experts)]

    small = jnp.concatenate(
        [
            att_router,
            ffn_router,
            gain_one[:, None],
            gain_two[:, None],
            jnp.zeros((shard_rows, PAD - 2 * experts - 2), bf16),
        ],
        1,
    )
    bundle = jnp.concatenate(
        [
            kv_weight.reshape(shard_rows, 2, experts, width)
            .transpose(2, 0, 1, 3)
            .reshape(experts, shard_rows, 2 * width),
            jnp.broadcast_to(small[None], (experts, shard_rows, PAD)),
        ],
        2,
    )
    bundle = exchange_direct(bundle, experts, own).reshape(experts * shard_rows, 2 * width + PAD)
    bundle = lax.all_gather(bundle, "dp", axis=0, tiled=True)
    kv_all = bundle[:, : 2 * width]
    att_all = bundle[:, 2 * width : 2 * width + experts]
    ffn_all = bundle[:, 2 * width + experts : 2 * width + 2 * experts]
    gain_first = bundle[:, 2 * width + 2 * experts].astype(f32)
    gain_second = bundle[:, 2 * width + 2 * experts + 1].astype(f32)

    query_all = gather_dp(query_weight)
    output_all = gather_dp(output_weight)
    gate_all = gather_dp(gate_weight)
    up_all = gather_dp(up_weight)
    down_all = gather_dp(down_weight)

    tagged = jnp.concatenate(
        [tokens, att_route.astype(bf16), jnp.zeros((row_count, PAD - 2), bf16)], 1
    )
    tree = jnp.zeros((experts * row_count, model_width + PAD), bf16)
    for k, block in enumerate(ring_gather(tagged, experts)):
        tree = lax.dynamic_update_slice_in_dim(tree, block, backs[k] * row_count, 0)
    tree_tokens = tree[:, :model_width].astype(f32)
    tree_routes = tree[:, model_width : model_width + 2].astype(jnp.int32)
    tree_index = jnp.arange(experts * row_count, dtype=jnp.int32)
    tree_segment, tree_position = layout(tree_index)
    tree_cos, tree_sin = rotary_tables(tree_position)
    tree_inverse = lax.rsqrt(jnp.mean(tree_tokens * tree_tokens, -1, keepdims=True) + norm_eps)
    normed_tree = (tree_tokens * tree_inverse * gain_first).astype(bf16)
    inputs = tokens.astype(f32)
    own_start = own * row_count
    inverse_one = lax.dynamic_slice_in_dim(tree_inverse, own_start, row_count, 0)
    normed_one = lax.dynamic_slice_in_dim(normed_tree, own_start, row_count, 0)

    kv_raw = mm(normed_tree, kv_all)
    kv_own = jnp.concatenate(
        [rotate(kv_raw[:, :width], tree_cos, tree_sin), kv_raw[:, width:]], 1
    ).astype(bf16)

    named = jnp.any(tree_routes == own, 1).reshape(experts, row_count)
    rank = earlier_count(named.T).T
    slots = jnp.arange(capacity, dtype=jnp.int32)
    chosen = named[:, None, :] & (rank[:, None, :] == slots[None, :, None])
    chosen_index = tree_index.reshape(experts, 1, row_count)
    query_index = jnp.sum(jnp.where(chosen, chosen_index, 0), 2).reshape(-1)
    chosen = chosen.astype(bf16)
    query_rows = (
        jnp.einsum(
            "ksr,krd->ksd",
            chosen,
            normed_tree.reshape(experts, row_count, model_width),
            preferred_element_type=f32,
        )
        .astype(bf16)
        .reshape(-1, model_width)
    )
    query_segment, query_position = layout(query_index)
    query_cos, query_sin = rotary_tables(query_position)
    key_mask = visible(query_index, query_segment, tree_index, tree_segment, parents)
    queries = rotate(mm(query_rows, query_all), query_cos, query_sin).astype(bf16)

    attended = jnp.zeros(queries.shape, bf16)
    saved = []
    kv_block = kv_own
    kv_next = ring_step(kv_own, experts)
    for k in range(experts):
        if k:
            kv_block = kv_next
            if k == 1:
                kv_block, queries = lax.optimization_barrier((kv_block, queries))
            else:
                kv_block, attended = lax.optimization_barrier((kv_block, attended))
            if k < experts - 1:
                kv_next = ring_step(kv_block, experts)
        start = backs[k] * width
        group_queries = lax.dynamic_slice_in_dim(queries, start, width, 1)
        keys, values = kv_block[:, :width], kv_block[:, width:]
        group_attended, log_total = attend(group_queries, keys, values, key_mask)
        attended = lax.dynamic_update_slice_in_dim(attended, group_attended, start, 1)
        saved.append((group_queries, keys, values, key_mask, log_total, group_attended))
    att_branch = mm(attended, output_all).astype(bf16)
    att_back = exchange(att_branch.reshape(experts, capacity, -1))

    att_logits = mm(normed_one, att_all)
    att_gate, att_picks = gate_weights(att_logits, att_route, experts)
    att_place = placement_of(att_route, capacity, experts)
    att_picked = take_back(att_place, att_back)
    mixed_stream = inputs + jnp.sum(att_gate.T[:, :, None] * att_picked, 0)
    inverse_two = lax.rsqrt(jnp.mean(mixed_stream * mixed_stream, -1, keepdims=True) + norm_eps)
    normed_two = (mixed_stream * inverse_two * gain_second).astype(bf16)
    ffn_logits = mm(normed_two, ffn_all)
    ffn_gate, ffn_picks = gate_weights(ffn_logits, ffn_route, experts)
    ffn_place = placement_of(ffn_route, capacity, experts)
    ffn_rows = exchange(send_rows(ffn_place, normed_two, experts)).reshape(-1, model_width)
    grad_out = cotangent.astype(f32)
    slot_gate = jnp.sum(ffn_place.astype(f32) * ffn_gate.T[:, :, None], (0, 1))
    packed_grads = jnp.concatenate(
        [
            send_rows(ffn_place, cotangent, experts),
            as_columns(slot_gate).reshape(experts, capacity, PAD),
        ],
        2,
    )
    ffn_rows, packed_grads = lax.optimization_barrier((ffn_rows, packed_grads))
    gate_value = mm(ffn_rows, gate_all)
    up_value = mm(ffn_rows, up_all)
    sigmoid_gate = jax.nn.sigmoid(gate_value)
    hidden = (gate_value * sigmoid_gate * up_value).astype(bf16)
    received_grads, hidden = lax.optimization_barrier((exchange(packed_grads), hidden))
    received_grads = received_grads.reshape(experts * capacity, -1)
    out_rows = received_grads[:, :model_width]
    row_gate = jnp.sum(received_grads[:, model_width:].astype(f32), 1, keepdims=True)
    ffn_grad_rows = (row_gate * out_rows.astype(f32)).astype(bf16)
    down_part = mm_tn(hidden, ffn_grad_rows).astype(bf16)
    down_part, hidden, out_rows = lax.optimization_barrier((down_part, hidden, out_rows))
    down_sum = reduce_dp(down_part)
    hidden_pull = mm_nt(out_rows, down_all)
    row_pull = jnp.sum(hidden.astype(f32) * hidden_pull, 1)
    hidden_grad = row_gate * hidden_pull
    gate_grad = (
        hidden_grad * up_value * sigmoid_gate * (1.0 + gate_value * (1.0 - sigmoid_gate))
    ).astype(bf16)
    up_grad = (hidden_grad * gate_value * sigmoid_gate).astype(bf16)
    half = model_width // 2
    left_grad = (mm_nt(gate_grad, gate_all[:half]) + mm_nt(up_grad, up_all[:half])).astype(bf16)
    left_grad = jnp.concatenate([left_grad, as_columns(row_pull)], 1)
    left_grad, gate_grad, up_grad = lax.optimization_barrier((left_grad, gate_grad, up_grad))
    left_back = exchange(left_grad.reshape(experts, capacity, -1))
    right_grad = (mm_nt(gate_grad, gate_all[half:]) + mm_nt(up_grad, up_all[half:])).astype(bf16)
    left_back, right_grad, gate_grad, up_grad = lax.optimization_barrier(
        (left_back, right_grad, gate_grad, up_grad)
    )
    right_back = exchange(right_grad.reshape(experts, capacity, -1))
    gate_part = mm_tn(ffn_rows, gate_grad).astype(bf16)
    gate_part, right_back = lax.optimization_barrier((gate_part, right_back))
    left_back = left_back.reshape(experts * capacity, -1)
    right_back = right_back.reshape(experts * capacity, -1)
    gate_sum = reduce_dp(gate_part)
    gate_pull = jnp.sum(take_back(ffn_place, left_back[:, half:]), 2).T
    ffn_logit_grad = router_back(ffn_gate, ffn_picks, gate_pull)
    ffn_slots = ffn_place[0] + ffn_place[1]
    normed_two_grad = jnp.concatenate(
        [mm(ffn_slots, left_back[:, :half]), mm(ffn_slots, right_back)], 1
    ) + jnp.dot(
        ffn_logit_grad, ffn_all.astype(f32).T, precision=highest
    )
    gain_two_part = jnp.sum(normed_two_grad * mixed_stream * inverse_two, 0)
    mixed_grad = grad_out + norm_back(mixed_stream, inverse_two, gain_second, normed_two_grad)

    att_logit_grad = router_back(
        att_gate, att_picks, jnp.sum(att_picked * mixed_grad[None], 2).T
    )
    packed_grads, hidden, up_grad = lax.optimization_barrier(
        (send_grads(att_place, att_gate, mixed_grad, experts), hidden, up_grad)
    )
    ffn_branch = mm(hidden, down_all).astype(bf16)
    up_part = mm_tn(ffn_rows, up_grad).astype(bf16)
    att_grad_rows, ffn_branch, up_part = lax.optimization_barrier(
        (exchange(packed_grads), ffn_branch, up_part)
    )
    up_sum = reduce_dp(up_part)
    att_grad_rows = att_grad_rows.reshape(-1, model_width)
    ffn_back = exchange(ffn_branch.reshape(experts, capacity, -1))
    att_grad_rows, down_sum = lax.optimization_barrier((att_grad_rows, down_sum))
    attended_grad = mm_nt(att_grad_rows, output_all).astype(bf16)
    query_grad = jnp.zeros(queries.shape, f32)
    kv_grad = None
    for step in range(1, experts + 1):
        k = step % experts
        start = backs[k] * width
        group_grad = lax.dynamic_slice_in_dim(
            attended_grad if step < 4 else late_grad, start, width, 1
        )
        group_query_grad, key_grad, value_grad = attend_back(*saved[k], group_grad)
        query_grad = lax.dynamic_update_slice_in_dim(query_grad, group_query_grad, start, 1)
        part = jnp.concatenate([key_grad, value_grad], 1)
        if k == 0:
            kv_grad, output_sum = lax.optimization_barrier((kv_grad, output_sum))
        if kv_grad is not None:
            part = part + kv_grad.astype(f32)
        if k == 0:
            kv_grad = part
            continue
        part = part.astype(bf16)
        if step == 2:
            part, att_grad_rows, ffn_back, late_grad = lax.optimization_barrier(
                (part, att_grad_rows, ffn_back, attended_grad)
            )
            output_sum = reduce_swaps(mm_tn(attended, att_grad_rows).astype(bf16))
        if step == experts - 1:
            part, query_rows = lax.optimization_barrier((part, query_rows))
        kv_grad = ring_step(part, experts)
    ffn_picked = take_back(ffn_place, ffn_back)
    result = mixed_stream + jnp.sum(ffn_gate.T[:, :, None] * ffn_picked, 0)
    query_raw_grad = rotate_back(query_grad, query_cos, query_sin).astype(bf16)
    query_sum = reduce_swaps(mm_tn(query_rows, query_raw_grad).astype(bf16))
    att_rows_grad = mm_nt(query_raw_grad, query_all).astype(bf16)
    kv_raw_grad = jnp.concatenate(
        [rotate_back(kv_grad[:, :width], tree_cos, tree_sin), kv_grad[:, width:]], 1
    ).astype(bf16)
    tree_grad = mm_nt(kv_raw_grad, kv_all).reshape(experts, row_count, -1) + jnp.einsum(
        "ksr,ksd->krd",
        chosen,
        att_rows_grad.reshape(experts, capacity, -1),
        preferred_element_type=f32,
    )
    router_grad = jnp.dot(att_logit_grad, att_all.astype(f32).T, precision=highest)
    gain_one_part = jnp.sum(router_grad * inputs * inverse_one, 0) + jnp.sum(
        tree_grad.reshape(tree_tokens.shape) * tree_tokens * tree_inverse, 0
    )
    att_router_part = lax.dot_general(
        att_logit_grad, normed_one.astype(f32), (((0,), (0,)), ((), ())), precision=highest
    )
    ffn_router_part = lax.dot_general(
        ffn_logit_grad, normed_two.astype(f32), (((0,), (0,)), ((), ())), precision=highest
    )
    small_part = jnp.concatenate(
        [
            att_router_part,
            ffn_router_part,
            gain_one_part[None],
            gain_two_part[None],
            jnp.zeros((PAD - 2 * experts - 2, model_width), f32),
        ],
        0,
    ).astype(bf16)
    shared_part = jnp.concatenate(
        [
            mm_tn(normed_tree, kv_raw_grad).astype(bf16),
            mm_tn(small_part, jnp.eye(PAD, dtype=bf16)).astype(bf16),
        ],
        1,
    )
    normed_one_grad = None
    for step in range(1, experts + 1):
        k = step % experts
        part = lax.dynamic_index_in_dim(tree_grad, backs[k], 0, keepdims=False)
        if normed_one_grad is not None:
            part = part + normed_one_grad.astype(f32)
        normed_one_grad = part if k == 0 else ring_step(part.astype(bf16), experts)
        if step == experts - 1:
            normed_one_grad, shared_part = lax.optimization_barrier(
                (normed_one_grad, reduce_dp(shared_part))
            )
        if step == 2:
            normed_one_grad, query_sum = lax.optimization_barrier((normed_one_grad, query_sum))
    normed_one_grad = normed_one_grad + router_grad
    input_grad = mixed_grad + norm_back(inputs, inverse_one, gain_first, normed_one_grad)
    shared_sum = exchange(shared_part.reshape(experts, shard_rows, -1)).astype(f32)
    kv_sum = (
        shared_sum[:, :, : 2 * width]
        .reshape(experts, shard_rows, 2, width)
        .transpose(1, 2, 0, 3)
        .reshape(shard_rows, 2 * head_width)
    )
    small_sum = jnp.sum(shared_sum[:, :, 2 * width :], 0)
    return (
        result.astype(bf16),
        input_grad,
        small_sum[:, 2 * experts],
        small_sum[:, 2 * experts + 1],
        kv_sum,
        small_sum[:, :experts],
        small_sum[:, experts : 2 * experts],
        query_sum.astype(f32)[None],
        output_sum.astype(f32)[None],
        gate_sum.astype(f32)[None],
        up_sum.astype(f32)[None],
        down_sum.astype(f32)[None],
    )

def solution(mesh):
    in_specs = (
        P(("dp", "expert"), None),
        P(("dp", "expert"), None),
        P(("dp", "expert")),
        P(("dp", "expert")),
        P(("dp", "expert"), None),
        P(("dp", "expert"), None),
        P(("dp", "expert"), None),
        P("expert", "dp", None),
        P("expert", "dp", None),
        P("expert", "dp", None),
        P("expert", "dp", None),
        P("expert", "dp", None),
        P("dp", None),
        P(("dp", "expert"), None),
        P(("dp", "expert"), None),
    )
    out_specs = (
        P(("dp", "expert"), None),
        P(("dp", "expert"), None),
        P(("dp", "expert")),
        P(("dp", "expert")),
        P(("dp", "expert"), None),
        P(("dp", "expert"), None),
        P(("dp", "expert"), None),
        P("expert", "dp", None),
        P("expert", "dp", None),
        P("expert", "dp", None),
        P("expert", "dp", None),
        P("expert", "dp", None),
    )
    return jax.shard_map(body, mesh=mesh, in_specs=in_specs, out_specs=out_specs, check_vma=False)
```

```python
import jax
import jax.numpy as jnp
from jax import lax
from jax.sharding import PartitionSpec as P

HEADS = 16
HEAD = 128
TRUNK = 512
BRANCH = 64
LEAF = 32
PAD = 128


norm_eps = 1e-05
highest = lax.Precision.HIGHEST
masked_score = -1e30
score_scale = HEAD ** (-0.5)
bf16 = jnp.bfloat16
f32 = jnp.float32


def layout(row_index):
    past_trunk = row_index - TRUNK
    in_branch = (row_index >= TRUNK) & (past_trunk < 4 * BRANCH)
    leaf_offset = past_trunk - 4 * BRANCH
    segment = jnp.where(
        row_index < TRUNK,
        0,
        jnp.where(in_branch, 1 + past_trunk // BRANCH, 5 + leaf_offset // LEAF),
    )
    position = jnp.where(
        row_index < TRUNK,
        row_index,
        jnp.where(in_branch, TRUNK + past_trunk % BRANCH, TRUNK + BRANCH + leaf_offset % LEAF),
    )
    return (segment, position)


def visible(query_index, query_segment, key_index, key_segment, parents):
    leaf_slot = query_segment - 5
    branch_of = jnp.sum(
        jnp.where(
            leaf_slot[:, None] == jnp.arange(8, dtype=jnp.int32)[None, :], parents[None, :], 0
        ),
        1,
    )
    ancestor = jnp.where(query_segment >= 5, branch_of, -1)
    same_segment = (key_segment[None, :] == query_segment[:, None]) & (
        key_index[None, :] <= query_index[:, None]
    )
    from_trunk = (key_segment[None, :] == 0) & (query_segment[:, None] > 0)
    from_branch = key_segment[None, :] == ancestor[:, None]
    return same_segment | from_trunk | from_branch


def rotary_tables(position):
    half_width = HEAD // 2
    frequency = 10000.0 ** (-2.0 * jnp.arange(half_width, dtype=f32) / HEAD)
    angle = position.astype(f32)[:, None] * frequency[None, :]
    return (jnp.cos(angle), jnp.sin(angle))


def rotate(vector, cosine, sine_table):
    length, width = vector.shape
    heads_view = vector.reshape(length, width // HEAD, HEAD)
    lead_half = heads_view[..., : HEAD // 2]
    tail_half = heads_view[..., HEAD // 2 :]
    cos_part = cosine[:, None, :]
    sin_part = sine_table[:, None, :]
    turned = jnp.concatenate(
        [lead_half * cos_part - tail_half * sin_part, tail_half * cos_part + lead_half * sin_part],
        -1,
    )
    return turned.reshape(length, width)


def rotate_back(grad_in, cosine, sine_table):
    return rotate(grad_in, cosine, -sine_table)


def mm(left, right):
    return jnp.dot(left, right, preferred_element_type=f32)


def mm_tn(left, right):
    return lax.dot_general(left, right, (((0,), (0,)), ((), ())), preferred_element_type=f32)


def mm_nt(left, right):
    return lax.dot_general(left, right, (((1,), (1,)), ((), ())), preferred_element_type=f32)


def earlier_count(named):
    rows = named.shape[0]
    before = jnp.tril(jnp.ones((rows, rows), bf16), -1)
    return mm(before, named.astype(bf16)).astype(jnp.int32)


def placement_of(routes, capacity, experts):
    picks = (routes[:, :, None] == jnp.arange(experts, dtype=jnp.int32)[None, None, :]).astype(
        jnp.int32
    )
    rank = earlier_count(jnp.sum(picks, 1))
    target = routes * capacity + jnp.sum(picks * rank[:, None, :], 2)
    slots_all = jnp.arange(experts * capacity, dtype=jnp.int32)
    return (target.T[:, :, None] == slots_all[None, None, :]).astype(bf16)


def gate_weights(logits, routes, experts):
    picks = (routes[:, :, None] == jnp.arange(experts, dtype=jnp.int32)[None, None, :]).astype(f32)
    chosen = jnp.sum(picks * logits[:, None, :], -1)
    return (jax.nn.softmax(chosen, -1), picks)


def router_back(gates, picks, gate_grad):
    chosen_grad = gates * (gate_grad - jnp.sum(gates * gate_grad, 1, keepdims=True))
    return jnp.sum(picks * chosen_grad[:, :, None], 1)


def send_rows(place, values, experts):
    packed = mm_tn(place[0] + place[1], values).astype(bf16)
    return packed.reshape(experts, -1, values.shape[1])


def send_grads(place, gates, grad_in, experts):
    scaled = (gates.T[:, :, None] * grad_in[None]).astype(bf16)
    packed = (mm_tn(place[0], scaled[0]) + mm_tn(place[1], scaled[1])).astype(bf16)
    return packed.reshape(experts, -1, grad_in.shape[1])


def as_columns(values):
    high = lax.reduce_precision(values, 8, 7)
    rest = values - high
    middle = lax.reduce_precision(rest, 8, 7)
    columns = jnp.stack([high, middle, rest - middle], 1).astype(bf16)
    return jnp.pad(columns, ((0, 0), (0, PAD - 3)))


def take_back(place, returned):
    flat_back = returned.reshape(place.shape[2], -1)
    return jnp.stack([mm(place[0], flat_back), mm(place[1], flat_back)])


def exchange(packed):
    return lax.all_to_all(packed, "expert", split_axis=0, concat_axis=0, tiled=True)


def exchange_direct(packed, experts, own):
    received = jnp.zeros(packed.shape, packed.dtype)
    for k in range(experts):
        block = lax.dynamic_index_in_dim(packed, (own + k) % experts, 0)
        if k:
            block = lax.ppermute(block, "expert", [(i, (i + k) % experts) for i in range(experts)])
        received = lax.dynamic_update_slice_in_dim(received, block, (own - k) % experts, 0)
    return received


def ring_step(block, experts):
    return lax.ppermute(block, "expert", [(i, (i + 1) % experts) for i in range(experts)])


def ring_gather(block, experts):
    blocks = [block]
    for _ in range(experts - 1):
        blocks.append(ring_step(blocks[-1], experts))
    return blocks


def norm_back(stream, inverse, gain, grad_in):
    scaled = grad_in * gain
    return inverse * scaled - stream * inverse**3 * jnp.mean(scaled * stream, -1, keepdims=True)


def group_scores(queries, keys):
    heads = queries.shape[1] // HEAD
    return (
        jnp.einsum(
            "qhd,khd->hqk",
            queries.reshape(-1, heads, HEAD),
            keys.reshape(-1, heads, HEAD),
            preferred_element_type=f32,
        )
        * score_scale
    )


def attend(queries, keys, values, key_mask):
    heads = queries.shape[1] // HEAD
    scores = jnp.where(key_mask[None], group_scores(queries, keys), masked_score)
    row_peak = jnp.max(scores, -1, keepdims=True)
    exponent = jnp.exp(scores - row_peak)
    row_total = jnp.sum(exponent, -1, keepdims=True)
    attended = jnp.einsum(
        "hqk,khd->qhd",
        (exponent / row_total).astype(bf16),
        values.reshape(-1, heads, HEAD),
        preferred_element_type=f32,
    ).reshape(queries.shape)
    return (attended.astype(bf16), row_peak + jnp.log(row_total))


def attend_back(queries, keys, values, key_mask, log_total, attended, attended_grad):
    heads = queries.shape[1] // HEAD
    scores = jnp.where(key_mask[None], group_scores(queries, keys), masked_score)
    probs = jnp.exp(scores - log_total)
    grad_heads = attended_grad.reshape(-1, heads, HEAD)
    value_heads = values.reshape(-1, heads, HEAD)
    prob_grad = jnp.einsum("qhd,khd->hqk", grad_heads, value_heads, preferred_element_type=f32)
    row_delta = jnp.sum(
        grad_heads.astype(f32) * attended.reshape(-1, heads, HEAD).astype(f32), -1
    ).T[:, :, None]
    score_grad = (probs * (prob_grad - row_delta)).astype(bf16)
    query_grad = jnp.einsum(
        "hqk,khd->qhd", score_grad, keys.reshape(-1, heads, HEAD), preferred_element_type=f32
    ).reshape(queries.shape)
    key_grad = jnp.einsum(
        "hqk,qhd->khd", score_grad, queries.reshape(-1, heads, HEAD), preferred_element_type=f32
    ).reshape(keys.shape)
    value_grad = jnp.einsum(
        "hqk,qhd->khd", probs.astype(bf16), grad_heads, preferred_element_type=f32
    ).reshape(values.shape)
    return (query_grad * score_scale, key_grad * score_scale, value_grad)


def gather_dp(weight):
    return lax.all_gather(weight[0], "dp", axis=0, tiled=True)


def reduce_dp(part):
    return lax.psum_scatter(part, "dp", scatter_dimension=0, tiled=True)


def swap(block, bit):
    return lax.ppermute(block, "dp", [(i, i ^ bit) for i in range(8)])


def bit_of(value, bit):
    return (value // bit) % 2


def halves(block, axis, bit):
    pick = bit_of(lax.axis_index("dp"), bit)
    kept = lax.dynamic_index_in_dim(block, pick, axis, keepdims=False)
    sent = lax.dynamic_index_in_dim(block, 1 - pick, axis, keepdims=False)
    return (kept.astype(f32), sent.astype(bf16))


def fold(block, axis, bit):
    kept, sent = halves(block, axis, bit)
    return kept + swap(sent, bit).astype(f32)


def swaps_fit():
    return lax.axis_size("dp") == 8


def reduce_core(part):
    if not swaps_fit():
        return part
    rows, columns = part.shape
    return fold(part.reshape(2, 2, 2, rows // 8, columns), 2, 1).astype(bf16)


def reduce_chips(grid):
    if not swaps_fit():
        return reduce_dp(grid).astype(f32)
    columns = grid.shape[-1]
    left, right = grid[..., : columns // 2], grid[..., columns // 2 :]
    left = fold(fold(left, 1, 2).astype(bf16), 0, 4)
    right = fold(fold(right, 0, 4).astype(bf16), 0, 2)
    return jnp.concatenate([left, right], 1)


def body(
    tokens,
    cotangent,
    gain_one,
    gain_two,
    kv_weight,
    att_router,
    ffn_router,
    query_weight,
    output_weight,
    gate_weight,
    up_weight,
    down_weight,
    leaf_parent,
    att_route,
    ffn_route,
):
    row_count, model_width = tokens.shape
    experts = att_router.shape[1]
    capacity = row_count * 5 // (2 * experts)
    head_width = HEADS * HEAD
    width = head_width // experts
    shard_rows = kv_weight.shape[0]
    parents = leaf_parent[0]
    own = lax.axis_index("expert")
    backs = [(own - k) % experts for k in range(experts)]

    small = jnp.concatenate(
        [
            att_router,
            ffn_router,
            gain_one[:, None],
            gain_two[:, None],
            jnp.zeros((shard_rows, PAD - 2 * experts - 2), bf16),
        ],
        1,
    )
    bundle = jnp.concatenate(
        [
            kv_weight.reshape(shard_rows, 2, experts, width)
            .transpose(2, 0, 1, 3)
            .reshape(experts, shard_rows, 2 * width),
            jnp.broadcast_to(small[None], (experts, shard_rows, PAD)),
        ],
        2,
    )
    bundle = exchange_direct(bundle, experts, own).reshape(experts * shard_rows, 2 * width + PAD)
    bundle = lax.all_gather(bundle, "dp", axis=0, tiled=True)
    kv_all = bundle[:, : 2 * width]
    att_all = bundle[:, 2 * width : 2 * width + experts]
    ffn_all = bundle[:, 2 * width + experts : 2 * width + 2 * experts]
    gain_first = bundle[:, 2 * width + 2 * experts].astype(f32)
    gain_second = bundle[:, 2 * width + 2 * experts + 1].astype(f32)

    query_all = gather_dp(query_weight)
    output_all = gather_dp(output_weight)
    gate_all = gather_dp(gate_weight)
    up_all = gather_dp(up_weight)
    down_all = gather_dp(down_weight)

    tagged = jnp.concatenate(
        [tokens, att_route.astype(bf16), jnp.zeros((row_count, PAD - 2), bf16)], 1
    )
    tree = jnp.zeros((experts * row_count, model_width + PAD), bf16)
    for k, block in enumerate(ring_gather(tagged, experts)):
        tree = lax.dynamic_update_slice_in_dim(tree, block, backs[k] * row_count, 0)
    tree_tokens = tree[:, :model_width].astype(f32)
    tree_routes = tree[:, model_width : model_width + 2].astype(jnp.int32)
    tree_index = jnp.arange(experts * row_count, dtype=jnp.int32)
    tree_segment, tree_position = layout(tree_index)
    tree_cos, tree_sin = rotary_tables(tree_position)
    tree_inverse = lax.rsqrt(jnp.mean(tree_tokens * tree_tokens, -1, keepdims=True) + norm_eps)
    normed_tree = (tree_tokens * tree_inverse * gain_first).astype(bf16)
    inputs = tokens.astype(f32)
    own_start = own * row_count
    inverse_one = lax.dynamic_slice_in_dim(tree_inverse, own_start, row_count, 0)
    normed_one = lax.dynamic_slice_in_dim(normed_tree, own_start, row_count, 0)

    kv_raw = mm(normed_tree, kv_all)
    kv_own = jnp.concatenate(
        [rotate(kv_raw[:, :width], tree_cos, tree_sin), kv_raw[:, width:]], 1
    ).astype(bf16)

    named = jnp.any(tree_routes == own, 1).reshape(experts, row_count)
    rank = earlier_count(named.T).T
    slots = jnp.arange(capacity, dtype=jnp.int32)
    chosen = named[:, None, :] & (rank[:, None, :] == slots[None, :, None])
    chosen_index = tree_index.reshape(experts, 1, row_count)
    query_index = jnp.sum(jnp.where(chosen, chosen_index, 0), 2).reshape(-1)
    chosen = chosen.astype(bf16)
    query_rows = (
        jnp.einsum(
            "ksr,krd->ksd",
            chosen,
            normed_tree.reshape(experts, row_count, model_width),
            preferred_element_type=f32,
        )
        .astype(bf16)
        .reshape(-1, model_width)
    )
    query_segment, query_position = layout(query_index)
    query_cos, query_sin = rotary_tables(query_position)
    key_mask = visible(query_index, query_segment, tree_index, tree_segment, parents)
    queries = rotate(mm(query_rows, query_all), query_cos, query_sin).astype(bf16)

    attended = jnp.zeros(queries.shape, bf16)
    saved = []
    kv_block = kv_own
    kv_next = ring_step(kv_own, experts)
    for k in range(experts):
        if k:
            kv_block = kv_next
            if k == 1:
                kv_block, queries = lax.optimization_barrier((kv_block, queries))
            else:
                kv_block, attended = lax.optimization_barrier((kv_block, attended))
            if k < experts - 1:
                kv_next = ring_step(kv_block, experts)
        start = backs[k] * width
        group_queries = lax.dynamic_slice_in_dim(queries, start, width, 1)
        keys, values = kv_block[:, :width], kv_block[:, width:]
        group_attended, log_total = attend(group_queries, keys, values, key_mask)
        attended = lax.dynamic_update_slice_in_dim(attended, group_attended, start, 1)
        saved.append((group_queries, keys, values, key_mask, log_total, group_attended))
    att_branch = mm(attended, output_all).astype(bf16)
    att_back = exchange(att_branch.reshape(experts, capacity, -1))

    att_logits = mm(normed_one, att_all)
    att_gate, att_picks = gate_weights(att_logits, att_route, experts)
    att_place = placement_of(att_route, capacity, experts)
    att_picked = take_back(att_place, att_back)
    mixed_stream = inputs + jnp.sum(att_gate.T[:, :, None] * att_picked, 0)
    inverse_two = lax.rsqrt(jnp.mean(mixed_stream * mixed_stream, -1, keepdims=True) + norm_eps)
    normed_two = (mixed_stream * inverse_two * gain_second).astype(bf16)
    ffn_logits = mm(normed_two, ffn_all)
    ffn_gate, ffn_picks = gate_weights(ffn_logits, ffn_route, experts)
    ffn_place = placement_of(ffn_route, capacity, experts)
    ffn_rows = exchange(send_rows(ffn_place, normed_two, experts)).reshape(-1, model_width)
    grad_out = cotangent.astype(f32)
    slot_gate = jnp.sum(ffn_place.astype(f32) * ffn_gate.T[:, :, None], (0, 1))
    packed_grads = jnp.concatenate(
        [
            send_rows(ffn_place, cotangent, experts),
            as_columns(slot_gate).reshape(experts, capacity, PAD),
        ],
        2,
    )
    ffn_rows, packed_grads = lax.optimization_barrier((ffn_rows, packed_grads))
    gate_value = mm(ffn_rows, gate_all)
    up_value = mm(ffn_rows, up_all)
    sigmoid_gate = jax.nn.sigmoid(gate_value)
    hidden = (gate_value * sigmoid_gate * up_value).astype(bf16)
    received_grads, hidden = lax.optimization_barrier((exchange(packed_grads), hidden))
    received_grads = received_grads.reshape(experts * capacity, -1)
    out_rows = received_grads[:, :model_width]
    row_gate = jnp.sum(received_grads[:, model_width:].astype(f32), 1, keepdims=True)
    ffn_grad_rows = (row_gate * out_rows.astype(f32)).astype(bf16)
    down_part = mm_tn(hidden, ffn_grad_rows).astype(bf16)
    down_part, hidden, out_rows = lax.optimization_barrier((down_part, hidden, out_rows))
    down_sum = reduce_dp(down_part)
    hidden_pull = mm_nt(out_rows, down_all)
    row_pull = jnp.sum(hidden.astype(f32) * hidden_pull, 1)
    hidden_grad = row_gate * hidden_pull
    gate_grad = (
        hidden_grad * up_value * sigmoid_gate * (1.0 + gate_value * (1.0 - sigmoid_gate))
    ).astype(bf16)
    up_grad = (hidden_grad * gate_value * sigmoid_gate).astype(bf16)
    half = model_width // 2
    left_grad = (mm_nt(gate_grad, gate_all[:half]) + mm_nt(up_grad, up_all[:half])).astype(bf16)
    left_grad = jnp.concatenate([left_grad, as_columns(row_pull)], 1)
    left_grad, gate_grad, up_grad = lax.optimization_barrier((left_grad, gate_grad, up_grad))
    left_back = exchange(left_grad.reshape(experts, capacity, -1))
    right_grad = (mm_nt(gate_grad, gate_all[half:]) + mm_nt(up_grad, up_all[half:])).astype(bf16)
    left_back, right_grad, gate_grad, up_grad = lax.optimization_barrier(
        (left_back, right_grad, gate_grad, up_grad)
    )
    right_back = exchange(right_grad.reshape(experts, capacity, -1))
    gate_part = mm_tn(ffn_rows, gate_grad).astype(bf16)
    gate_part, right_back = lax.optimization_barrier((gate_part, right_back))
    left_back = left_back.reshape(experts * capacity, -1)
    right_back = right_back.reshape(experts * capacity, -1)
    gate_sum = reduce_dp(gate_part)
    gate_pull = jnp.sum(take_back(ffn_place, left_back[:, half:]), 2).T
    ffn_logit_grad = router_back(ffn_gate, ffn_picks, gate_pull)
    ffn_slots = ffn_place[0] + ffn_place[1]
    normed_two_grad = jnp.concatenate(
        [mm(ffn_slots, left_back[:, :half]), mm(ffn_slots, right_back)], 1
    ) + jnp.dot(
        ffn_logit_grad, ffn_all.astype(f32).T, precision=highest
    )
    gain_two_part = jnp.sum(normed_two_grad * mixed_stream * inverse_two, 0)
    mixed_grad = grad_out + norm_back(mixed_stream, inverse_two, gain_second, normed_two_grad)

    att_logit_grad = router_back(
        att_gate, att_picks, jnp.sum(att_picked * mixed_grad[None], 2).T
    )
    packed_grads, hidden, up_grad = lax.optimization_barrier(
        (send_grads(att_place, att_gate, mixed_grad, experts), hidden, up_grad)
    )
    ffn_branch = mm(hidden, down_all).astype(bf16)
    up_part = mm_tn(ffn_rows, up_grad).astype(bf16)
    att_grad_rows, ffn_branch, up_part = lax.optimization_barrier(
        (exchange(packed_grads), ffn_branch, up_part)
    )
    up_sum = reduce_dp(up_part)
    att_grad_rows = att_grad_rows.reshape(-1, model_width)
    ffn_back = exchange(ffn_branch.reshape(experts, capacity, -1))
    att_grad_rows, down_sum = lax.optimization_barrier((att_grad_rows, down_sum))
    attended_grad = mm_nt(att_grad_rows, output_all).astype(bf16)
    output_part = mm_tn(attended, att_grad_rows).astype(bf16)
    attended_grad, output_part = lax.optimization_barrier((attended_grad, output_part))
    output_core = reduce_core(output_part)
    query_grad = jnp.zeros(queries.shape, f32)
    kv_grad = None
    for step in range(1, experts + 1):
        k = step % experts
        start = backs[k] * width
        group_grad = lax.dynamic_slice_in_dim(
            attended_grad if step < 4 else late_grad, start, width, 1
        )
        group_query_grad, key_grad, value_grad = attend_back(*saved[k], group_grad)
        query_grad = lax.dynamic_update_slice_in_dim(query_grad, group_query_grad, start, 1)
        part = jnp.concatenate([key_grad, value_grad], 1)
        if k == 0:
            kv_grad, output_sum = lax.optimization_barrier((kv_grad, output_sum))
        if step == 2:
            kv_grad, output_core = lax.optimization_barrier((kv_grad, output_core))
            output_sum = reduce_chips(output_core)
        if step == experts - 1:
            kv_grad, output_sum = lax.optimization_barrier((kv_grad, output_sum))
        if k == 0:
            query_raw_grad = rotate_back(query_grad, query_cos, query_sin).astype(bf16)
            query_core = reduce_core(mm_tn(query_rows, query_raw_grad).astype(bf16))
        if kv_grad is not None:
            part = part + kv_grad.astype(f32)
        if k == 0:
            kv_grad = part
            continue
        part = part.astype(bf16)
        if step == 2:
            part, ffn_back, late_grad = lax.optimization_barrier((part, ffn_back, attended_grad))
        if step == experts - 1:
            part, query_rows = lax.optimization_barrier((part, query_rows))
        kv_grad = ring_step(part, experts)
    ffn_picked = take_back(ffn_place, ffn_back)
    result = mixed_stream + jnp.sum(ffn_gate.T[:, :, None] * ffn_picked, 0)
    att_rows_grad = mm_nt(query_raw_grad, query_all).astype(bf16)
    kv_raw_grad = jnp.concatenate(
        [rotate_back(kv_grad[:, :width], tree_cos, tree_sin), kv_grad[:, width:]], 1
    ).astype(bf16)
    tree_grad = mm_nt(kv_raw_grad, kv_all).reshape(experts, row_count, -1) + jnp.einsum(
        "ksr,ksd->krd",
        chosen,
        att_rows_grad.reshape(experts, capacity, -1),
        preferred_element_type=f32,
    )
    router_grad = jnp.dot(att_logit_grad, att_all.astype(f32).T, precision=highest)
    gain_one_part = jnp.sum(router_grad * inputs * inverse_one, 0) + jnp.sum(
        tree_grad.reshape(tree_tokens.shape) * tree_tokens * tree_inverse, 0
    )
    att_router_part = lax.dot_general(
        att_logit_grad, normed_one.astype(f32), (((0,), (0,)), ((), ())), precision=highest
    )
    ffn_router_part = lax.dot_general(
        ffn_logit_grad, normed_two.astype(f32), (((0,), (0,)), ((), ())), precision=highest
    )
    small_part = jnp.concatenate(
        [
            att_router_part,
            ffn_router_part,
            gain_one_part[None],
            gain_two_part[None],
            jnp.zeros((PAD - 2 * experts - 2, model_width), f32),
        ],
        0,
    ).astype(bf16)
    shared_part = jnp.concatenate(
        [
            mm_tn(normed_tree, kv_raw_grad).astype(bf16),
            mm_tn(small_part, jnp.eye(PAD, dtype=bf16)).astype(bf16),
        ],
        1,
    )
    normed_one_grad = None
    for step in range(1, experts + 1):
        k = step % experts
        part = lax.dynamic_index_in_dim(tree_grad, backs[k], 0, keepdims=False)
        if normed_one_grad is not None:
            part = part + normed_one_grad.astype(f32)
        normed_one_grad = part if k == 0 else ring_step(part.astype(bf16), experts)
        if step == experts - 1:
            normed_one_grad, shared_part = lax.optimization_barrier(
                (normed_one_grad, reduce_dp(shared_part))
            )
        if step == 1:
            normed_one_grad, query_core = lax.optimization_barrier((normed_one_grad, query_core))
            query_sum = reduce_chips(query_core)
        if k == 0:
            normed_one_grad, query_sum = lax.optimization_barrier((normed_one_grad, query_sum))
    normed_one_grad = normed_one_grad + router_grad
    input_grad = mixed_grad + norm_back(inputs, inverse_one, gain_first, normed_one_grad)
    shared_sum = exchange(shared_part.reshape(experts, shard_rows, -1)).astype(f32)
    kv_sum = (
        shared_sum[:, :, : 2 * width]
        .reshape(experts, shard_rows, 2, width)
        .transpose(1, 2, 0, 3)
        .reshape(shard_rows, 2 * head_width)
    )
    small_sum = jnp.sum(shared_sum[:, :, 2 * width :], 0)
    return (
        result.astype(bf16),
        input_grad,
        small_sum[:, 2 * experts],
        small_sum[:, 2 * experts + 1],
        kv_sum,
        small_sum[:, :experts],
        small_sum[:, experts : 2 * experts],
        query_sum.astype(f32)[None],
        output_sum.astype(f32)[None],
        gate_sum.astype(f32)[None],
        up_sum.astype(f32)[None],
        down_sum.astype(f32)[None],
    )

def solution(mesh):
    in_specs = (
        P(("dp", "expert"), None),
        P(("dp", "expert"), None),
        P(("dp", "expert")),
        P(("dp", "expert")),
        P(("dp", "expert"), None),
        P(("dp", "expert"), None),
        P(("dp", "expert"), None),
        P("expert", "dp", None),
        P("expert", "dp", None),
        P("expert", "dp", None),
        P("expert", "dp", None),
        P("expert", "dp", None),
        P("dp", None),
        P(("dp", "expert"), None),
        P(("dp", "expert"), None),
    )
    out_specs = (
        P(("dp", "expert"), None),
        P(("dp", "expert"), None),
        P(("dp", "expert")),
        P(("dp", "expert")),
        P(("dp", "expert"), None),
        P(("dp", "expert"), None),
        P(("dp", "expert"), None),
        P("expert", "dp", None),
        P("expert", "dp", None),
        P("expert", "dp", None),
        P("expert", "dp", None),
        P("expert", "dp", None),
    )
    return jax.shard_map(body, mesh=mesh, in_specs=in_specs, out_specs=out_specs, check_vma=False)
```

```python
import jax
import jax.numpy as jnp
from jax import lax
from jax.sharding import PartitionSpec as P

HEADS = 16
HEAD = 128
TRUNK = 512
BRANCH = 64
LEAF = 32
PAD = 128


norm_eps = 1e-05
highest = lax.Precision.HIGHEST
masked_score = -1e30
score_scale = HEAD ** (-0.5)
bf16 = jnp.bfloat16
f32 = jnp.float32


def layout(row_index):
    past_trunk = row_index - TRUNK
    in_branch = (row_index >= TRUNK) & (past_trunk < 4 * BRANCH)
    leaf_offset = past_trunk - 4 * BRANCH
    segment = jnp.where(
        row_index < TRUNK,
        0,
        jnp.where(in_branch, 1 + past_trunk // BRANCH, 5 + leaf_offset // LEAF),
    )
    position = jnp.where(
        row_index < TRUNK,
        row_index,
        jnp.where(in_branch, TRUNK + past_trunk % BRANCH, TRUNK + BRANCH + leaf_offset % LEAF),
    )
    return (segment, position)


def visible(query_index, query_segment, key_index, key_segment, parents):
    leaf_slot = query_segment - 5
    branch_of = jnp.sum(
        jnp.where(
            leaf_slot[:, None] == jnp.arange(8, dtype=jnp.int32)[None, :], parents[None, :], 0
        ),
        1,
    )
    ancestor = jnp.where(query_segment >= 5, branch_of, -1)
    same_segment = (key_segment[None, :] == query_segment[:, None]) & (
        key_index[None, :] <= query_index[:, None]
    )
    from_trunk = (key_segment[None, :] == 0) & (query_segment[:, None] > 0)
    from_branch = key_segment[None, :] == ancestor[:, None]
    return same_segment | from_trunk | from_branch


def rotary_tables(position):
    half_width = HEAD // 2
    frequency = 10000.0 ** (-2.0 * jnp.arange(half_width, dtype=f32) / HEAD)
    angle = position.astype(f32)[:, None] * frequency[None, :]
    return (jnp.cos(angle), jnp.sin(angle))


def rotate(vector, cosine, sine_table):
    length, width = vector.shape
    heads_view = vector.reshape(length, width // HEAD, HEAD)
    lead_half = heads_view[..., : HEAD // 2]
    tail_half = heads_view[..., HEAD // 2 :]
    cos_part = cosine[:, None, :]
    sin_part = sine_table[:, None, :]
    turned = jnp.concatenate(
        [lead_half * cos_part - tail_half * sin_part, tail_half * cos_part + lead_half * sin_part],
        -1,
    )
    return turned.reshape(length, width)


def rotate_back(grad_in, cosine, sine_table):
    return rotate(grad_in, cosine, -sine_table)


def mm(left, right):
    return jnp.dot(left, right, preferred_element_type=f32)


def mm_tn(left, right):
    return lax.dot_general(left, right, (((0,), (0,)), ((), ())), preferred_element_type=f32)


def mm_nt(left, right):
    return lax.dot_general(left, right, (((1,), (1,)), ((), ())), preferred_element_type=f32)


def earlier_count(named):
    rows = named.shape[0]
    before = jnp.tril(jnp.ones((rows, rows), bf16), -1)
    return mm(before, named.astype(bf16)).astype(jnp.int32)


def placement_of(routes, capacity, experts):
    picks = (routes[:, :, None] == jnp.arange(experts, dtype=jnp.int32)[None, None, :]).astype(
        jnp.int32
    )
    rank = earlier_count(jnp.sum(picks, 1))
    target = routes * capacity + jnp.sum(picks * rank[:, None, :], 2)
    slots_all = jnp.arange(experts * capacity, dtype=jnp.int32)
    return (target.T[:, :, None] == slots_all[None, None, :]).astype(bf16)


def gate_weights(logits, routes, experts):
    picks = (routes[:, :, None] == jnp.arange(experts, dtype=jnp.int32)[None, None, :]).astype(f32)
    chosen = jnp.sum(picks * logits[:, None, :], -1)
    return (jax.nn.softmax(chosen, -1), picks)


def router_back(gates, picks, gate_grad):
    chosen_grad = gates * (gate_grad - jnp.sum(gates * gate_grad, 1, keepdims=True))
    return jnp.sum(picks * chosen_grad[:, :, None], 1)


def send_rows(place, values, experts):
    packed = mm_tn(place[0] + place[1], values).astype(bf16)
    return packed.reshape(experts, -1, values.shape[1])


def send_grads(place, gates, grad_in, experts):
    scaled = (gates.T[:, :, None] * grad_in[None]).astype(bf16)
    packed = (mm_tn(place[0], scaled[0]) + mm_tn(place[1], scaled[1])).astype(bf16)
    return packed.reshape(experts, -1, grad_in.shape[1])


def as_columns(values):
    high = lax.reduce_precision(values, 8, 7)
    rest = values - high
    middle = lax.reduce_precision(rest, 8, 7)
    columns = jnp.stack([high, middle, rest - middle], 1).astype(bf16)
    return jnp.pad(columns, ((0, 0), (0, PAD - 3)))


def take_back(place, returned):
    flat_back = returned.reshape(place.shape[2], -1)
    return jnp.stack([mm(place[0], flat_back), mm(place[1], flat_back)])


def exchange(packed):
    return lax.all_to_all(packed, "expert", split_axis=0, concat_axis=0, tiled=True)


def exchange_direct(packed, experts, own):
    received = jnp.zeros(packed.shape, packed.dtype)
    for k in range(experts):
        block = lax.dynamic_index_in_dim(packed, (own + k) % experts, 0)
        if k:
            block = lax.ppermute(block, "expert", [(i, (i + k) % experts) for i in range(experts)])
        received = lax.dynamic_update_slice_in_dim(received, block, (own - k) % experts, 0)
    return received


def ring_step(block, experts):
    return lax.ppermute(block, "expert", [(i, (i + 1) % experts) for i in range(experts)])


def ring_gather(block, experts):
    blocks = [block]
    for _ in range(experts - 1):
        blocks.append(ring_step(blocks[-1], experts))
    return blocks


def norm_back(stream, inverse, gain, grad_in):
    scaled = grad_in * gain
    return inverse * scaled - stream * inverse**3 * jnp.mean(scaled * stream, -1, keepdims=True)


def group_scores(queries, keys):
    heads = queries.shape[1] // HEAD
    return (
        jnp.einsum(
            "qhd,khd->hqk",
            queries.reshape(-1, heads, HEAD),
            keys.reshape(-1, heads, HEAD),
            preferred_element_type=f32,
        )
        * score_scale
    )


def attend(queries, keys, values, key_mask):
    heads = queries.shape[1] // HEAD
    scores = jnp.where(key_mask[None], group_scores(queries, keys), masked_score)
    row_peak = jnp.max(scores, -1, keepdims=True)
    exponent = jnp.exp(scores - row_peak)
    row_total = jnp.sum(exponent, -1, keepdims=True)
    attended = jnp.einsum(
        "hqk,khd->qhd",
        (exponent / row_total).astype(bf16),
        values.reshape(-1, heads, HEAD),
        preferred_element_type=f32,
    ).reshape(queries.shape)
    return (attended.astype(bf16), row_peak + jnp.log(row_total))


def attend_back(queries, keys, values, key_mask, log_total, attended, attended_grad):
    heads = queries.shape[1] // HEAD
    scores = jnp.where(key_mask[None], group_scores(queries, keys), masked_score)
    probs = jnp.exp(scores - log_total)
    grad_heads = attended_grad.reshape(-1, heads, HEAD)
    value_heads = values.reshape(-1, heads, HEAD)
    prob_grad = jnp.einsum("qhd,khd->hqk", grad_heads, value_heads, preferred_element_type=f32)
    row_delta = jnp.sum(
        grad_heads.astype(f32) * attended.reshape(-1, heads, HEAD).astype(f32), -1
    ).T[:, :, None]
    score_grad = (probs * (prob_grad - row_delta)).astype(bf16)
    query_grad = jnp.einsum(
        "hqk,khd->qhd", score_grad, keys.reshape(-1, heads, HEAD), preferred_element_type=f32
    ).reshape(queries.shape)
    key_grad = jnp.einsum(
        "hqk,qhd->khd", score_grad, queries.reshape(-1, heads, HEAD), preferred_element_type=f32
    ).reshape(keys.shape)
    value_grad = jnp.einsum(
        "hqk,qhd->khd", probs.astype(bf16), grad_heads, preferred_element_type=f32
    ).reshape(values.shape)
    return (query_grad * score_scale, key_grad * score_scale, value_grad)


def gather_dp(weight):
    return lax.all_gather(weight[0], "dp", axis=0, tiled=True)


def reduce_dp(part):
    return lax.psum_scatter(part, "dp", scatter_dimension=0, tiled=True)


def swap(block, bit):
    return lax.ppermute(block, "dp", [(i, i ^ bit) for i in range(8)])


def bit_of(value, bit):
    return (value // bit) % 2


def halves(block, axis, bit):
    pick = bit_of(lax.axis_index("dp"), bit)
    kept = lax.dynamic_index_in_dim(block, pick, axis, keepdims=False)
    sent = lax.dynamic_index_in_dim(block, 1 - pick, axis, keepdims=False)
    return (kept.astype(f32), sent.astype(bf16))


def fold(block, axis, bit):
    kept, sent = halves(block, axis, bit)
    return kept + swap(sent, bit).astype(f32)


def swaps_fit():
    return lax.axis_size("dp") == 8


def reduce_core(part):
    if not swaps_fit():
        return part
    rows, columns = part.shape
    return fold(part.reshape(2, 2, 2, rows // 8, columns), 2, 1).astype(bf16)


def reduce_first(grid):
    if not swaps_fit():
        return (grid,)
    columns = grid.shape[-1]
    left, right = grid[..., : columns // 2], grid[..., columns // 2 :]
    return (fold(left, 1, 2).astype(bf16), fold(right, 0, 4).astype(bf16))


def reduce_last(halved):
    if not swaps_fit():
        return reduce_dp(halved[0]).astype(f32)
    return jnp.concatenate([fold(halved[0], 0, 4), fold(halved[1], 0, 2)], 1)


def body(
    tokens,
    cotangent,
    gain_one,
    gain_two,
    kv_weight,
    att_router,
    ffn_router,
    query_weight,
    output_weight,
    gate_weight,
    up_weight,
    down_weight,
    leaf_parent,
    att_route,
    ffn_route,
):
    row_count, model_width = tokens.shape
    experts = att_router.shape[1]
    capacity = row_count * 5 // (2 * experts)
    head_width = HEADS * HEAD
    width = head_width // experts
    shard_rows = kv_weight.shape[0]
    parents = leaf_parent[0]
    own = lax.axis_index("expert")
    backs = [(own - k) % experts for k in range(experts)]

    small = jnp.concatenate(
        [
            att_router,
            ffn_router,
            gain_one[:, None],
            gain_two[:, None],
            jnp.zeros((shard_rows, PAD - 2 * experts - 2), bf16),
        ],
        1,
    )
    bundle = jnp.concatenate(
        [
            kv_weight.reshape(shard_rows, 2, experts, width)
            .transpose(2, 0, 1, 3)
            .reshape(experts, shard_rows, 2 * width),
            jnp.broadcast_to(small[None], (experts, shard_rows, PAD)),
        ],
        2,
    )
    bundle = exchange_direct(bundle, experts, own).reshape(experts * shard_rows, 2 * width + PAD)
    bundle = lax.all_gather(bundle, "dp", axis=0, tiled=True)
    kv_all = bundle[:, : 2 * width]
    att_all = bundle[:, 2 * width : 2 * width + experts]
    ffn_all = bundle[:, 2 * width + experts : 2 * width + 2 * experts]
    gain_first = bundle[:, 2 * width + 2 * experts].astype(f32)
    gain_second = bundle[:, 2 * width + 2 * experts + 1].astype(f32)

    query_all = gather_dp(query_weight)
    output_all = gather_dp(output_weight)
    gate_all = gather_dp(gate_weight)
    up_all = gather_dp(up_weight)
    down_all = gather_dp(down_weight)

    tagged = jnp.concatenate(
        [tokens, att_route.astype(bf16), jnp.zeros((row_count, PAD - 2), bf16)], 1
    )
    tree = jnp.zeros((experts * row_count, model_width + PAD), bf16)
    for k, block in enumerate(ring_gather(tagged, experts)):
        tree = lax.dynamic_update_slice_in_dim(tree, block, backs[k] * row_count, 0)
    tree_tokens = tree[:, :model_width].astype(f32)
    tree_routes = tree[:, model_width : model_width + 2].astype(jnp.int32)
    tree_index = jnp.arange(experts * row_count, dtype=jnp.int32)
    tree_segment, tree_position = layout(tree_index)
    tree_cos, tree_sin = rotary_tables(tree_position)
    tree_inverse = lax.rsqrt(jnp.mean(tree_tokens * tree_tokens, -1, keepdims=True) + norm_eps)
    normed_tree = (tree_tokens * tree_inverse * gain_first).astype(bf16)
    inputs = tokens.astype(f32)
    own_start = own * row_count
    inverse_one = lax.dynamic_slice_in_dim(tree_inverse, own_start, row_count, 0)
    normed_one = lax.dynamic_slice_in_dim(normed_tree, own_start, row_count, 0)

    kv_raw = mm(normed_tree, kv_all)
    kv_own = jnp.concatenate(
        [rotate(kv_raw[:, :width], tree_cos, tree_sin), kv_raw[:, width:]], 1
    ).astype(bf16)

    named = jnp.any(tree_routes == own, 1).reshape(experts, row_count)
    rank = earlier_count(named.T).T
    slots = jnp.arange(capacity, dtype=jnp.int32)
    chosen = named[:, None, :] & (rank[:, None, :] == slots[None, :, None])
    chosen_index = tree_index.reshape(experts, 1, row_count)
    query_index = jnp.sum(jnp.where(chosen, chosen_index, 0), 2).reshape(-1)
    chosen = chosen.astype(bf16)
    query_rows = (
        jnp.einsum(
            "ksr,krd->ksd",
            chosen,
            normed_tree.reshape(experts, row_count, model_width),
            preferred_element_type=f32,
        )
        .astype(bf16)
        .reshape(-1, model_width)
    )
    query_segment, query_position = layout(query_index)
    query_cos, query_sin = rotary_tables(query_position)
    key_mask = visible(query_index, query_segment, tree_index, tree_segment, parents)
    queries = rotate(mm(query_rows, query_all), query_cos, query_sin).astype(bf16)

    attended = jnp.zeros(queries.shape, bf16)
    saved = []
    kv_block = kv_own
    kv_next = ring_step(kv_own, experts)
    for k in range(experts):
        if k:
            kv_block = kv_next
            if k == 1:
                kv_block, queries = lax.optimization_barrier((kv_block, queries))
            else:
                kv_block, attended = lax.optimization_barrier((kv_block, attended))
            if k < experts - 1:
                kv_next = ring_step(kv_block, experts)
        start = backs[k] * width
        group_queries = lax.dynamic_slice_in_dim(queries, start, width, 1)
        keys, values = kv_block[:, :width], kv_block[:, width:]
        group_attended, log_total = attend(group_queries, keys, values, key_mask)
        attended = lax.dynamic_update_slice_in_dim(attended, group_attended, start, 1)
        saved.append((group_queries, keys, values, key_mask, log_total, group_attended))
    att_branch = mm(attended, output_all).astype(bf16)
    att_back = exchange(att_branch.reshape(experts, capacity, -1))

    att_logits = mm(normed_one, att_all)
    att_gate, att_picks = gate_weights(att_logits, att_route, experts)
    att_place = placement_of(att_route, capacity, experts)
    att_picked = take_back(att_place, att_back)
    mixed_stream = inputs + jnp.sum(att_gate.T[:, :, None] * att_picked, 0)
    inverse_two = lax.rsqrt(jnp.mean(mixed_stream * mixed_stream, -1, keepdims=True) + norm_eps)
    normed_two = (mixed_stream * inverse_two * gain_second).astype(bf16)
    ffn_logits = mm(normed_two, ffn_all)
    ffn_gate, ffn_picks = gate_weights(ffn_logits, ffn_route, experts)
    ffn_place = placement_of(ffn_route, capacity, experts)
    ffn_rows = exchange(send_rows(ffn_place, normed_two, experts)).reshape(-1, model_width)
    grad_out = cotangent.astype(f32)
    slot_gate = jnp.sum(ffn_place.astype(f32) * ffn_gate.T[:, :, None], (0, 1))
    packed_grads = jnp.concatenate(
        [
            send_rows(ffn_place, cotangent, experts),
            as_columns(slot_gate).reshape(experts, capacity, PAD),
        ],
        2,
    )
    ffn_rows, packed_grads = lax.optimization_barrier((ffn_rows, packed_grads))
    gate_value = mm(ffn_rows, gate_all)
    up_value = mm(ffn_rows, up_all)
    sigmoid_gate = jax.nn.sigmoid(gate_value)
    hidden = (gate_value * sigmoid_gate * up_value).astype(bf16)
    received_grads, hidden = lax.optimization_barrier((exchange(packed_grads), hidden))
    received_grads = received_grads.reshape(experts * capacity, -1)
    out_rows = received_grads[:, :model_width]
    row_gate = jnp.sum(received_grads[:, model_width:].astype(f32), 1, keepdims=True)
    ffn_grad_rows = (row_gate * out_rows.astype(f32)).astype(bf16)
    down_part = mm_tn(hidden, ffn_grad_rows).astype(bf16)
    down_part, hidden, out_rows = lax.optimization_barrier((down_part, hidden, out_rows))
    down_sum = reduce_dp(down_part)
    hidden_pull = mm_nt(out_rows, down_all)
    row_pull = jnp.sum(hidden.astype(f32) * hidden_pull, 1)
    hidden_grad = row_gate * hidden_pull
    gate_grad = (
        hidden_grad * up_value * sigmoid_gate * (1.0 + gate_value * (1.0 - sigmoid_gate))
    ).astype(bf16)
    up_grad = (hidden_grad * gate_value * sigmoid_gate).astype(bf16)
    half = model_width // 2
    left_grad = (mm_nt(gate_grad, gate_all[:half]) + mm_nt(up_grad, up_all[:half])).astype(bf16)
    left_grad = jnp.concatenate([left_grad, as_columns(row_pull)], 1)
    left_grad, gate_grad, up_grad = lax.optimization_barrier((left_grad, gate_grad, up_grad))
    left_back = exchange(left_grad.reshape(experts, capacity, -1))
    right_grad = (mm_nt(gate_grad, gate_all[half:]) + mm_nt(up_grad, up_all[half:])).astype(bf16)
    left_back, right_grad, gate_grad, up_grad = lax.optimization_barrier(
        (left_back, right_grad, gate_grad, up_grad)
    )
    right_back = exchange(right_grad.reshape(experts, capacity, -1))
    gate_part = mm_tn(ffn_rows, gate_grad).astype(bf16)
    gate_part, right_back = lax.optimization_barrier((gate_part, right_back))
    left_back = left_back.reshape(experts * capacity, -1)
    right_back = right_back.reshape(experts * capacity, -1)
    gate_sum = reduce_dp(gate_part)
    gate_pull = jnp.sum(take_back(ffn_place, left_back[:, half:]), 2).T
    ffn_logit_grad = router_back(ffn_gate, ffn_picks, gate_pull)
    ffn_slots = ffn_place[0] + ffn_place[1]
    normed_two_grad = jnp.concatenate(
        [mm(ffn_slots, left_back[:, :half]), mm(ffn_slots, right_back)], 1
    ) + jnp.dot(
        ffn_logit_grad, ffn_all.astype(f32).T, precision=highest
    )
    gain_two_part = jnp.sum(normed_two_grad * mixed_stream * inverse_two, 0)
    mixed_grad = grad_out + norm_back(mixed_stream, inverse_two, gain_second, normed_two_grad)

    att_logit_grad = router_back(
        att_gate, att_picks, jnp.sum(att_picked * mixed_grad[None], 2).T
    )
    packed_grads, hidden, up_grad = lax.optimization_barrier(
        (send_grads(att_place, att_gate, mixed_grad, experts), hidden, up_grad)
    )
    ffn_branch = mm(hidden, down_all).astype(bf16)
    up_part = mm_tn(ffn_rows, up_grad).astype(bf16)
    att_grad_rows, ffn_branch, up_part = lax.optimization_barrier(
        (exchange(packed_grads), ffn_branch, up_part)
    )
    up_sum = reduce_dp(up_part)
    att_grad_rows = att_grad_rows.reshape(-1, model_width)
    ffn_back = exchange(ffn_branch.reshape(experts, capacity, -1))
    att_grad_rows, down_sum = lax.optimization_barrier((att_grad_rows, down_sum))
    attended_grad = mm_nt(att_grad_rows, output_all).astype(bf16)
    output_part = mm_tn(attended, att_grad_rows).astype(bf16)
    attended_grad, output_part = lax.optimization_barrier((attended_grad, output_part))
    output_core = reduce_core(output_part)
    query_grad = jnp.zeros(queries.shape, f32)
    kv_grad = None
    for step in range(1, experts + 1):
        k = step % experts
        start = backs[k] * width
        group_grad = lax.dynamic_slice_in_dim(
            attended_grad if step < 4 else late_grad, start, width, 1
        )
        group_query_grad, key_grad, value_grad = attend_back(*saved[k], group_grad)
        query_grad = lax.dynamic_update_slice_in_dim(query_grad, group_query_grad, start, 1)
        part = jnp.concatenate([key_grad, value_grad], 1)
        if k == 0:
            kv_grad, output_sum = lax.optimization_barrier((kv_grad, output_sum))
        if step == 2:
            kv_grad, output_core = lax.optimization_barrier((kv_grad, output_core))
            output_core = reduce_first(output_core)
        if step == experts - 1:
            kv_grad, output_core = lax.optimization_barrier((kv_grad, output_core))
            output_sum = reduce_last(output_core)
        if k == 0:
            kv_grad, output_sum = lax.optimization_barrier((kv_grad, output_sum))
        if k == 0:
            query_raw_grad = rotate_back(query_grad, query_cos, query_sin).astype(bf16)
            query_core = reduce_core(mm_tn(query_rows, query_raw_grad).astype(bf16))
        if kv_grad is not None:
            part = part + kv_grad.astype(f32)
        if k == 0:
            kv_grad = part
            continue
        part = part.astype(bf16)
        if step == 2:
            part, ffn_back, late_grad = lax.optimization_barrier((part, ffn_back, attended_grad))
        if step == experts - 1:
            part, query_rows = lax.optimization_barrier((part, query_rows))
        kv_grad = ring_step(part, experts)
    att_rows_grad = mm_nt(query_raw_grad, query_all).astype(bf16)
    kv_raw_grad = jnp.concatenate(
        [rotate_back(kv_grad[:, :width], tree_cos, tree_sin), kv_grad[:, width:]], 1
    ).astype(bf16)
    tree_grad = mm_nt(kv_raw_grad, kv_all).reshape(experts, row_count, -1) + jnp.einsum(
        "ksr,ksd->krd",
        chosen,
        att_rows_grad.reshape(experts, capacity, -1),
        preferred_element_type=f32,
    )
    router_grad = jnp.dot(att_logit_grad, att_all.astype(f32).T, precision=highest)
    gain_one_part = jnp.sum(router_grad * inputs * inverse_one, 0) + jnp.sum(
        tree_grad.reshape(tree_tokens.shape) * tree_tokens * tree_inverse, 0
    )
    att_router_part = lax.dot_general(
        att_logit_grad, normed_one.astype(f32), (((0,), (0,)), ((), ())), precision=highest
    )
    ffn_router_part = lax.dot_general(
        ffn_logit_grad, normed_two.astype(f32), (((0,), (0,)), ((), ())), precision=highest
    )
    small_part = jnp.concatenate(
        [
            att_router_part,
            ffn_router_part,
            gain_one_part[None],
            gain_two_part[None],
            jnp.zeros((PAD - 2 * experts - 2, model_width), f32),
        ],
        0,
    ).astype(bf16)
    shared_part = jnp.concatenate(
        [
            mm_tn(normed_tree, kv_raw_grad).astype(bf16),
            mm_tn(small_part, jnp.eye(PAD, dtype=bf16)).astype(bf16),
        ],
        1,
    )
    normed_one_grad = None
    for step in range(1, experts + 1):
        k = step % experts
        part = lax.dynamic_index_in_dim(tree_grad, backs[k], 0, keepdims=False)
        if normed_one_grad is not None:
            part = part + normed_one_grad.astype(f32)
        normed_one_grad = part if k == 0 else ring_step(part.astype(bf16), experts)
        if step == experts - 1:
            normed_one_grad, shared_part = lax.optimization_barrier(
                (normed_one_grad, reduce_dp(shared_part))
            )
        if step == 1:
            normed_one_grad, query_core, ffn_back = lax.optimization_barrier(
                (normed_one_grad, query_core, ffn_back)
            )
            query_core = reduce_first(query_core)
        if step == 2:
            normed_one_grad, query_core = lax.optimization_barrier((normed_one_grad, query_core))
            query_sum = reduce_last(query_core)
        if k == 0:
            normed_one_grad, query_sum = lax.optimization_barrier((normed_one_grad, query_sum))
    normed_one_grad = normed_one_grad + router_grad
    ffn_picked = take_back(ffn_place, ffn_back)
    result = mixed_stream + jnp.sum(ffn_gate.T[:, :, None] * ffn_picked, 0)
    input_grad = mixed_grad + norm_back(inputs, inverse_one, gain_first, normed_one_grad)
    shared_sum = exchange(shared_part.reshape(experts, shard_rows, -1)).astype(f32)
    kv_sum = (
        shared_sum[:, :, : 2 * width]
        .reshape(experts, shard_rows, 2, width)
        .transpose(1, 2, 0, 3)
        .reshape(shard_rows, 2 * head_width)
    )
    small_sum = jnp.sum(shared_sum[:, :, 2 * width :], 0)
    return (
        result.astype(bf16),
        input_grad,
        small_sum[:, 2 * experts],
        small_sum[:, 2 * experts + 1],
        kv_sum,
        small_sum[:, :experts],
        small_sum[:, experts : 2 * experts],
        query_sum.astype(f32)[None],
        output_sum.astype(f32)[None],
        gate_sum.astype(f32)[None],
        up_sum.astype(f32)[None],
        down_sum.astype(f32)[None],
    )

def solution(mesh):
    in_specs = (
        P(("dp", "expert"), None),
        P(("dp", "expert"), None),
        P(("dp", "expert")),
        P(("dp", "expert")),
        P(("dp", "expert"), None),
        P(("dp", "expert"), None),
        P(("dp", "expert"), None),
        P("expert", "dp", None),
        P("expert", "dp", None),
        P("expert", "dp", None),
        P("expert", "dp", None),
        P("expert", "dp", None),
        P("dp", None),
        P(("dp", "expert"), None),
        P(("dp", "expert"), None),
    )
    out_specs = (
        P(("dp", "expert"), None),
        P(("dp", "expert"), None),
        P(("dp", "expert")),
        P(("dp", "expert")),
        P(("dp", "expert"), None),
        P(("dp", "expert"), None),
        P(("dp", "expert"), None),
        P("expert", "dp", None),
        P("expert", "dp", None),
        P("expert", "dp", None),
        P("expert", "dp", None),
        P("expert", "dp", None),
    )
    return jax.shard_map(body, mesh=mesh, in_specs=in_specs, out_specs=out_specs, check_vma=False)
```

```python
import jax
import jax.numpy as jnp
from jax import lax
from jax.sharding import PartitionSpec as P

HEADS = 16
HEAD = 128
TRUNK = 512
BRANCH = 64
LEAF = 32
PAD = 128


norm_eps = 1e-05
highest = lax.Precision.HIGHEST
masked_score = -1e30
score_scale = HEAD ** (-0.5)
bf16 = jnp.bfloat16
f32 = jnp.float32


def layout(row_index):
    past_trunk = row_index - TRUNK
    in_branch = (row_index >= TRUNK) & (past_trunk < 4 * BRANCH)
    leaf_offset = past_trunk - 4 * BRANCH
    segment = jnp.where(
        row_index < TRUNK,
        0,
        jnp.where(in_branch, 1 + past_trunk // BRANCH, 5 + leaf_offset // LEAF),
    )
    position = jnp.where(
        row_index < TRUNK,
        row_index,
        jnp.where(in_branch, TRUNK + past_trunk % BRANCH, TRUNK + BRANCH + leaf_offset % LEAF),
    )
    return (segment, position)


def visible(query_index, query_segment, key_index, key_segment, parents):
    leaf_slot = query_segment - 5
    branch_of = jnp.sum(
        jnp.where(
            leaf_slot[:, None] == jnp.arange(8, dtype=jnp.int32)[None, :], parents[None, :], 0
        ),
        1,
    )
    ancestor = jnp.where(query_segment >= 5, branch_of, -1)
    same_segment = (key_segment[None, :] == query_segment[:, None]) & (
        key_index[None, :] <= query_index[:, None]
    )
    from_trunk = (key_segment[None, :] == 0) & (query_segment[:, None] > 0)
    from_branch = key_segment[None, :] == ancestor[:, None]
    return same_segment | from_trunk | from_branch


def rotary_tables(position):
    half_width = HEAD // 2
    frequency = 10000.0 ** (-2.0 * jnp.arange(half_width, dtype=f32) / HEAD)
    angle = position.astype(f32)[:, None] * frequency[None, :]
    return (jnp.cos(angle), jnp.sin(angle))


def rotate(vector, cosine, sine_table):
    length, width = vector.shape
    heads_view = vector.reshape(length, width // HEAD, HEAD)
    lead_half = heads_view[..., : HEAD // 2]
    tail_half = heads_view[..., HEAD // 2 :]
    cos_part = cosine[:, None, :]
    sin_part = sine_table[:, None, :]
    turned = jnp.concatenate(
        [lead_half * cos_part - tail_half * sin_part, tail_half * cos_part + lead_half * sin_part],
        -1,
    )
    return turned.reshape(length, width)


def rotate_back(grad_in, cosine, sine_table):
    return rotate(grad_in, cosine, -sine_table)


def mm(left, right):
    return jnp.dot(left, right, preferred_element_type=f32)


def mm_tn(left, right):
    return lax.dot_general(left, right, (((0,), (0,)), ((), ())), preferred_element_type=f32)


def mm_nt(left, right):
    return lax.dot_general(left, right, (((1,), (1,)), ((), ())), preferred_element_type=f32)


def earlier_count(named):
    rows = named.shape[0]
    before = jnp.tril(jnp.ones((rows, rows), bf16), -1)
    return mm(before, named.astype(bf16)).astype(jnp.int32)


def placement_of(routes, capacity, experts):
    picks = (routes[:, :, None] == jnp.arange(experts, dtype=jnp.int32)[None, None, :]).astype(
        jnp.int32
    )
    rank = earlier_count(jnp.sum(picks, 1))
    target = routes * capacity + jnp.sum(picks * rank[:, None, :], 2)
    slots_all = jnp.arange(experts * capacity, dtype=jnp.int32)
    return (target.T[:, :, None] == slots_all[None, None, :]).astype(bf16)


def gate_weights(logits, routes, experts):
    picks = (routes[:, :, None] == jnp.arange(experts, dtype=jnp.int32)[None, None, :]).astype(f32)
    chosen = jnp.sum(picks * logits[:, None, :], -1)
    return (jax.nn.softmax(chosen, -1), picks)


def router_back(gates, picks, gate_grad):
    chosen_grad = gates * (gate_grad - jnp.sum(gates * gate_grad, 1, keepdims=True))
    return jnp.sum(picks * chosen_grad[:, :, None], 1)


def send_rows(place, values, experts):
    packed = mm_tn(place[0] + place[1], values).astype(bf16)
    return packed.reshape(experts, -1, values.shape[1])


def send_grads(place, gates, grad_in, experts):
    scaled = (gates.T[:, :, None] * grad_in[None]).astype(bf16)
    packed = (mm_tn(place[0], scaled[0]) + mm_tn(place[1], scaled[1])).astype(bf16)
    return packed.reshape(experts, -1, grad_in.shape[1])


def as_columns(values):
    high = lax.reduce_precision(values, 8, 7)
    rest = values - high
    middle = lax.reduce_precision(rest, 8, 7)
    columns = jnp.stack([high, middle, rest - middle], 1).astype(bf16)
    return jnp.pad(columns, ((0, 0), (0, PAD - 3)))


def take_back(place, returned):
    flat_back = returned.reshape(place.shape[2], -1)
    return jnp.stack([mm(place[0], flat_back), mm(place[1], flat_back)])


def exchange(packed):
    return lax.all_to_all(packed, "expert", split_axis=0, concat_axis=0, tiled=True)


def exchange_direct(packed, experts, own):
    received = jnp.zeros(packed.shape, packed.dtype)
    for k in range(experts):
        block = lax.dynamic_index_in_dim(packed, (own + k) % experts, 0)
        if k:
            block = lax.ppermute(block, "expert", [(i, (i + k) % experts) for i in range(experts)])
        received = lax.dynamic_update_slice_in_dim(received, block, (own - k) % experts, 0)
    return received


def ring_step(block, experts):
    return lax.ppermute(block, "expert", [(i, (i + 1) % experts) for i in range(experts)])


def ring_gather(block, experts):
    blocks = [block]
    for _ in range(experts - 1):
        blocks.append(ring_step(blocks[-1], experts))
    return blocks


def norm_back(stream, inverse, gain, grad_in):
    scaled = grad_in * gain
    return inverse * scaled - stream * inverse**3 * jnp.mean(scaled * stream, -1, keepdims=True)


def group_scores(queries, keys):
    heads = queries.shape[1] // HEAD
    return (
        jnp.einsum(
            "qhd,khd->hqk",
            queries.reshape(-1, heads, HEAD),
            keys.reshape(-1, heads, HEAD),
            preferred_element_type=f32,
        )
        * score_scale
    )


def attend(queries, keys, values, key_mask):
    heads = queries.shape[1] // HEAD
    scores = jnp.where(key_mask[None], group_scores(queries, keys), masked_score)
    row_peak = jnp.max(scores, -1, keepdims=True)
    exponent = jnp.exp(scores - row_peak)
    row_total = jnp.sum(exponent, -1, keepdims=True)
    attended = jnp.einsum(
        "hqk,khd->qhd",
        (exponent / row_total).astype(bf16),
        values.reshape(-1, heads, HEAD),
        preferred_element_type=f32,
    ).reshape(queries.shape)
    return (attended.astype(bf16), row_peak + jnp.log(row_total))


def attend_back(queries, keys, values, key_mask, log_total, attended, attended_grad):
    heads = queries.shape[1] // HEAD
    scores = jnp.where(key_mask[None], group_scores(queries, keys), masked_score)
    probs = jnp.exp(scores - log_total)
    grad_heads = attended_grad.reshape(-1, heads, HEAD)
    value_heads = values.reshape(-1, heads, HEAD)
    prob_grad = jnp.einsum("qhd,khd->hqk", grad_heads, value_heads, preferred_element_type=f32)
    row_delta = jnp.sum(
        grad_heads.astype(f32) * attended.reshape(-1, heads, HEAD).astype(f32), -1
    ).T[:, :, None]
    score_grad = (probs * (prob_grad - row_delta)).astype(bf16)
    query_grad = jnp.einsum(
        "hqk,khd->qhd", score_grad, keys.reshape(-1, heads, HEAD), preferred_element_type=f32
    ).reshape(queries.shape)
    key_grad = jnp.einsum(
        "hqk,qhd->khd", score_grad, queries.reshape(-1, heads, HEAD), preferred_element_type=f32
    ).reshape(keys.shape)
    value_grad = jnp.einsum(
        "hqk,qhd->khd", probs.astype(bf16), grad_heads, preferred_element_type=f32
    ).reshape(values.shape)
    return (query_grad * score_scale, key_grad * score_scale, value_grad)


def gather_dp(weight):
    return lax.all_gather(weight[0], "dp", axis=0, tiled=True)


def reduce_dp(part):
    return lax.psum_scatter(part, "dp", scatter_dimension=0, tiled=True)


def swap(block, bit):
    return lax.ppermute(block, "dp", [(i, i ^ bit) for i in range(8)])


def bit_of(value, bit):
    return (value // bit) % 2


def halves(block, axis, bit):
    pick = bit_of(lax.axis_index("dp"), bit)
    kept = lax.dynamic_index_in_dim(block, pick, axis, keepdims=False)
    sent = lax.dynamic_index_in_dim(block, 1 - pick, axis, keepdims=False)
    return (kept.astype(f32), sent.astype(bf16))


def fold(block, axis, bit):
    kept, sent = halves(block, axis, bit)
    return kept + swap(sent, bit).astype(f32)


def swaps_fit():
    return lax.axis_size("dp") == 8


def reduce_core(part):
    if not swaps_fit():
        return part
    rows, columns = part.shape
    return fold(part.reshape(2, 2, 2, rows // 8, columns), 2, 1).astype(bf16)


def reduce_first(grid):
    if not swaps_fit():
        return (grid,)
    columns = grid.shape[-1]
    left, right = grid[..., : columns // 2], grid[..., columns // 2 :]
    return (fold(left, 1, 2).astype(bf16), fold(right, 0, 4).astype(bf16))


def reduce_last(halved):
    if not swaps_fit():
        return reduce_dp(halved[0]).astype(f32)
    return jnp.concatenate([fold(halved[0], 0, 4), fold(halved[1], 0, 2)], 1)


def body(
    tokens,
    cotangent,
    gain_one,
    gain_two,
    kv_weight,
    att_router,
    ffn_router,
    query_weight,
    output_weight,
    gate_weight,
    up_weight,
    down_weight,
    leaf_parent,
    att_route,
    ffn_route,
):
    row_count, model_width = tokens.shape
    experts = att_router.shape[1]
    capacity = row_count * 5 // (2 * experts)
    head_width = HEADS * HEAD
    width = head_width // experts
    shard_rows = kv_weight.shape[0]
    parents = leaf_parent[0]
    own = lax.axis_index("expert")
    backs = [(own - k) % experts for k in range(experts)]

    small = jnp.concatenate(
        [
            att_router,
            ffn_router,
            gain_one[:, None],
            gain_two[:, None],
            jnp.zeros((shard_rows, PAD - 2 * experts - 2), bf16),
        ],
        1,
    )
    bundle = jnp.concatenate(
        [
            kv_weight.reshape(shard_rows, 2, experts, width)
            .transpose(2, 0, 1, 3)
            .reshape(experts, shard_rows, 2 * width),
            jnp.broadcast_to(small[None], (experts, shard_rows, PAD)),
        ],
        2,
    )
    bundle = exchange_direct(bundle, experts, own).reshape(experts * shard_rows, 2 * width + PAD)
    bundle = lax.all_gather(bundle, "dp", axis=0, tiled=True)
    kv_all = bundle[:, : 2 * width]
    att_all = bundle[:, 2 * width : 2 * width + experts]
    ffn_all = bundle[:, 2 * width + experts : 2 * width + 2 * experts]
    gain_first = bundle[:, 2 * width + 2 * experts].astype(f32)
    gain_second = bundle[:, 2 * width + 2 * experts + 1].astype(f32)

    query_all = gather_dp(query_weight)
    output_all = gather_dp(output_weight)
    gate_all = gather_dp(gate_weight)
    up_all = gather_dp(up_weight)
    down_all = gather_dp(down_weight)

    tagged = jnp.concatenate(
        [tokens, att_route.astype(bf16), jnp.zeros((row_count, PAD - 2), bf16)], 1
    )
    tree = jnp.zeros((experts * row_count, model_width + PAD), bf16)
    for k, block in enumerate(ring_gather(tagged, experts)):
        tree = lax.dynamic_update_slice_in_dim(tree, block, backs[k] * row_count, 0)
    tree_tokens = tree[:, :model_width].astype(f32)
    tree_routes = tree[:, model_width : model_width + 2].astype(jnp.int32)
    tree_index = jnp.arange(experts * row_count, dtype=jnp.int32)
    tree_segment, tree_position = layout(tree_index)
    tree_cos, tree_sin = rotary_tables(tree_position)
    tree_inverse = lax.rsqrt(jnp.mean(tree_tokens * tree_tokens, -1, keepdims=True) + norm_eps)
    normed_tree = (tree_tokens * tree_inverse * gain_first).astype(bf16)
    inputs = tokens.astype(f32)
    own_start = own * row_count
    inverse_one = lax.dynamic_slice_in_dim(tree_inverse, own_start, row_count, 0)
    normed_one = lax.dynamic_slice_in_dim(normed_tree, own_start, row_count, 0)

    kv_raw = mm(normed_tree, kv_all)
    kv_own = jnp.concatenate(
        [rotate(kv_raw[:, :width], tree_cos, tree_sin), kv_raw[:, width:]], 1
    ).astype(bf16)

    named = jnp.any(tree_routes == own, 1).reshape(experts, row_count)
    rank = earlier_count(named.T).T
    slots = jnp.arange(capacity, dtype=jnp.int32)
    chosen = named[:, None, :] & (rank[:, None, :] == slots[None, :, None])
    chosen_index = tree_index.reshape(experts, 1, row_count)
    query_index = jnp.sum(jnp.where(chosen, chosen_index, 0), 2).reshape(-1)
    chosen = chosen.astype(bf16)
    query_rows = (
        jnp.einsum(
            "ksr,krd->ksd",
            chosen,
            normed_tree.reshape(experts, row_count, model_width),
            preferred_element_type=f32,
        )
        .astype(bf16)
        .reshape(-1, model_width)
    )
    query_segment, query_position = layout(query_index)
    query_cos, query_sin = rotary_tables(query_position)
    key_mask = visible(query_index, query_segment, tree_index, tree_segment, parents)
    queries = rotate(mm(query_rows, query_all), query_cos, query_sin).astype(bf16)

    attended = jnp.zeros(queries.shape, bf16)
    saved = []
    kv_block = kv_own
    kv_next = ring_step(kv_own, experts)
    for k in range(experts):
        if k:
            kv_block = kv_next
            if k == 1:
                kv_block, queries = lax.optimization_barrier((kv_block, queries))
            else:
                kv_block, attended = lax.optimization_barrier((kv_block, attended))
            if k < experts - 1:
                kv_next = ring_step(kv_block, experts)
        start = backs[k] * width
        group_queries = lax.dynamic_slice_in_dim(queries, start, width, 1)
        keys, values = kv_block[:, :width], kv_block[:, width:]
        group_attended, log_total = attend(group_queries, keys, values, key_mask)
        attended = lax.dynamic_update_slice_in_dim(attended, group_attended, start, 1)
        saved.append((group_queries, keys, values, key_mask, log_total, group_attended))
    att_branch = mm(attended, output_all).astype(bf16)
    att_back = exchange(att_branch.reshape(experts, capacity, -1))

    att_logits = mm(normed_one, att_all)
    att_gate, att_picks = gate_weights(att_logits, att_route, experts)
    att_place = placement_of(att_route, capacity, experts)
    att_picked = take_back(att_place, att_back)
    mixed_stream = inputs + jnp.sum(att_gate.T[:, :, None] * att_picked, 0)
    inverse_two = lax.rsqrt(jnp.mean(mixed_stream * mixed_stream, -1, keepdims=True) + norm_eps)
    normed_two = (mixed_stream * inverse_two * gain_second).astype(bf16)
    ffn_logits = mm(normed_two, ffn_all)
    ffn_gate, ffn_picks = gate_weights(ffn_logits, ffn_route, experts)
    ffn_place = placement_of(ffn_route, capacity, experts)
    ffn_rows = exchange(send_rows(ffn_place, normed_two, experts)).reshape(-1, model_width)
    grad_out = cotangent.astype(f32)
    slot_gate = jnp.sum(ffn_place.astype(f32) * ffn_gate.T[:, :, None], (0, 1))
    packed_grads = jnp.concatenate(
        [
            send_rows(ffn_place, cotangent, experts),
            as_columns(slot_gate).reshape(experts, capacity, PAD),
        ],
        2,
    )
    ffn_rows, packed_grads = lax.optimization_barrier((ffn_rows, packed_grads))
    gate_value = mm(ffn_rows, gate_all)
    up_value = mm(ffn_rows, up_all)
    sigmoid_gate = jax.nn.sigmoid(gate_value)
    hidden = (gate_value * sigmoid_gate * up_value).astype(bf16)
    received_grads, hidden = lax.optimization_barrier((exchange(packed_grads), hidden))
    received_grads = received_grads.reshape(experts * capacity, -1)
    out_rows = received_grads[:, :model_width]
    row_gate = jnp.sum(received_grads[:, model_width:].astype(f32), 1, keepdims=True)
    ffn_grad_rows = (row_gate * out_rows.astype(f32)).astype(bf16)
    down_part = mm_tn(hidden, ffn_grad_rows).astype(bf16)
    down_part, hidden, out_rows = lax.optimization_barrier((down_part, hidden, out_rows))
    down_sum = reduce_dp(down_part)
    hidden_pull = mm_nt(out_rows, down_all)
    row_pull = jnp.sum(hidden.astype(f32) * hidden_pull, 1)
    hidden_grad = row_gate * hidden_pull
    gate_grad = (
        hidden_grad * up_value * sigmoid_gate * (1.0 + gate_value * (1.0 - sigmoid_gate))
    ).astype(bf16)
    up_grad = (hidden_grad * gate_value * sigmoid_gate).astype(bf16)
    half = model_width // 2
    left_grad = (mm_nt(gate_grad, gate_all[:half]) + mm_nt(up_grad, up_all[:half])).astype(bf16)
    left_grad = jnp.concatenate([left_grad, as_columns(row_pull)], 1)
    left_grad, gate_grad, up_grad = lax.optimization_barrier((left_grad, gate_grad, up_grad))
    left_back = exchange(left_grad.reshape(experts, capacity, -1))
    right_grad = (mm_nt(gate_grad, gate_all[half:]) + mm_nt(up_grad, up_all[half:])).astype(bf16)
    left_back, right_grad, gate_grad, up_grad = lax.optimization_barrier(
        (left_back, right_grad, gate_grad, up_grad)
    )
    right_back = exchange(right_grad.reshape(experts, capacity, -1))
    gate_part = mm_tn(ffn_rows, gate_grad).astype(bf16)
    gate_part, right_back = lax.optimization_barrier((gate_part, right_back))
    left_back = left_back.reshape(experts * capacity, -1)
    right_back = right_back.reshape(experts * capacity, -1)
    gate_sum = reduce_dp(gate_part)
    gate_pull = jnp.sum(take_back(ffn_place, left_back[:, half:]), 2).T
    ffn_logit_grad = router_back(ffn_gate, ffn_picks, gate_pull)
    ffn_slots = ffn_place[0] + ffn_place[1]
    normed_two_grad = jnp.concatenate(
        [mm(ffn_slots, left_back[:, :half]), mm(ffn_slots, right_back)], 1
    ) + jnp.dot(
        ffn_logit_grad, ffn_all.astype(f32).T, precision=highest
    )
    gain_two_part = jnp.sum(normed_two_grad * mixed_stream * inverse_two, 0)
    mixed_grad = grad_out + norm_back(mixed_stream, inverse_two, gain_second, normed_two_grad)

    att_logit_grad = router_back(
        att_gate, att_picks, jnp.sum(att_picked * mixed_grad[None], 2).T
    )
    packed_grads, hidden, up_grad = lax.optimization_barrier(
        (send_grads(att_place, att_gate, mixed_grad, experts), hidden, up_grad)
    )
    ffn_branch = mm(hidden, down_all).astype(bf16)
    up_part = mm_tn(ffn_rows, up_grad).astype(bf16)
    att_grad_rows, ffn_branch, up_part = lax.optimization_barrier(
        (exchange(packed_grads), ffn_branch, up_part)
    )
    up_sum = reduce_dp(up_part)
    att_grad_rows = att_grad_rows.reshape(-1, model_width)
    ffn_back = exchange(ffn_branch.reshape(experts, capacity, -1))
    att_grad_rows, down_sum = lax.optimization_barrier((att_grad_rows, down_sum))
    attended_grad = mm_nt(att_grad_rows, output_all).astype(bf16)
    output_part = mm_tn(attended, att_grad_rows).astype(bf16)
    attended_grad, output_part = lax.optimization_barrier((attended_grad, output_part))
    output_core = reduce_core(output_part)
    query_grad = jnp.zeros(queries.shape, f32)
    kv_grad = None
    for step in range(1, experts + 1):
        k = step % experts
        start = backs[k] * width
        group_grad = lax.dynamic_slice_in_dim(
            attended_grad if step < 4 else late_grad, start, width, 1
        )
        group_query_grad, key_grad, value_grad = attend_back(*saved[k], group_grad)
        query_grad = lax.dynamic_update_slice_in_dim(query_grad, group_query_grad, start, 1)
        part = jnp.concatenate([key_grad, value_grad], 1)
        if k == 0:
            kv_grad, output_sum = lax.optimization_barrier((kv_grad, output_sum))
        if step == 2:
            _, output_core = lax.optimization_barrier((kv_grad, output_core))
            output_core = reduce_first(output_core)
        if step == experts - 1:
            kv_grad, output_core = lax.optimization_barrier((kv_grad, output_core))
            output_sum = reduce_last(output_core)
        if k == 0:
            kv_grad, output_sum = lax.optimization_barrier((kv_grad, output_sum))
        if k == 0:
            query_raw_grad = rotate_back(query_grad, query_cos, query_sin).astype(bf16)
            query_core = reduce_core(mm_tn(query_rows, query_raw_grad).astype(bf16))
        if kv_grad is not None:
            part = part + kv_grad.astype(f32)
        if k == 0:
            kv_grad = part
            continue
        part = part.astype(bf16)
        if step == 2:
            part, ffn_back, late_grad = lax.optimization_barrier((part, ffn_back, attended_grad))
        if step == experts - 1:
            part, query_rows = lax.optimization_barrier((part, query_rows))
        kv_grad = ring_step(part, experts)
    att_rows_grad = mm_nt(query_raw_grad, query_all).astype(bf16)
    kv_raw_grad = jnp.concatenate(
        [rotate_back(kv_grad[:, :width], tree_cos, tree_sin), kv_grad[:, width:]], 1
    ).astype(bf16)
    tree_grad = mm_nt(kv_raw_grad, kv_all).reshape(experts, row_count, -1) + jnp.einsum(
        "ksr,ksd->krd",
        chosen,
        att_rows_grad.reshape(experts, capacity, -1),
        preferred_element_type=f32,
    )
    router_grad = jnp.dot(att_logit_grad, att_all.astype(f32).T, precision=highest)
    gain_one_part = jnp.sum(router_grad * inputs * inverse_one, 0) + jnp.sum(
        tree_grad.reshape(tree_tokens.shape) * tree_tokens * tree_inverse, 0
    )
    att_router_part = lax.dot_general(
        att_logit_grad, normed_one.astype(f32), (((0,), (0,)), ((), ())), precision=highest
    )
    ffn_router_part = lax.dot_general(
        ffn_logit_grad, normed_two.astype(f32), (((0,), (0,)), ((), ())), precision=highest
    )
    small_part = jnp.concatenate(
        [
            att_router_part,
            ffn_router_part,
            gain_one_part[None],
            gain_two_part[None],
            jnp.zeros((PAD - 2 * experts - 2, model_width), f32),
        ],
        0,
    ).astype(bf16)
    shared_part = jnp.concatenate(
        [
            mm_tn(normed_tree, kv_raw_grad).astype(bf16),
            mm_tn(small_part, jnp.eye(PAD, dtype=bf16)).astype(bf16),
        ],
        1,
    )
    normed_one_grad = None
    for step in range(1, experts + 1):
        k = step % experts
        part = lax.dynamic_index_in_dim(tree_grad, backs[k], 0, keepdims=False)
        if normed_one_grad is not None:
            part = part + normed_one_grad.astype(f32)
        normed_one_grad = part if k == 0 else ring_step(part.astype(bf16), experts)
        if step == experts - 1:
            normed_one_grad, shared_part = lax.optimization_barrier(
                (normed_one_grad, reduce_dp(shared_part))
            )
        if step == 1:
            normed_one_grad, query_core, ffn_back = lax.optimization_barrier(
                (normed_one_grad, query_core, ffn_back)
            )
            query_core = reduce_first(query_core)
        if step == 2:
            normed_one_grad, query_core = lax.optimization_barrier((normed_one_grad, query_core))
            query_sum = reduce_last(query_core)
        if k == 0:
            normed_one_grad, query_sum = lax.optimization_barrier((normed_one_grad, query_sum))
    normed_one_grad = normed_one_grad + router_grad
    ffn_picked = take_back(ffn_place, ffn_back)
    result = mixed_stream + jnp.sum(ffn_gate.T[:, :, None] * ffn_picked, 0)
    input_grad = mixed_grad + norm_back(inputs, inverse_one, gain_first, normed_one_grad)
    shared_sum = exchange(shared_part.reshape(experts, shard_rows, -1)).astype(f32)
    kv_sum = (
        shared_sum[:, :, : 2 * width]
        .reshape(experts, shard_rows, 2, width)
        .transpose(1, 2, 0, 3)
        .reshape(shard_rows, 2 * head_width)
    )
    small_sum = jnp.sum(shared_sum[:, :, 2 * width :], 0)
    return (
        result.astype(bf16),
        input_grad,
        small_sum[:, 2 * experts],
        small_sum[:, 2 * experts + 1],
        kv_sum,
        small_sum[:, :experts],
        small_sum[:, experts : 2 * experts],
        query_sum.astype(f32)[None],
        output_sum.astype(f32)[None],
        gate_sum.astype(f32)[None],
        up_sum.astype(f32)[None],
        down_sum.astype(f32)[None],
    )

def solution(mesh):
    in_specs = (
        P(("dp", "expert"), None),
        P(("dp", "expert"), None),
        P(("dp", "expert")),
        P(("dp", "expert")),
        P(("dp", "expert"), None),
        P(("dp", "expert"), None),
        P(("dp", "expert"), None),
        P("expert", "dp", None),
        P("expert", "dp", None),
        P("expert", "dp", None),
        P("expert", "dp", None),
        P("expert", "dp", None),
        P("dp", None),
        P(("dp", "expert"), None),
        P(("dp", "expert"), None),
    )
    out_specs = (
        P(("dp", "expert"), None),
        P(("dp", "expert"), None),
        P(("dp", "expert")),
        P(("dp", "expert")),
        P(("dp", "expert"), None),
        P(("dp", "expert"), None),
        P(("dp", "expert"), None),
        P("expert", "dp", None),
        P("expert", "dp", None),
        P("expert", "dp", None),
        P("expert", "dp", None),
        P("expert", "dp", None),
    )
    return jax.shard_map(body, mesh=mesh, in_specs=in_specs, out_specs=out_specs, check_vma=False)
```
